32 devices in a mesh: parts: 2 (over x), xy: 16 (over z, y, core).
Axes of the slice: x: 2, y: 2, z: 4, core: 2. Of those that a mesh axis runs over, the one named last changes fastest.
Arguments:
- affinity: bfloat16 [3, 256, 64, 128], P(None, ('parts', 'xy')), parts along dimension 1, may hold values from 0 to 1
- block_scale: float32 [3, 256, 64], P(None, ('parts', 'xy')), parts along dimension 1, may hold values from 0.5 to 2
- slot_map: int32 [256, 64, 128], P(('parts', 'xy')), parts along dimension 0, may hold values from 0 to 7, as said below
- edge_list: int32 [256, 64, 8], P(('parts', 'xy')), parts along dimension 0, may hold values from 0 to 8191, as said below
- valid_count: int32 [256, 64], P(('parts', 'xy')), parts along dimension 0, may hold values from 5 to 8
- edge_home: int32 [16384], P('parts'), parts along dimension 0, may hold values from 0 to 8191, as said below
Outputs:
- edge_features: float32 [16384, 64], P(('parts', 'xy')), parts along dimension 0
The draws below stay inside these ranges and needn't reach their ends.
There are 2 independent parts, one for each index of `parts`. The reference program is written for one: setup_inputs(seed, part) draws one part's arguments, and reference() takes and returns one part's arrays. A program takes and returns all parts, laid end to end along the dimension named above; each array names one. Nothing has to cross between parts.
Inputs may be any that keep to these rules, and one draw needn't show every extreme that they name: `slot_map`: every voxel's entry is below its block's valid_count. `edge_list`: among the used entries of the blocks of one device (8 planes), at most 512 name edges whose edge_home lies in any one range [k * 512, (k + 1) * 512); in every draw some range receives exactly 512 from every device. `edge_home`: a permutation of 0 to 8191.
All inputs are finite; a program needn't handle non-finite values.
Results may differ from the reference program's by a relative error of at most 0.0003.
Values sent between devices are 32-bit elements; how exact they have to be, the bound alone decides.
No kernel may reach another device: no remote copies, remote signals or barrier semaphores. Data moves between devices by JAX's collectives and lax.ppermute only.
A program may use at most 64 MiB of HBM per device.

```python
import math
import jax
import jax.numpy as jnp
from jax import lax

CX = 8
CY = 128
CZ = 64
SLOTS = 8
HALO = 8
FEAT = 64
E_DEV = 512
NX = 128
BPP = 64
EDGES = 8192
CAP = 512
N_XY = 16


def layout(key):
    keys = [jax.random.fold_in(key, 7000 + number) for number in range(7)]
    home = jax.random.permutation(keys[0], EDGES).astype(jnp.int32)
    inverse = jnp.argsort(home).astype(jnp.int32)
    counts = jax.random.randint(keys[1], (NX, BPP), SLOTS // 2 + 1, SLOTS + 1, dtype=jnp.int32)
    per_device = CX * BPP * SLOTS
    valid = (jnp.arange(SLOTS, dtype=jnp.int32) < counts[..., None]).reshape(N_XY, per_device)
    scores = jnp.where(valid, jax.random.randint(keys[2], (N_XY, per_device), 0, 1 << 29, dtype=jnp.int32), 1 << 30)
    order = jnp.argsort(scores, axis=1, stable=True)
    ranks = jnp.argsort(order, axis=1, stable=True).astype(jnp.int32)
    hottest = jax.random.randint(keys[3], (), 0, N_XY, dtype=jnp.int32)
    others = (ranks - CAP) % (N_XY - 1)
    others = others + (others >= hottest).astype(jnp.int32)
    target = jnp.where(ranks < CAP, hottest, others)
    within = jax.random.randint(keys[4], (N_XY, per_device), 0, E_DEV, dtype=jnp.int32)
    chosen = inverse[target * E_DEV + within]
    filler = jax.random.randint(keys[5], (N_XY, per_device), 0, EDGES, dtype=jnp.int32)
    edges = jnp.where(valid, chosen, filler).reshape(NX, BPP, SLOTS)
    slots = jax.random.randint(keys[6], (NX, BPP, 128), 0, counts[..., None], dtype=jnp.int32).reshape(NX, CZ, CY)
    return (home, edges, counts, slots)


def draw_slot_map(key, part):
    return layout(key)[3]


def draw_edge_list(key, part):
    return layout(key)[1]


def draw_valid_count(key, part):
    return layout(key)[2]


def draw_edge_home(key, part):
    return layout(key)[0]


def expand_cells(cells, along_x, along_z, along_y):
    lead, cell_x, cell_z, cell_y = cells.shape
    grown = jnp.broadcast_to(cells[:, :, None, :, None, :, None], (lead, cell_x, along_x, cell_z, along_z, cell_y, along_y))
    return grown.reshape(lead, cell_x * along_x, cell_z * along_z, cell_y * along_y)


def draw_affinity(key, part):
    keys = [jax.random.fold_in(key, 8000 + number) for number in range(4)]
    coarse_draw = jax.random.randint(keys[0], (3, NX // 8, CZ // 8, CY // 16), 0, 5, dtype=jnp.int32)
    middle_draw = jax.random.randint(keys[1], (3, NX // 2, CZ // 2, CY // 2), 0, 2, dtype=jnp.int32)
    fine_rate = jax.random.randint(keys[2], (3, NX, CZ, 1), 1, 8, dtype=jnp.int32)
    fine_draw = jax.random.randint(keys[3], (3, NX, CZ, CY), 0, 8, dtype=jnp.int32)
    fine_on = (fine_draw < fine_rate).astype(jnp.float32)
    middle_on = expand_cells((middle_draw < 1).astype(jnp.float32), 2, 2, 2)
    coarse_on = expand_cells((coarse_draw < 2).astype(jnp.float32), 8, 8, 16)
    value = 0.5 * coarse_on + 0.25 * middle_on + 0.25 * fine_on
    return value.astype(jnp.float32).astype(jnp.bfloat16)


def levels(rng, shape, split, least, high):
    level, own = 1.0, jax.random.fold_in(rng, 6)
    for dim, parts in split:
        draws = jnp.exp(jax.random.uniform(jax.random.fold_in(own, dim), (parts,), jnp.float32, least / len(split), high / len(split)))
        level = level * jnp.repeat(draws, shape[dim] // parts).reshape([-1 if axis == dim else 1 for axis in range(len(shape))])
    return level


def setup_inputs(seed: int = 0, part: int = 0) -> dict:
    splits = jax.random.split(jax.random.key(seed), 7)
    own_keys = jax.random.split(jax.random.fold_in(splits[6], part), 7)
    return {
        "affinity": draw_affinity(jax.random.fold_in(jax.random.fold_in(splits[6], part), 71), part),
        "block_scale": jnp.clip(jnp.exp(math.log(2.0) - 1.3862944 * jax.random.uniform(own_keys[1], (3, NX, BPP), jnp.float32) ** levels(own_keys[1], (3, NX, BPP), ((1, 16),), -0.2, 0.2)), 0.5, 2.0),
        "slot_map": draw_slot_map(jax.random.fold_in(jax.random.fold_in(splits[6], part), 71), part),
        "edge_list": draw_edge_list(jax.random.fold_in(jax.random.fold_in(splits[6], part), 71), part),
        "valid_count": draw_valid_count(jax.random.fold_in(jax.random.fold_in(splits[6], part), 71), part),
        "edge_home": draw_edge_home(jax.random.fold_in(jax.random.fold_in(splits[6], part), 71), part),
    }


sigma_list = (0.8, 1.3, 2.0, 3.0)


def kernel_for(sigma_value):
    offsets = jnp.arange(-HALO, HALO + 1).astype(jnp.float32)
    weights = jnp.exp(-offsets * offsets / (2.0 * sigma_value * sigma_value))
    return weights / jnp.sum(weights)


def blur_axis(field, axis, kernel):
    widths = [(0, 0)] * field.ndim
    widths[axis] = (HALO, HALO)
    padded = jnp.pad(field, widths)
    length = field.shape[axis]
    total = jnp.zeros(field.shape, jnp.float32)
    for offset in range(2 * HALO + 1):
        total = total + kernel[offset] * lax.slice_in_dim(padded, offset, offset + length, axis=axis)
    return total


def feature_rows(resp, raw):
    square = resp * resp
    pairs = []
    for scale_index in range(4):
        base = resp[3 * scale_index:3 * scale_index + 3]
        pairs += [base[0] * base[1], base[0] * base[2], base[1] * base[2]]
    ones = jnp.ones((1, resp.shape[1]), jnp.float32)
    return jnp.concatenate([resp, square, square * resp, square * square, jnp.stack(pairs), raw, ones], 0)


def finalize(table):
    count = table[:, 63]
    means = table[:, :63] / jnp.maximum(count, 1.0)[:, None]
    return jnp.concatenate([means, jnp.log1p(count)[:, None]], 1)


def reference(affinity, block_scale, slot_map, edge_list, valid_count, edge_home):
    planes = affinity.shape[1]
    dequant = (affinity.astype(jnp.float32).reshape(3, planes, BPP, 128) * block_scale[..., None]).reshape(3, planes, CZ, CY)
    fields = []
    for sigma_value in sigma_list:
        kernel = kernel_for(sigma_value)
        field = blur_axis(dequant, 1, kernel)
        field = blur_axis(field, 2, kernel)
        fields.append(blur_axis(field, 3, kernel))
    resp = jnp.concatenate(fields, 0)

    def plane_sums(inputs):
        plane_resp, plane_raw, plane_slots = inputs
        feats = feature_rows(plane_resp.reshape(12, -1), plane_raw.reshape(3, -1)).reshape(FEAT, BPP, 128)
        one_hot = (plane_slots.reshape(BPP, 128, 1) == jnp.arange(SLOTS).astype(jnp.int32)).astype(jnp.float32)
        return jnp.einsum('fbv,bvs->bsf', feats, one_hot, precision=lax.Precision.HIGHEST)

    sums = lax.map(plane_sums, (jnp.moveaxis(resp, 1, 0), jnp.moveaxis(dequant, 1, 0), slot_map))
    home = edge_home[edge_list]
    valid = jnp.arange(SLOTS).astype(jnp.int32) < valid_count[..., None]
    index = jnp.where(valid, home, EDGES).astype(jnp.int32)
    table = jnp.zeros((EDGES, FEAT), jnp.float32).at[index.reshape(-1)].add(sums.reshape(-1, FEAT), mode='drop')
    return finalize(table)
```

```python
import functools

import jax
import jax.numpy as jnp
import numpy as np
from jax import lax
from jax.experimental import pallas as pl
from jax.experimental.pallas import tpu as pltpu
from jax.sharding import PartitionSpec as P

SLOTS = 8
HALO = 8
FEAT = 64
LANES = 128

sigma_list = (0.8, 1.3, 2.0, 3.0)
SCALES = len(sigma_list)
RESP = 3 * SCALES
ROWS = 2 * RESP + 2 * RESP + 8


def taps(sigma):
    offsets = np.arange(-HALO, HALO + 1).astype(np.float32)
    weights = np.exp(-offsets * offsets / np.float32(2.0 * sigma * sigma)).astype(np.float32)
    return (weights / weights.sum(dtype=np.float32)).astype(np.float32)


def band(weights, length):
    rows = np.arange(length)[:, None]
    cols = np.arange(length)[None, :]
    offset = cols - rows + HALO
    inside = (offset >= 0) & (offset <= 2 * HALO)
    return np.where(inside, weights[np.clip(offset, 0, 2 * HALO)], 0.0).astype(np.float32)


def halves(value):
    high = value.astype(jnp.bfloat16)
    low = (value - high.astype(jnp.float32)).astype(jnp.bfloat16)
    return high, low


def constant_halves(value):
    high = value.astype(jnp.bfloat16)
    low = (value - high.astype(np.float32)).astype(jnp.bfloat16)
    return high, low


def filter_constants(height, depth):
    along_y, along_z = [], []
    for sigma in sigma_list:
        high, low = constant_halves(band(taps(sigma), depth).T)
        along_y.append(np.concatenate([high, high, low], 0))
        high, low = constant_halves(band(taps(sigma), height))
        along_z.append(np.concatenate([high, high, low], 1))
    return np.stack(along_y), np.stack(along_z)


def column_constants():
    columns = np.arange(LANES)
    block = np.where(columns < 120, columns % 24 // 12, (columns - 120) // 4)
    feature = np.where(columns < 120, columns // 24 * 12 + columns % 12, 60 + columns % 4)
    place = np.zeros((LANES, 2 * LANES), np.float32)
    place[columns, feature] = 1.0
    place[columns, LANES + FEAT + feature] = 1.0
    keep = (np.repeat(np.arange(2), SLOTS)[:, None] == block[None, :]).astype(np.float32)
    return np.concatenate([place, place], 0).astype(jnp.bfloat16), keep


def order_bits(owners):
    bits = owners.bit_length() - 1
    first = list(range(bits))
    return first, [0] + first[2:] + first[1:2]


def index_kernel(owners, rows_owned, height, me_ref, edge_ref, count_ref, home_ref, target_ref, source_ref):
    lists = edge_ref[...]
    both = jnp.concatenate([lists, lists], 1)
    high = both // LANES
    low = both % LANES

    def pick(row, found):
        line = jnp.broadcast_to(home_ref[pl.ds(row, 1), :], both.shape)
        return jnp.where(high == row, jnp.take_along_axis(line, low, axis=1), found)

    home = lax.fori_loop(0, home_ref.shape[0], pick, jnp.zeros(both.shape, jnp.int32))[:, :height]
    entry = lax.broadcasted_iota(jnp.int32, home.shape, 0)
    slot = entry % SLOTS
    plane = entry // SLOTS
    column = lax.broadcasted_iota(jnp.int32, home.shape, 1)
    half = height // 2
    number = ((plane * half + column % half) * 2 + column // half) * SLOTS + slot
    owner = (home // rows_owned) ^ me_ref[0]
    within = home % rows_owned
    quarter = rows_owned // 4
    part = within // (2 * quarter)
    first, second = order_bits(owners)
    bits = len(first)
    place_first = jnp.zeros_like(owner)
    place_second = jnp.zeros_like(owner)
    for position in range(bits):
        place_first += ((owner >> first[position]) & 1) << (bits - 1 - position)
        place_second += ((owner >> second[position]) & 1) << (bits - 1 - position)
    place = jnp.where(part == 0, place_first, owners + place_second)
    row = place * quarter + within % quarter
    side = (within // quarter) % 2
    valid = slot < count_ref[...]
    target_ref[...] = jnp.where(valid, row, 2 * owners * quarter)
    source_ref[...] = side * (entry.shape[0] * height) + number


def main_kernel(
    copies, before_ref, own_ref, after_ref, slots_ref, y_ref, z_ref, place_ref, keep_ref, target_ref, source_ref,
    first_ref, second_ref, *scratch,
):
    blurred, fields, entries = scratch[:3]
    tables = scratch[3:]
    planes, height, depth = own_ref.shape[1:]
    half = height // 2
    weights = [[float(w) for w in taps(sigma)] for sigma in sigma_list]

    for table in tables:
        def clear(step, carry, table=table):
            table[pl.ds(pl.multiple_of(step * 64, 64), 64), :] = jnp.zeros((64, LANES), jnp.float32)
            return carry
        lax.fori_loop(0, table.shape[0] // 64, clear, 0)

    tiles = height // 8

    def across(step, carry):
        channel = step // tiles
        rows = pl.ds(pl.multiple_of(step % tiles * 8, 8), 8)
        values = [before_ref[channel, planes - HALO + p, rows, :] for p in range(HALO)]
        values += [own_ref[channel, p, rows, :] for p in range(planes)]
        values += [after_ref[channel, p, rows, :] for p in range(HALO)]
        for q in range(planes):
            center = q + HALO
            sums = [values[center]] + [values[center - t] + values[center + t] for t in range(1, HALO + 1)]
            for scale in range(SCALES):
                total = sums[0] * weights[scale][HALO]
                for t in range(1, HALO + 1):
                    total = total + sums[t] * weights[scale][HALO + t]
                blurred[scale * 3 + channel, q, rows, :] = total
        return carry

    lax.fori_loop(0, 3 * tiles, across, 0)

    def put(row, value):
        for q in range(planes):
            for b in range(2):
                start = q * half * ROWS + row + b * (RESP if row < 4 * RESP else 4)
                fields[pl.ds(start, half, stride=ROWS), :] = value[b * half : (b + 1) * half, q * LANES : (q + 1) * LANES]

    for scale in range(SCALES):
        results = []
        for channel in range(3):
            high, low = halves(blurred[scale * 3 + channel].reshape(planes * height, depth))
            line = jnp.dot(jnp.concatenate([high, low, high], 1), y_ref[scale], preferred_element_type=jnp.float32)
            high, low = halves(line)
            stacked = jnp.concatenate([high.reshape(planes, height, depth), low.reshape(planes, height, depth), high.reshape(planes, height, depth)], 1)
            side_by_side = jnp.concatenate([stacked[q] for q in range(planes)], 1)
            result = jnp.dot(z_ref[scale], side_by_side, preferred_element_type=jnp.float32)
            put(scale * 3 + channel, result)
            results.append(result)
        for number, (a, b) in enumerate(((0, 1), (0, 2), (1, 2))):
            put(2 * RESP + scale * 3 + number, results[a] * results[b])
    for channel in range(3):
        put(4 * RESP + channel, jnp.concatenate([own_ref[channel, q] for q in range(planes)], 1))
    put(4 * RESP + 3, jnp.ones((height, planes * LANES), jnp.float32))

    sub = lax.broadcasted_iota(jnp.int32, (SLOTS, LANES), 0)
    keep = keep_ref[...]
    place = place_ref[...]
    group = 8
    entry_count = planes * height * SLOTS

    def block_sums(step, carry):
        plane = step // (half // group)
        base = step % (half // group) * group
        parts = []
        for g in range(group):
            zz = base + g
            tile = fields[pl.ds(pl.multiple_of((plane * half + zz) * ROWS, 8), ROWS), :]
            resp = tile[: 2 * RESP]
            square = resp * resp
            feats = jnp.concatenate(
                [resp, square, square * resp, square * square, tile[2 * RESP :]], 0
            )
            high, low = halves(feats)
            upper = (slots_ref[plane, pl.ds(zz, 1), :] == sub).astype(jnp.float32)
            lower = (slots_ref[plane, pl.ds(zz + half, 1), :] == sub).astype(jnp.float32)
            hot = jnp.concatenate([upper, lower], 0).astype(jnp.bfloat16)
            dims = (((1,), (1,)), ((), ()))
            sums = lax.dot_general(
                jnp.concatenate([hot, hot], 1), jnp.concatenate([high, low], 1), dims, preferred_element_type=jnp.float32
            )
            parts.append(sums * keep)
        high, low = halves(jnp.concatenate(parts, 0))
        placed = jnp.dot(jnp.concatenate([high, low], 1), place, preferred_element_type=jnp.float32)
        start = pl.multiple_of(step * (group * 2 * SLOTS), group * 2 * SLOTS)
        entries[pl.ds(start, group * 2 * SLOTS), :] = placed[:, :LANES]
        entries[pl.ds(entry_count + start, group * 2 * SLOTS), :] = placed[:, LANES:]
        return carry

    lax.fori_loop(0, planes * half // group, block_sums, 0)

    def scatter(step, carry):
        row = step // (height // 16)
        first = step % (height // 16) * 16
        for offset in range(0, 16, copies):
            for number, table in enumerate(tables):
                column = first + offset + number
                target = target_ref[row, column]
                source = source_ref[row, column]
                table[pl.ds(target, 1), :] = table[pl.ds(target, 1), :] + entries[pl.ds(source, 1), :]
        return carry

    lax.fori_loop(0, planes * SLOTS * (height // 16), scatter, 0)

    length = first_ref.shape[0]

    def combine(step, carry):
        for out, offset in ((first_ref, 0), (second_ref, length)):
            start = pl.multiple_of(step * 64, 64)
            total = tables[0][pl.ds(offset + start, 64), :]
            for table in tables[1:]:
                total = total + table[pl.ds(offset + start, 64), :]
            out[pl.ds(start, 64), :] = total
        return carry

    lax.fori_loop(0, length // 64, combine, 0)


def final_kernel(first_keep, first_got, second_keep, second_got, out_ref):
    quarter = first_keep.shape[0]
    for number, (keep, got) in enumerate(((first_keep, first_got), (second_keep, second_got))):
        table = keep[...] + got[...]
        for side in range(2):
            rows = table[:, side * FEAT : (side + 1) * FEAT]
            count = rows[:, FEAT - 1 : FEAT]
            lane = lax.broadcasted_iota(jnp.int32, rows.shape, 1)
            means = rows / jnp.maximum(count, 1.0)
            result = jnp.where(lane == FEAT - 1, jnp.log(1.0 + rows), means)
            out_ref[pl.ds((2 * number + side) * quarter, quarter), :] = result


def shards(affinity, block_scale, slot_map, edge_list, valid_count, edge_home):
    planes, height, depth = affinity.shape[1:]
    owners = lax.axis_size("xy")
    rows_owned = edge_home.shape[0] // owners
    quarter = rows_owned // 4
    vmem = pl.BlockSpec(memory_space=pltpu.VMEM)
    smem = pl.BlockSpec(memory_space=pltpu.SMEM)

    dequant = affinity.astype(jnp.float32) * block_scale[..., None]
    up = [(i, i + 1) for i in range(owners - 1)]
    down = [(j, i) for i, j in up]
    before = lax.ppermute(dequant[:, planes - HALO :], "xy", up)
    after = lax.ppermute(dequant[:, :HALO], "xy", down)

    me = lax.axis_index("xy").astype(jnp.int32).reshape(1)
    lists = edge_list.transpose(0, 2, 1).reshape(planes * SLOTS, height)
    counts = jnp.broadcast_to(valid_count[:, None, :], (planes, SLOTS, height)).reshape(planes * SLOTS, height)
    index_shape = jax.ShapeDtypeStruct((planes * SLOTS, height), jnp.int32)
    target, source = pl.pallas_call(
        functools.partial(index_kernel, owners, rows_owned, height),
        out_shape=(index_shape, index_shape),
        in_specs=[smem, vmem, vmem, vmem],
        out_specs=(vmem, vmem),
        name="index",
    )(me, lists, counts, edge_home.reshape(-1, LANES))

    along_y, along_z = filter_constants(height, depth)
    place, keep = column_constants()
    table_rows = 2 * owners * quarter
    copies = 4 if table_rows <= 4096 else 2
    table_shape = jax.ShapeDtypeStruct((owners * quarter, LANES), jnp.float32)
    entry_count = planes * height * SLOTS
    first, second = pl.pallas_call(
        functools.partial(main_kernel, copies),
        out_shape=(table_shape, table_shape),
        in_specs=[vmem] * 8 + [smem, smem],
        out_specs=(vmem, vmem),
        scratch_shapes=[
            pltpu.VMEM((RESP, planes, height, depth), jnp.float32),
            pltpu.VMEM((planes * (height // 2) * ROWS, LANES), jnp.float32),
            pltpu.VMEM((2 * entry_count, LANES), jnp.float32),
        ]
        + [pltpu.VMEM((table_rows + 64, LANES), jnp.float32)] * copies,
        compiler_params=pltpu.CompilerParams(vmem_limit_bytes=56 << 20),
        name="features",
    )(before, dequant, after, slot_map, jnp.asarray(along_y), jnp.asarray(along_z), jnp.asarray(place), jnp.asarray(keep), target, source)

    order_first, order_second = order_bits(owners)

    def exchange(value, bit):
        middle = value.shape[0] // 2
        pairs = [(i, i ^ (1 << bit)) for i in range(owners)]
        return value[:middle], lax.ppermute(value[middle:], "xy", pairs)

    for stage in range(len(order_first)):
        first_pair = exchange(first, order_first[stage])
        second_pair = exchange(second, order_second[stage])
        if stage < len(order_first) - 1:
            first = first_pair[0] + first_pair[1]
            second = second_pair[0] + second_pair[1]
    return pl.pallas_call(
        final_kernel,
        out_shape=jax.ShapeDtypeStruct((rows_owned, FEAT), jnp.float32),
        in_specs=[vmem] * 4,
        out_specs=vmem,
        name="final",
    )(*first_pair, *second_pair)


def solution(mesh):
    in_specs = (
        P(None, ("parts", "xy"), None, None),
        P(None, ("parts", "xy"), None),
        P(("parts", "xy"), None, None),
        P(("parts", "xy"), None, None),
        P(("parts", "xy"), None),
        P("parts"),
    )
    out_specs = P(("parts", "xy"), None)
    return jax.shard_map(shards, mesh=mesh, in_specs=in_specs, out_specs=out_specs, check_vma=False)
```

```python
import functools

import jax
import jax.numpy as jnp
import numpy as np
from jax import lax
from jax.experimental import pallas as pl
from jax.experimental.pallas import tpu as pltpu
from jax.sharding import PartitionSpec as P

SLOTS = 8
HALO = 8
FEAT = 64
LANES = 128

sigma_list = (0.8, 1.3, 2.0, 3.0)
SCALES = len(sigma_list)
RESP = 3 * SCALES
ROWS = 2 * RESP + 2 * RESP + 8


def taps(sigma):
    offsets = np.arange(-HALO, HALO + 1).astype(np.float32)
    weights = np.exp(-offsets * offsets / np.float32(2.0 * sigma * sigma)).astype(np.float32)
    return (weights / weights.sum(dtype=np.float32)).astype(np.float32)


def band(weights, length):
    rows = np.arange(length)[:, None]
    cols = np.arange(length)[None, :]
    offset = cols - rows + HALO
    inside = (offset >= 0) & (offset <= 2 * HALO)
    return np.where(inside, weights[np.clip(offset, 0, 2 * HALO)], 0.0).astype(np.float32)


def halves(value):
    high = value.astype(jnp.bfloat16)
    low = (value - high.astype(jnp.float32)).astype(jnp.bfloat16)
    return high, low


def constant_halves(value):
    high = value.astype(jnp.bfloat16)
    low = (value - high.astype(np.float32)).astype(jnp.bfloat16)
    return high, low


def filter_constants(height, depth):
    along_y, along_z = [], []
    for sigma in sigma_list:
        high, low = constant_halves(band(taps(sigma), depth).T)
        along_y.append(np.concatenate([high, high, low], 0))
        high, low = constant_halves(band(taps(sigma), height))
        along_z.append(np.concatenate([high, high, low], 1))
    return np.stack(along_y), np.stack(along_z)


def order_bits(owners):
    bits = owners.bit_length() - 1
    first = list(range(bits))
    return first, [0] + first[2:] + first[1:2]


def index_kernel(owners, rows_owned, height, me_ref, edge_ref, count_ref, home_ref, target_ref):
    lists = edge_ref[...]
    both = jnp.concatenate([lists, lists], 1)
    high = both // LANES
    low = both % LANES

    def pick(row, found):
        line = jnp.broadcast_to(home_ref[pl.ds(row, 1), :], both.shape)
        return jnp.where(high == row, jnp.take_along_axis(line, low, axis=1), found)

    home = lax.fori_loop(0, home_ref.shape[0], pick, jnp.zeros(both.shape, jnp.int32))[:, :height]
    entry = lax.broadcasted_iota(jnp.int32, home.shape, 0)
    slot = entry % SLOTS
    owner = (home // rows_owned) ^ me_ref[0]
    within = home % rows_owned
    quarter = rows_owned // 4
    part = within // (2 * quarter)
    first, second = order_bits(owners)
    bits = len(first)
    place_first = jnp.zeros_like(owner)
    place_second = jnp.zeros_like(owner)
    for position in range(bits):
        place_first += ((owner >> first[position]) & 1) << (bits - 1 - position)
        place_second += ((owner >> second[position]) & 1) << (bits - 1 - position)
    place = jnp.where(part == 0, place_first, owners + place_second)
    row = place * (2 * quarter) + within % (2 * quarter)
    valid = slot < count_ref[...]
    target_ref[...] = jnp.where(valid, row, owners * rows_owned)


def main_kernel(
    copies, quarter, before_ref, own_ref, after_ref, slots_ref, y_ref, z_ref, target_ref, keep_ref, send_ref, *scratch
):
    blurred, fields, entries = scratch[:3]
    tables = scratch[3:]
    planes, height, depth = own_ref.shape[1:]
    half = height // 2
    weights = [[float(w) for w in taps(sigma)] for sigma in sigma_list]
    tiles = height // 8

    def across(step, carry):
        channel = step // tiles
        rows = pl.ds(pl.multiple_of(step % tiles * 8, 8), 8)
        values = [before_ref[channel, planes - HALO + p, rows, :] for p in range(HALO)]
        values += [own_ref[channel, p, rows, :] for p in range(planes)]
        values += [after_ref[channel, p, rows, :] for p in range(HALO)]
        for q in range(planes):
            center = q + HALO
            sums = [values[center]] + [values[center - t] + values[center + t] for t in range(1, HALO + 1)]
            for scale in range(SCALES):
                total = sums[0] * weights[scale][HALO]
                for t in range(1, HALO + 1):
                    total = total + sums[t] * weights[scale][HALO + t]
                blurred[scale * 3 + channel, q, rows, :] = total
        return carry

    lax.fori_loop(0, 3 * tiles, across, 0)

    def put(row_first, row_second, value):
        for q in range(planes):
            for b, row in enumerate((row_first, row_second)):
                start = q * half * ROWS + row
                fields[pl.ds(start, half, stride=ROWS), :] = value[b * half : (b + 1) * half, q * LANES : (q + 1) * LANES]

    def put_resp(number, value):
        put(number, 16 + number if number < 8 else 4 + number, value)

    def put_other(number, value):
        put(2 * RESP + number, 2 * RESP + 16 + number, value)

    for scale in range(SCALES):
        results = []
        for channel in range(3):
            high, low = halves(blurred[scale * 3 + channel].reshape(planes * height, depth))
            line = jnp.dot(jnp.concatenate([high, low, high], 1), y_ref[scale], preferred_element_type=jnp.float32)
            high, low = halves(line)
            high, low = high.reshape(planes, height, depth), low.reshape(planes, height, depth)
            stacked = jnp.concatenate([high, low, high], 1)
            side_by_side = jnp.concatenate([stacked[q] for q in range(planes)], 1)
            result = jnp.dot(z_ref[scale], side_by_side, preferred_element_type=jnp.float32)
            put_resp(scale * 3 + channel, result)
            results.append(result)
        for number, (a, b) in enumerate(((0, 1), (0, 2), (1, 2))):
            put_other(scale * 3 + number, results[a] * results[b])
    for channel in range(3):
        put_other(RESP + channel, jnp.concatenate([own_ref[channel, q] for q in range(planes)], 1))
    put_other(RESP + 3, jnp.ones((height, planes * LANES), jnp.float32))

    sub = lax.broadcasted_iota(jnp.int32, (SLOTS, LANES), 0)
    group = 8
    steps = planes * half // group

    def block_sums(step, carry):
        plane = step // (half // group)
        base = step % (half // group) * group
        parts = []
        for g in range(group):
            zz = base + g
            tile = fields[pl.ds(pl.multiple_of((plane * half + zz) * ROWS, 8), ROWS), :]
            powers = []
            for piece in range(3):
                resp = tile[8 * piece : 8 * piece + 8]
                square = resp * resp
                powers.append((resp, square, square * resp, square * square))
            shared = powers[1]
            shifted = [pltpu.roll(value, 4, 0) for value in shared]
            mixed = [
                [jnp.where(sub < 4, shared[k], shifted[k + 1]) for k in (0, 2)],
                [jnp.where(sub < 4, shifted[k], shared[k + 1]) for k in (0, 2)],
            ]
            highs, lows = [], []
            for b in range(2):
                other = tile[2 * RESP + 16 * b : 2 * RESP + 16 * b + 16]
                high, low = halves(jnp.concatenate([*powers[2 * b], *mixed[b], other], 0))
                highs.append(high)
                lows.append(low)
            upper = (slots_ref[plane, pl.ds(zz, 1), :] == sub).astype(jnp.float32)
            lower = (slots_ref[plane, pl.ds(zz + half, 1), :] == sub).astype(jnp.float32)
            none = jnp.zeros_like(upper)
            hot = jnp.concatenate([jnp.concatenate([upper, none], 0), jnp.concatenate([none, lower], 0)], 1)
            hot = hot.astype(jnp.bfloat16)
            dims = (((1,), (1,)), ((), ()))
            parts.append(
                lax.dot_general(
                    jnp.concatenate(highs + lows, 1), jnp.concatenate([hot, hot], 1), dims, preferred_element_type=jnp.float32
                )
            )
        sums = jnp.concatenate(parts, 1)
        start = pl.multiple_of(step * (group * 2 * SLOTS), group * 2 * SLOTS)
        entries[pl.ds(start, group * 2 * SLOTS), :] = jnp.concatenate([sums, sums], 0).T
        for table in tables:
            rows = table.shape[0] // steps // 8 * 8
            table[pl.ds(pl.multiple_of(step * rows, 8), rows), :] = jnp.zeros((rows, LANES), jnp.float32)
        return carry

    lax.fori_loop(0, steps, block_sums, 0)

    def scatter(step, carry):
        base = step // SLOTS * (height * SLOTS) + step % SLOTS
        for column in range(height):
            table = tables[column % copies]
            target = pl.ds(target_ref[step, column], 1)
            source = pl.ds(base + (column % half * 2 + column // half) * SLOTS, 1)
            table[target, :] = table[target, :] + entries[source, :]
        return carry

    lax.fori_loop(0, planes * SLOTS, scatter, 0)

    kept = keep_ref.shape[0]
    places = kept // (2 * quarter)
    left = lax.broadcasted_iota(jnp.int32, (quarter, LANES), 1) < FEAT

    def combine(step, carry):
        for part in range(2):
            for out, first in ((keep_ref, 0), (send_ref, places)):
                row = pl.multiple_of((part * 2 * places + first + step) * 2 * quarter, 2 * quarter)
                total = tables[0][pl.ds(row, 2 * quarter), :]
                for table in tables[1:]:
                    total = total + table[pl.ds(row, 2 * quarter), :]
                place = pl.multiple_of((part * places + step) * quarter, quarter)
                out[pl.ds(place, quarter), :] = jnp.where(left, total[:quarter], total[quarter:])
        return carry

    lax.fori_loop(0, places, combine, 0)


def final_kernel(first_keep, first_got, second_keep, second_got, out_ref):
    quarter = first_keep.shape[0]
    moves = [(8 * k, 12 * k, 8) for k in range(4)] + [(32 + 4 * k, 12 * k + 8, 4) for k in range(4)] + [(48, 48, 16)]
    for number, (keep, got) in enumerate(((first_keep, first_got), (second_keep, second_got))):
        table = (keep[...] + got[...]).T
        for side in range(2):
            rows = table[side * FEAT : (side + 1) * FEAT]
            count = rows[FEAT - 1 :]
            lane = lax.broadcasted_iota(jnp.int32, rows.shape, 0)
            result = jnp.where(lane == FEAT - 1, jnp.log(1.0 + rows), rows / jnp.maximum(count, 1.0))
            columns = pl.ds((2 * number + side) * quarter, quarter)
            for source, target, length in moves:
                out_ref[target : target + length, columns] = result[source : source + length]


def shards(affinity, block_scale, slot_map, edge_list, valid_count, edge_home):
    planes, height, depth = affinity.shape[1:]
    owners = lax.axis_size("xy")
    rows_owned = edge_home.shape[0] // owners
    quarter = rows_owned // 4
    vmem = pl.BlockSpec(memory_space=pltpu.VMEM)
    smem = pl.BlockSpec(memory_space=pltpu.SMEM)

    dequant = affinity.astype(jnp.float32) * block_scale[..., None]
    up = [(i, i + 1) for i in range(owners - 1)]
    down = [(j, i) for i, j in up]
    before = lax.ppermute(dequant[:, planes - HALO :], "xy", up)
    after = lax.ppermute(dequant[:, :HALO], "xy", down)

    me = lax.axis_index("xy").astype(jnp.int32).reshape(1)
    lists = edge_list.transpose(0, 2, 1).reshape(planes * SLOTS, height)
    counts = jnp.broadcast_to(valid_count[:, None, :], (planes, SLOTS, height)).reshape(planes * SLOTS, height)
    index_shape = jax.ShapeDtypeStruct((planes * SLOTS, height), jnp.int32)
    target = pl.pallas_call(
        functools.partial(index_kernel, owners, rows_owned, height),
        out_shape=jax.ShapeDtypeStruct((planes * SLOTS, height), jnp.int32),
        in_specs=[smem, vmem, vmem, vmem],
        out_specs=vmem,
        name="index",
    )(me, lists, counts, edge_home.reshape(-1, LANES))

    along_y, along_z = filter_constants(height, depth)
    table_rows = owners * rows_owned
    copies = 4 if table_rows <= 8192 else 1
    table_shape = jax.ShapeDtypeStruct((owners * quarter, LANES), jnp.float32)
    keep, send = pl.pallas_call(
        functools.partial(main_kernel, copies, quarter),
        out_shape=(table_shape, table_shape),
        in_specs=[vmem] * 6 + [smem],
        out_specs=(vmem, vmem),
        scratch_shapes=[
            pltpu.VMEM((RESP, planes, height, depth), jnp.float32),
            pltpu.VMEM((planes * (height // 2) * ROWS, LANES), jnp.float32),
            pltpu.VMEM((planes * height * SLOTS, LANES), jnp.float32),
        ]
        + [pltpu.VMEM((table_rows + 8, LANES), jnp.float32)] * copies,
        compiler_params=pltpu.CompilerParams(vmem_limit_bytes=58 << 20),
        name="features",
    )(before, dequant, after, slot_map, jnp.asarray(along_y), jnp.asarray(along_z), target)

    def swap(value, bit):
        return lax.ppermute(value, "xy", [(i, i ^ (1 << bit)) for i in range(owners)])

    order_first, order_second = order_bits(owners)
    table = keep + swap(send, 0)
    first, second = table[: owners // 2 * quarter], table[owners // 2 * quarter :]
    for bit_first, bit_second in zip(order_first[1:], order_second[1:]):
        middle = first.shape[0] // 2
        got_first, got_second = swap(first[middle:], bit_first), swap(second[middle:], bit_second)
        first, second = first[:middle], second[:middle]
        if middle > quarter:
            first, second = first + got_first, second + got_second
    out = pl.pallas_call(
        final_kernel,
        out_shape=jax.ShapeDtypeStruct((FEAT, rows_owned), jnp.float32),
        in_specs=[vmem] * 4,
        out_specs=vmem,
        name="final",
    )(first, got_first, second, got_second)
    return out.T


def solution(mesh):
    in_specs = (
        P(None, ("parts", "xy"), None, None),
        P(None, ("parts", "xy"), None),
        P(("parts", "xy"), None, None),
        P(("parts", "xy"), None, None),
        P(("parts", "xy"), None),
        P("parts"),
    )
    out_specs = P(("parts", "xy"), None)
    return jax.shard_map(shards, mesh=mesh, in_specs=in_specs, out_specs=out_specs, check_vma=False)
```

```python
import functools

import jax
import jax.numpy as jnp
import numpy as np
from jax import lax
from jax.experimental import pallas as pl
from jax.experimental.pallas import tpu as pltpu
from jax.sharding import PartitionSpec as P

SLOTS = 8
HALO = 8
FEAT = 64
LANES = 128

sigma_list = (0.8, 1.3, 2.0, 3.0)
SCALES = len(sigma_list)
RESP = 3 * SCALES
ROWS = 2 * RESP + 2 * RESP + 8


def taps(sigma):
    offsets = np.arange(-HALO, HALO + 1).astype(np.float32)
    weights = np.exp(-offsets * offsets / np.float32(2.0 * sigma * sigma)).astype(np.float32)
    return (weights / weights.sum(dtype=np.float32)).astype(np.float32)


def band(weights, length):
    rows = np.arange(length)[:, None]
    cols = np.arange(length)[None, :]
    offset = cols - rows + HALO
    inside = (offset >= 0) & (offset <= 2 * HALO)
    return np.where(inside, weights[np.clip(offset, 0, 2 * HALO)], 0.0).astype(np.float32)


def halves(value):
    high = value.astype(jnp.bfloat16)
    low = (value - high.astype(jnp.float32)).astype(jnp.bfloat16)
    return high, low


def constant_halves(value):
    high = value.astype(jnp.bfloat16)
    low = (value - high.astype(np.float32)).astype(jnp.bfloat16)
    return high, low


def filter_constants(height, depth):
    along_y, along_z = [], []
    for sigma in sigma_list:
        high, low = constant_halves(band(taps(sigma), depth).T)
        along_y.append(np.concatenate([np.concatenate([high, low], 1), np.concatenate([high, np.zeros_like(low)], 1)], 0))
        high, low = constant_halves(band(taps(sigma), height))
        along_z.append(np.concatenate([high, high, low], 1))
    return np.stack(along_y), np.stack(along_z)


def order_bits(owners):
    bits = owners.bit_length() - 1
    first = list(range(bits))
    return first, [0] + first[2:] + first[1:2]


def index_kernel(owners, rows_owned, height, me_ref, edge_ref, count_ref, home_ref, target_ref):
    lists = edge_ref[...]
    both = jnp.concatenate([lists, lists], 1)
    high = both // LANES
    low = both % LANES

    def pick(row, found):
        line = jnp.broadcast_to(home_ref[pl.ds(row, 1), :], both.shape)
        return jnp.where(high == row, jnp.take_along_axis(line, low, axis=1), found)

    home = lax.fori_loop(0, home_ref.shape[0], pick, jnp.zeros(both.shape, jnp.int32))[:, :height]
    entry = lax.broadcasted_iota(jnp.int32, home.shape, 0)
    slot = entry % SLOTS
    owner = (home // rows_owned) ^ me_ref[0]
    within = home % rows_owned
    quarter = rows_owned // 4
    part = within // (2 * quarter)
    first, second = order_bits(owners)
    bits = len(first)
    place_first = jnp.zeros_like(owner)
    place_second = jnp.zeros_like(owner)
    for position in range(bits):
        place_first += ((owner >> first[position]) & 1) << (bits - 1 - position)
        place_second += ((owner >> second[position]) & 1) << (bits - 1 - position)
    place = jnp.where(part == 0, place_first, owners + place_second)
    row = place * (2 * quarter) + within % (2 * quarter)
    valid = slot < count_ref[...]
    target_ref[...] = jnp.where(valid, row, owners * rows_owned)


def main_kernel(
    copies, quarter, before_ref, own_ref, after_ref, slots_ref, y_ref, z_ref, target_ref, keep_ref, send_ref, *scratch
):
    blurred, fields, pending, entries = scratch[:4]
    tables = scratch[4:]
    planes, height, depth = own_ref.shape[1:]
    half = height // 2
    weights = [[float(w) for w in taps(sigma)] for sigma in sigma_list]
    tiles = height // 8
    cleared = tables[0].shape[0] // (3 * tiles)

    def across(step, carry):
        channel = step // tiles
        rows = pl.ds(pl.multiple_of(step % tiles * 8, 8), 8)
        values = [before_ref[channel, planes - HALO + p, rows, :] for p in range(HALO)]
        values += [own_ref[channel, p, rows, :] for p in range(planes)]
        values += [after_ref[channel, p, rows, :] for p in range(HALO)]
        for q in range(planes):
            center = q + HALO
            sums = [values[center]] + [values[center - t] + values[center + t] for t in range(1, HALO + 1)]
            for scale in range(SCALES):
                total = sums[0] * weights[scale][HALO]
                for t in range(1, HALO + 1):
                    total = total + sums[t] * weights[scale][HALO + t]
                blurred[scale * 3 + channel, q, rows, :] = total
        for table in tables:
            table[pl.ds(pl.multiple_of(step * cleared, 8), cleared), :] = jnp.zeros((cleared, LANES), jnp.float32)
        return carry

    lax.fori_loop(0, 3 * tiles, across, 0)

    def put(row_first, row_second, value):
        for q in range(planes):
            for b, row in enumerate((row_first, row_second)):
                start = q * half * ROWS + row
                fields[pl.ds(start, half, stride=ROWS), :] = value[b * half : (b + 1) * half, q * LANES : (q + 1) * LANES]

    def put_resp(number, value):
        put(number, 16 + number if number < 8 else 4 + number, value)

    def put_other(number, value):
        put(2 * RESP + number, 2 * RESP + 16 + number, value)

    for scale in range(SCALES):
        high, low = halves(blurred[3 * scale : 3 * scale + 3].reshape(3 * planes * height, depth))
        line = jnp.dot(jnp.concatenate([high, low], 1), y_ref[scale], preferred_element_type=jnp.float32)
        high, low = halves(line[:, :depth] + line[:, depth:])
        high, low = high.reshape(3 * planes, height, depth), low.reshape(3 * planes, height, depth)
        stacked = jnp.concatenate([high, low, high], 1)
        side_by_side = jnp.concatenate([stacked[p] for p in range(3 * planes)], 1)
        result = jnp.dot(z_ref[scale], side_by_side, preferred_element_type=jnp.float32)
        results = [result[:, c * planes * depth : (c + 1) * planes * depth] for c in range(3)]
        for channel in range(3):
            put_resp(scale * 3 + channel, results[channel])
        for number, (a, b) in enumerate(((0, 1), (0, 2), (1, 2))):
            put_other(scale * 3 + number, results[a] * results[b])
    for channel in range(3):
        put_other(RESP + channel, jnp.concatenate([own_ref[channel, q] for q in range(planes)], 1))
    put_other(RESP + 3, jnp.ones((height, planes * LANES), jnp.float32))

    sub = lax.broadcasted_iota(jnp.int32, (SLOTS, LANES), 0)
    group = LANES // (2 * SLOTS)
    owner_lane = lax.broadcasted_iota(jnp.int32, (FEAT, LANES), 1) // (2 * SLOTS)
    steps = planes * half // group

    def scatter(step):
        for number in range(LANES):
            table = tables[number % copies]
            target = pl.ds(target_ref[step, number], 1)
            table[target, :] = table[target, :] + entries[number : number + 1, :]

    def turn():
        sums = pending[...]
        entries[...] = jnp.concatenate([sums, sums], 0).T

    def block_sums(step):
        scatter(step)
        turn()
        plane = step // (half // group)
        base = step % (half // group) * group
        parts, hots = [], []
        for g in range(group):
            zz = base + g
            tile = fields[pl.ds(pl.multiple_of((plane * half + zz) * ROWS, 8), ROWS), :]
            powers = []
            for piece in range(3):
                resp = tile[8 * piece : 8 * piece + 8]
                square = resp * resp
                powers.append((resp, square, square * resp, square * square))
            shared = powers[1]
            shifted = [pltpu.roll(value, 4, 0) for value in shared]
            mixed = [
                [jnp.where(sub < 4, shared[k], shifted[k + 1]) for k in (0, 2)],
                [jnp.where(sub < 4, shifted[k], shared[k + 1]) for k in (0, 2)],
            ]
            highs, lows = [], []
            for b in range(2):
                other = tile[2 * RESP + 16 * b : 2 * RESP + 16 * b + 16]
                high, low = halves(jnp.concatenate([*powers[2 * b], *mixed[b], other], 0))
                highs.append(high)
                lows.append(low)
            upper = (slots_ref[plane, pl.ds(zz, 1), :] == sub).astype(jnp.float32)
            lower = (slots_ref[plane, pl.ds(zz + half, 1), :] == sub).astype(jnp.float32)
            none = jnp.zeros_like(upper)
            hots += [jnp.concatenate([upper, none], 1), jnp.concatenate([none, lower], 1)]
            parts += [jnp.concatenate(highs, 1), jnp.concatenate(lows, 1)]
        hot = jnp.concatenate(hots, 0).astype(jnp.bfloat16)
        dims = (((1,), (1,)), ((), ()))
        products = lax.dot_general(jnp.concatenate(parts, 0), hot, dims, preferred_element_type=jnp.float32)
        sums = jnp.zeros((FEAT, LANES), jnp.float32)
        for g in range(group):
            own = products[2 * g * FEAT : (2 * g + 1) * FEAT] + products[(2 * g + 1) * FEAT : (2 * g + 2) * FEAT]
            sums = jnp.where(owner_lane == g, own, sums)
        pending[...] = sums

    unroll = 2 if steps % 2 == 0 else 1

    def several(step, carry):
        for number in range(unroll):
            block_sums(step * unroll + number)
        return carry

    lax.fori_loop(0, steps // unroll, several, 0)
    scatter(steps)
    turn()
    scatter(steps + 1)

    kept = keep_ref.shape[0]
    places = kept // (2 * quarter)
    left = lax.broadcasted_iota(jnp.int32, (quarter, LANES), 1) < FEAT

    def combine(step, carry):
        for part in range(2):
            for out, first in ((keep_ref, 0), (send_ref, places)):
                row = pl.multiple_of((part * 2 * places + first + step) * 2 * quarter, 2 * quarter)
                total = tables[0][pl.ds(row, 2 * quarter), :]
                for table in tables[1:]:
                    total = total + table[pl.ds(row, 2 * quarter), :]
                place = pl.multiple_of((part * places + step) * quarter, quarter)
                out[pl.ds(place, quarter), :] = jnp.where(left, total[:quarter], total[quarter:])
        return carry

    lax.fori_loop(0, places, combine, 0)


def add_kernel(layers, *refs):
    ins, outs = refs[:-2], refs[-2:]
    count = len(ins) // 2
    for number, out in enumerate(outs):
        total = None
        for ref, start in zip(ins[number * count : (number + 1) * count], layers[number]):
            piece = ref[start : start + out.shape[0], :]
            total = piece if total is None else total + piece
        out[...] = total


def final_kernel(layers, *refs):
    ins, out_ref = refs[:-1], refs[-1]
    count = len(ins) // 2
    quarter = ins[count - 1].shape[0]
    moves = [(8 * k, 12 * k, 8) for k in range(4)] + [(32 + 4 * k, 12 * k + 8, 4) for k in range(4)] + [(48, 48, 16)]
    for number in range(2):
        table = None
        for ref, start in zip(ins[number * count : (number + 1) * count], layers[number]):
            piece = ref[start : start + quarter, :]
            table = piece if table is None else table + piece
        table = table.T
        for side in range(2):
            rows = table[side * FEAT : (side + 1) * FEAT]
            count_row = rows[FEAT - 1 :]
            lane = lax.broadcasted_iota(jnp.int32, rows.shape, 0)
            result = jnp.where(lane == FEAT - 1, jnp.log(1.0 + rows), rows / jnp.maximum(count_row, 1.0))
            columns = pl.ds((2 * number + side) * quarter, quarter)
            for source, target, length in moves:
                out_ref[target : target + length, columns] = result[source : source + length]


def on_chip(value):
    return pltpu.with_memory_space_constraint(value, pltpu.VMEM)


def shards(affinity, block_scale, slot_map, edge_list, valid_count, edge_home):
    planes, height, depth = affinity.shape[1:]
    owners = lax.axis_size("xy")
    rows_owned = edge_home.shape[0] // owners
    quarter = rows_owned // 4
    vmem = pl.BlockSpec(memory_space=pltpu.VMEM)
    smem = pl.BlockSpec(memory_space=pltpu.SMEM)

    dequant = affinity.astype(jnp.float32) * block_scale[..., None]
    up = [(i, i + 1) for i in range(owners - 1)]
    down = [(j, i) for i, j in up]
    before = on_chip(lax.ppermute(dequant[:, planes - HALO :], "xy", up))
    after = on_chip(lax.ppermute(dequant[:, :HALO], "xy", down))

    me = lax.axis_index("xy").astype(jnp.int32).reshape(1)
    lists = edge_list.transpose(0, 2, 1).reshape(planes * SLOTS, height)
    counts = jnp.broadcast_to(valid_count[:, None, :], (planes, SLOTS, height)).reshape(planes * SLOTS, height)
    index_shape = jax.ShapeDtypeStruct((planes * SLOTS, height), jnp.int32)
    target = pl.pallas_call(
        functools.partial(index_kernel, owners, rows_owned, height),
        out_shape=jax.ShapeDtypeStruct((planes * SLOTS, height), jnp.int32),
        in_specs=[smem, vmem, vmem, vmem],
        out_specs=vmem,
        name="index",
    )(me, lists, counts, edge_home.reshape(-1, LANES))

    target = target.reshape(planes, SLOTS, 2, height // 2).transpose(0, 3, 2, 1).reshape(-1, LANES)
    target = jnp.pad(target, ((2, 0), (0, 0)), constant_values=owners * rows_owned)

    along_y, along_z = filter_constants(height, depth)
    table_rows = owners * rows_owned
    copies = 4 if table_rows <= 8192 else 1
    clear_steps = 3 * height // 8
    cleared = -(-(table_rows + 8) // (8 * clear_steps)) * 8
    table_shape = jax.ShapeDtypeStruct((owners * quarter, LANES), jnp.float32)
    keep, send = pl.pallas_call(
        functools.partial(main_kernel, copies, quarter),
        out_shape=(table_shape, table_shape),
        in_specs=[vmem] * 6 + [smem],
        out_specs=(vmem, vmem),
        scratch_shapes=[
            pltpu.VMEM((RESP, planes, height, depth), jnp.float32),
            pltpu.VMEM((planes * (height // 2) * ROWS, LANES), jnp.float32),
            pltpu.VMEM((FEAT, LANES), jnp.float32),
            pltpu.VMEM((LANES, LANES), jnp.float32),
        ]
        + [pltpu.VMEM((clear_steps * cleared, LANES), jnp.float32)] * copies,
        compiler_params=pltpu.CompilerParams(vmem_limit_bytes=44 << 20),
        name="features",
    )(before, on_chip(dequant), after, slot_map, jnp.asarray(along_y), jnp.asarray(along_z), target)

    small = table_rows <= 8192
    near = on_chip if small else lambda value: value

    def swap(value, bit):
        return near(lax.ppermute(value, "xy", [(i, i ^ (1 << bit)) for i in range(owners)]))

    order_first, order_second = order_bits(owners)
    whole = owners // 2 * quarter
    got = swap(send, 0)
    keep = near(keep)
    first, second = [keep, got], [keep, got]
    starts = ([0, 0], [whole, whole])
    middle = whole
    for bit_first, bit_second in zip(order_first[1:], order_second[1:]):
        middle //= 2
        layers = tuple(tuple(start + middle for start in part) for part in starts)
        shape = jax.ShapeDtypeStruct((middle, LANES), jnp.float32)
        send_first, send_second = pl.pallas_call(
            functools.partial(add_kernel, layers),
            out_shape=(shape, shape),
            in_specs=[vmem] * (2 * len(first)),
            out_specs=(vmem, vmem),
            name="add",
        )(*first, *second)
        first, second = first + [swap(send_first, bit_first)], second + [swap(send_second, bit_second)]
        starts = (starts[0] + [0], starts[1] + [0])
    out = pl.pallas_call(
        functools.partial(final_kernel, starts),
        out_shape=jax.ShapeDtypeStruct((FEAT, rows_owned), jnp.float32),
        in_specs=[vmem] * (2 * len(first)),
        out_specs=vmem,
        name="final",
    )(*first, *second)
    return out.T


def solution(mesh):
    in_specs = (
        P(None, ("parts", "xy"), None, None),
        P(None, ("parts", "xy"), None),
        P(("parts", "xy"), None, None),
        P(("parts", "xy"), None, None),
        P(("parts", "xy"), None),
        P("parts"),
    )
    out_specs = P(("parts", "xy"), None)
    return jax.shard_map(shards, mesh=mesh, in_specs=in_specs, out_specs=out_specs, check_vma=False)
```

```python
import functools

import jax
import jax.numpy as jnp
import numpy as np
from jax import lax
from jax.experimental import pallas as pl
from jax.experimental.pallas import tpu as pltpu
from jax.sharding import PartitionSpec as P


SLOTS = 8
HALO = 8
FEAT = 64
LANES = 128

sigma_list = (0.8, 1.3, 2.0, 3.0)
SCALES = len(sigma_list)
RESP = 3 * SCALES


def taps(sigma):
    offsets = np.arange(-HALO, HALO + 1).astype(np.float32)
    weights = np.exp(-offsets * offsets / np.float32(2.0 * sigma * sigma)).astype(np.float32)
    return (weights / weights.sum(dtype=np.float32)).astype(np.float32)


def band(weights, length):
    rows = np.arange(length)[:, None]
    cols = np.arange(length)[None, :]
    offset = cols - rows + HALO
    inside = (offset >= 0) & (offset <= 2 * HALO)
    return np.where(inside, weights[np.clip(offset, 0, 2 * HALO)], 0.0).astype(np.float32)


def halves(value):
    high = value.astype(jnp.bfloat16)
    low = (value - high.astype(jnp.float32)).astype(jnp.bfloat16)
    return high, low


def constant_halves(value):
    high = value.astype(jnp.bfloat16)
    low = (value - high.astype(np.float32)).astype(jnp.bfloat16)
    return high, low


def filter_constants(height, depth):
    along_y, along_z = [], []
    for sigma in sigma_list:
        high, low = constant_halves(band(taps(sigma), depth).T)
        along_y.append(np.concatenate([np.concatenate([high, low], 1), np.concatenate([high, np.zeros_like(low)], 1)], 0))
        high, low = constant_halves(band(taps(sigma), height))
        along_z.append(np.concatenate([high, high, low], 1))
    return np.stack(along_y), np.stack(along_z)


def order_bits(owners):
    bits = owners.bit_length() - 1
    first = list(range(bits))
    return first, [0] + first[2:] + first[1:2]


def put(fields, row, value, planes, half):
    for q in range(planes):
        for b in range(2):
            fields[pl.ds(q * half * 8 + b * 4 + row, half, stride=8), :] = value(q)[b * half : (b + 1) * half]


def prepare_kernel(owners, rows_owned, height, me_ref, edge_ref, count_ref, home_ref, own_ref, target_ref, raw_ref):
    planes = own_ref.shape[1]
    for channel in range(3):
        put(raw_ref, channel, lambda q: own_ref[channel, q], planes, height // 2)
    put(raw_ref, 3, lambda q: jnp.ones((height, LANES), jnp.float32), planes, height // 2)
    lists = edge_ref[...]
    both = jnp.concatenate([lists, lists], 1)
    high = both // LANES
    low = both % LANES

    def pick(row, found):
        line = jnp.broadcast_to(home_ref[pl.ds(row, 1), :], both.shape)
        return jnp.where(high == row, jnp.take_along_axis(line, low, axis=1), found)

    home = lax.fori_loop(0, home_ref.shape[0], pick, jnp.zeros(both.shape, jnp.int32))[:, :height]
    entry = lax.broadcasted_iota(jnp.int32, home.shape, 0)
    slot = entry % SLOTS
    owner = (home // rows_owned) ^ me_ref[0]
    within = home % rows_owned
    quarter = rows_owned // 4
    part = within // (2 * quarter)
    first, second = order_bits(owners)
    bits = len(first)
    place_first = jnp.zeros_like(owner)
    place_second = jnp.zeros_like(owner)
    for position in range(bits):
        place_first += ((owner >> first[position]) & 1) << (bits - 1 - position)
        place_second += ((owner >> second[position]) & 1) << (bits - 1 - position)
    place = jnp.where(part == 0, place_first, owners + place_second)
    row = place * (2 * quarter) + within % (2 * quarter)
    valid = slot < count_ref[...]
    target_ref[...] = jnp.where(valid, row, owners * rows_owned)


def blur(before_ref, own_ref, after_ref, y_ref, z_ref, fields, blurred, tables):
    planes, height, depth = own_ref.shape
    weights = [[float(w) for w in taps(sigma)] for sigma in sigma_list]
    tiles = height // 8
    cleared = tables[0].shape[0] // tiles if tables else 0

    def across(step, carry):
        rows = pl.ds(pl.multiple_of(step * 8, 8), 8)
        values = [before_ref[planes - HALO + p, rows, :] for p in range(HALO)]
        values += [own_ref[p, rows, :] for p in range(planes)]
        values += [after_ref[p, rows, :] for p in range(HALO)]
        for q in range(planes):
            center = q + HALO
            sums = [values[center]] + [values[center - t] + values[center + t] for t in range(1, HALO + 1)]
            for scale in range(SCALES):
                total = sums[0] * weights[scale][HALO]
                for t in range(1, HALO + 1):
                    total = total + sums[t] * weights[scale][HALO + t]
                blurred[scale, q, rows, :] = total
        for table in tables:
            table[pl.ds(pl.multiple_of(step * cleared, 8), cleared), :] = jnp.zeros((cleared, LANES), jnp.float32)
        return carry

    lax.fori_loop(0, tiles, across, 0)
    lines = []
    for scale in range(SCALES):
        high, low = halves(blurred[scale].reshape(planes * height, depth))
        line = jnp.dot(jnp.concatenate([high, low], 1), y_ref[scale], preferred_element_type=jnp.float32)
        lines.append(line[:, :depth] + line[:, depth:])
    for scale in range(SCALES):
        high, low = halves(lines[scale])
        high, low = high.reshape(planes, height, depth), low.reshape(planes, height, depth)
        stacked = jnp.concatenate([high, low, high], 1)
        side_by_side = jnp.concatenate([stacked[q] for q in range(planes)], 1)
        result = jnp.dot(z_ref[scale], side_by_side, preferred_element_type=jnp.float32)
        put(fields, scale, lambda q: result[:, q * depth : (q + 1) * depth], planes, height // 2)


def blur_kernel(before_ref, own_ref, after_ref, y_ref, z_ref, fields, blurred):
    blur(before_ref, own_ref, after_ref, y_ref, z_ref, fields, blurred, [])


def main_kernel(
    copies, quarter, before_ref, own_ref, after_ref, y_ref, z_ref, zero_ref, one_ref, raw_ref, slots_ref, target_ref,
    keep_ref, send_ref, *scratch
):
    blurred, two_ref, pending, entries = scratch[:4]
    tables = scratch[4:]
    planes, height, depth = own_ref.shape
    half = height // 2
    blur(before_ref, own_ref, after_ref, y_ref, z_ref, two_ref, blurred, tables)

    sub = lax.broadcasted_iota(jnp.int32, (SLOTS, LANES), 0)
    group = LANES // (2 * SLOTS)
    owner_row = lax.broadcasted_iota(jnp.int32, (2 * FEAT, LANES), 0) % 8 // 4
    owner_lane = lax.broadcasted_iota(jnp.int32, (2 * FEAT, LANES), 1) // SLOTS
    owner = owner_lane - owner_row
    steps = planes * half // group

    def scatter(step):
        for number in range(LANES):
            table = tables[number % copies]
            target = pl.ds(target_ref[step, number], 1)
            table[target, :] = table[target, :] + entries[number : number + 1, :]

    def turn():
        sums = pending[...]
        entries[...] = jnp.concatenate([sums, sums], 0).T

    def block_sums(step):
        scatter(step)
        turn()
        plane = step // (half // group)
        base = step % (half // group) * group
        parts, hots = [], []
        for g in range(group):
            zz = base + g
            rows = pl.ds(pl.multiple_of((plane * half + zz) * 8, 8), 8)
            resp = [ref[rows, :] for ref in (zero_ref, one_ref, two_ref)]
            square = [r * r for r in resp]
            cube = [s * r for s, r in zip(square, resp)]
            fourth = [s * s for s in square]
            pairs = [resp[a] * resp[b] for a, b in ((0, 1), (0, 2), (1, 2))]
            high, low = halves(jnp.concatenate([*resp, *square, *cube, *fourth, *pairs, raw_ref[rows, :]], 0))
            parts.append(jnp.concatenate([high, low], 1))
            hots.append((slots_ref[plane, pl.ds(zz, 1), :] == sub).astype(jnp.float32))
            hots.append((slots_ref[plane, pl.ds(zz + half, 1), :] == sub).astype(jnp.float32))
        hot = jnp.concatenate(hots, 0).astype(jnp.bfloat16)
        dims = (((1,), (1,)), ((), ()))
        products = lax.dot_general(
            jnp.concatenate(parts, 0), jnp.concatenate([hot, hot], 1), dims, preferred_element_type=jnp.float32
        )
        sums = jnp.zeros((2 * FEAT, LANES), jnp.float32)
        for g in range(group):
            sums = jnp.where(owner == 2 * g, products[2 * g * FEAT : (2 * g + 2) * FEAT], sums)
        folded = []
        for number in range(2 * FEAT // 8):
            piece = sums[8 * number : 8 * number + 8]
            folded.append(piece + pltpu.roll(piece, 4, 0))
        pending[...] = jnp.concatenate(
            [jnp.where(sub < 4, folded[k], folded[k + 1]) for k in range(0, len(folded), 2)], 0
        )

    unroll = 2 if steps % 2 == 0 else 1

    def several(step, carry):
        for number in range(unroll):
            block_sums(step * unroll + number)
        return carry

    lax.fori_loop(0, steps // unroll, several, 0)
    scatter(steps)
    turn()
    scatter(steps + 1)

    kept = keep_ref.shape[0]
    places = kept // (2 * quarter)
    left = lax.broadcasted_iota(jnp.int32, (quarter, LANES), 1) < FEAT

    def combine(step, carry):
        for part in range(2):
            for out, first in ((keep_ref, 0), (send_ref, places)):
                row = pl.multiple_of((part * 2 * places + first + step) * 2 * quarter, 2 * quarter)
                total = tables[0][pl.ds(row, 2 * quarter), :]
                for table in tables[1:]:
                    total = total + table[pl.ds(row, 2 * quarter), :]
                place = pl.multiple_of((part * places + step) * quarter, quarter)
                out[pl.ds(place, quarter), :] = jnp.where(left, total[:quarter], total[quarter:])
        return carry

    lax.fori_loop(0, places, combine, 0)


def add_kernel(layers, *refs):
    ins, outs = refs[:-2], refs[-2:]
    count = len(ins) // 2
    for number, out in enumerate(outs):
        total = None
        for ref, start in zip(ins[number * count : (number + 1) * count], layers[number]):
            piece = ref[start : start + out.shape[0], :]
            total = piece if total is None else total + piece
        out[...] = total


def final_kernel(layers, *refs):
    ins, out_ref, ordered = refs[:-2], refs[-2], refs[-1]
    count = len(ins) // 2
    quarter = ins[count - 1].shape[0]
    for number in range(2):
        table = None
        for ref, start in zip(ins[number * count : (number + 1) * count], layers[number]):
            piece = ref[start : start + quarter, :]
            table = piece if table is None else table + piece
        table = table.T
        for side in range(2):
            rows = table[side * FEAT : (side + 1) * FEAT]
            count_row = rows[FEAT - 1 :]
            lane = lax.broadcasted_iota(jnp.int32, rows.shape, 0)
            result = jnp.where(lane == FEAT - 1, jnp.log(1.0 + rows), rows / jnp.maximum(count_row, 1.0))
            columns = pl.ds((2 * number + side) * quarter, quarter)
            first_row = (2 * number + side) * FEAT
            for kind in range(15):
                ordered[pl.ds(first_row + kind // 3 * RESP + kind % 3, SCALES, stride=3), :] = result[4 * kind : 4 * kind + 4]
            ordered[first_row + FEAT - 4 : first_row + FEAT, :] = result[FEAT - 4 :]
            out_ref[:, columns] = ordered[first_row : first_row + FEAT, :]


def on_chip(value):
    return pltpu.with_memory_space_constraint(value, pltpu.VMEM)


def shards(affinity, block_scale, slot_map, edge_list, valid_count, edge_home):
    planes, height, depth = affinity.shape[1:]
    owners = lax.axis_size("xy")
    rows_owned = edge_home.shape[0] // owners
    quarter = rows_owned // 4
    vmem = pl.BlockSpec(memory_space=pltpu.VMEM)
    smem = pl.BlockSpec(memory_space=pltpu.SMEM)

    small = owners * rows_owned <= 8192

    def room(mib):
        return pltpu.CompilerParams(vmem_limit_bytes=mib << 20) if small else None

    dequant = affinity.astype(jnp.float32) * block_scale[..., None]
    up = [(i, i + 1) for i in range(owners - 1)]
    down = [(j, i) for i, j in up]
    before, after = [], []
    for channel in range(3):
        before.append(on_chip(lax.ppermute(dequant[channel, planes - HALO :], "xy", up)))
        after.append(on_chip(lax.ppermute(dequant[channel, :HALO], "xy", down)))

    me = lax.axis_index("xy").astype(jnp.int32).reshape(1)
    lists = edge_list.transpose(0, 2, 1).reshape(planes * SLOTS, height)
    counts = jnp.broadcast_to(valid_count[:, None, :], (planes, SLOTS, height)).reshape(planes * SLOTS, height)
    index_shape = jax.ShapeDtypeStruct((planes * SLOTS, height), jnp.int32)
    field_shape = jax.ShapeDtypeStruct((planes * height * 4, LANES), jnp.float32)
    target, raw = pl.pallas_call(
        functools.partial(prepare_kernel, owners, rows_owned, height),
        out_shape=(jax.ShapeDtypeStruct((planes * SLOTS, height), jnp.int32), field_shape),
        in_specs=[smem] + [vmem] * 4,
        out_specs=(vmem, vmem),
        compiler_params=room(6),
        name="prepare",
    )(me, lists, counts, edge_home.reshape(-1, LANES), dequant)
    target = target.reshape(planes, SLOTS, 2, height // 2).transpose(0, 3, 2, 1).reshape(-1, LANES)
    target = jnp.pad(target, ((2, 0), (0, 0)), constant_values=owners * rows_owned)

    along_y, along_z = filter_constants(height, depth)
    table_rows = owners * rows_owned
    copies = 4 if table_rows <= 8192 else 1
    clear_steps = height // 8
    cleared = -(-(table_rows + 8) // (8 * clear_steps)) * 8
    blurred = pltpu.VMEM((SCALES, planes, height, depth), jnp.float32)
    filters = (on_chip(jnp.asarray(along_y)), on_chip(jnp.asarray(along_z)))
    fields = []
    for channel in range(2):
        fields.append(
            on_chip(
                pl.pallas_call(
                    blur_kernel,
                    out_shape=field_shape,
                    in_specs=[vmem] * 5,
                    out_specs=vmem,
                    scratch_shapes=[blurred],
                    compiler_params=room(10),
                    name="blur",
                )(before[channel], on_chip(dequant[channel]), after[channel], *filters)
            )
        )
    table_shape = jax.ShapeDtypeStruct((owners * quarter, LANES), jnp.float32)
    keep, send = pl.pallas_call(
        functools.partial(main_kernel, copies, quarter),
        out_shape=(table_shape, table_shape),
        in_specs=[vmem] * 9 + [smem],
        out_specs=(vmem, vmem),
        scratch_shapes=[
            blurred,
            pltpu.VMEM(field_shape.shape, jnp.float32),
            pltpu.VMEM((FEAT, LANES), jnp.float32),
            pltpu.VMEM((LANES, LANES), jnp.float32),
        ]
        + [pltpu.VMEM((clear_steps * cleared, LANES), jnp.float32)] * copies,
        compiler_params=pltpu.CompilerParams(vmem_limit_bytes=44 << 20),
        name="features",
    )(before[2], on_chip(dequant[2]), after[2], *filters, *fields, on_chip(raw), on_chip(slot_map), target)

    near = on_chip if small else lambda value: value

    def swap(value, bit):
        return near(lax.ppermute(value, "xy", [(i, i ^ (1 << bit)) for i in range(owners)]))

    order_first, order_second = order_bits(owners)
    whole = owners // 2 * quarter
    got = swap(send, 0)
    keep = near(keep)
    first, second = [keep, got], [keep, got]
    starts = ([0, 0], [whole, whole])
    middle = whole
    for bit_first, bit_second in zip(order_first[1:], order_second[1:]):
        middle //= 2
        layers = tuple(tuple(start + middle for start in part) for part in starts)
        shape = jax.ShapeDtypeStruct((middle, LANES), jnp.float32)
        send_first, send_second = pl.pallas_call(
            functools.partial(add_kernel, layers),
            out_shape=(shape, shape),
            in_specs=[vmem] * (2 * len(first)),
            out_specs=(vmem, vmem),
            compiler_params=room(10),
            name="add",
        )(*first, *second)
        first, second = first + [swap(send_first, bit_first)], second + [swap(send_second, bit_second)]
        starts = (starts[0] + [0], starts[1] + [0])
    out = pl.pallas_call(
        functools.partial(final_kernel, starts),
        out_shape=jax.ShapeDtypeStruct((FEAT, rows_owned), jnp.float32),
        in_specs=[vmem] * (2 * len(first)),
        out_specs=vmem,
        scratch_shapes=[pltpu.VMEM((4 * FEAT, LANES), jnp.float32)],
        compiler_params=room(10),
        name="final",
    )(*first, *second)
    return out.T


def solution(mesh):
    in_specs = (
        P(None, ("parts", "xy"), None, None),
        P(None, ("parts", "xy"), None),
        P(("parts", "xy"), None, None),
        P(("parts", "xy"), None, None),
        P(("parts", "xy"), None),
        P("parts"),
    )
    out_specs = P(("parts", "xy"), None)
    return jax.shard_map(shards, mesh=mesh, in_specs=in_specs, out_specs=out_specs, check_vma=False)
```

```python
import functools

import jax
import jax.numpy as jnp
import numpy as np
from jax import lax
from jax.experimental import pallas as pl
from jax.experimental.pallas import tpu as pltpu
from jax.sharding import PartitionSpec as P


SLOTS = 8
HALO = 8
FEAT = 64
LANES = 128

sigma_list = (0.8, 1.3, 2.0, 3.0)
SCALES = len(sigma_list)
RESP = 3 * SCALES


def taps(sigma):
    offsets = np.arange(-HALO, HALO + 1).astype(np.float32)
    weights = np.exp(-offsets * offsets / np.float32(2.0 * sigma * sigma)).astype(np.float32)
    return (weights / weights.sum(dtype=np.float32)).astype(np.float32)


def band(weights, length):
    rows = np.arange(length)[:, None]
    cols = np.arange(length)[None, :]
    offset = cols - rows + HALO
    inside = (offset >= 0) & (offset <= 2 * HALO)
    return np.where(inside, weights[np.clip(offset, 0, 2 * HALO)], 0.0).astype(np.float32)


def halves(value):
    high = value.astype(jnp.bfloat16)
    low = (value - high.astype(jnp.float32)).astype(jnp.bfloat16)
    return high, low


def constant_halves(value):
    high = value.astype(jnp.bfloat16)
    low = (value - high.astype(np.float32)).astype(jnp.bfloat16)
    return high, low


def filter_constants(height, depth):
    along_y, along_z = [], []
    for sigma in sigma_list:
        high, low = constant_halves(band(taps(sigma), depth).T)
        along_y.append(np.concatenate([np.concatenate([high, low], 1), np.concatenate([high, np.zeros_like(low)], 1)], 0))
        high, low = constant_halves(band(taps(sigma), height))
        along_z.append(np.concatenate([high, high, low], 1))
    return np.stack(along_y), np.stack(along_z)


def order_bits(owners):
    bits = owners.bit_length() - 1
    first = list(range(bits))
    return first, [0] + first[2:] + first[1:2]


def put(fields, row, value, planes, half):
    for q in range(planes):
        for b in range(2):
            fields[pl.ds(q * half * 8 + b * 4 + row, half, stride=8), :] = value(q)[b * half : (b + 1) * half]


def prepare_kernel(owners, rows_owned, height, me_ref, edge_ref, count_ref, home_ref, pair_ref, last_ref, target_ref, raw_ref):
    planes = last_ref.shape[1]
    for channel in range(3):
        own_ref = pair_ref.at[channel] if channel < 2 else last_ref.at[0]
        put(raw_ref, channel, lambda q: own_ref[q], planes, height // 2)
    put(raw_ref, 3, lambda q: jnp.ones((height, LANES), jnp.float32), planes, height // 2)
    lists = edge_ref[...]
    both = jnp.concatenate([lists, lists], 1)
    high = both // LANES
    low = both % LANES

    def pick(row, found):
        line = jnp.broadcast_to(home_ref[pl.ds(row, 1), :], both.shape)
        return jnp.where(high == row, jnp.take_along_axis(line, low, axis=1), found)

    home = lax.fori_loop(0, home_ref.shape[0], pick, jnp.zeros(both.shape, jnp.int32))[:, :height]
    entry = lax.broadcasted_iota(jnp.int32, home.shape, 0)
    slot = entry % SLOTS
    owner = (home // rows_owned) ^ me_ref[0]
    within = home % rows_owned
    quarter = rows_owned // 4
    part = within // (2 * quarter)
    first, second = order_bits(owners)
    bits = len(first)
    place_first = jnp.zeros_like(owner)
    place_second = jnp.zeros_like(owner)
    for position in range(bits):
        place_first += ((owner >> first[position]) & 1) << (bits - 1 - position)
        place_second += ((owner >> second[position]) & 1) << (bits - 1 - position)
    place = jnp.where(part == 0, place_first, owners + place_second)
    row = place * (2 * quarter) + within % (2 * quarter)
    valid = slot < count_ref[...]
    target_ref[...] = jnp.where(valid, row, owners * rows_owned)


def blur(before_ref, own_ref, after_ref, y_ref, z_ref, fields, blurred, tables):
    planes, height, depth = own_ref.shape
    weights = [[float(w) for w in taps(sigma)] for sigma in sigma_list]
    tiles = height // 8
    cleared = tables[0].shape[0] // tiles if tables else 0

    def across(step, carry):
        rows = pl.ds(pl.multiple_of(step * 8, 8), 8)
        values = [before_ref[planes - HALO + p, rows, :] for p in range(HALO)]
        values += [own_ref[p, rows, :] for p in range(planes)]
        values += [after_ref[p, rows, :] for p in range(HALO)]
        for q in range(planes):
            center = q + HALO
            sums = [values[center]] + [values[center - t] + values[center + t] for t in range(1, HALO + 1)]
            for scale in range(SCALES):
                total = sums[0] * weights[scale][HALO]
                for t in range(1, HALO + 1):
                    total = total + sums[t] * weights[scale][HALO + t]
                blurred[scale, q, rows, :] = total
        for table in tables:
            table[pl.ds(pl.multiple_of(step * cleared, 8), cleared), :] = jnp.zeros((cleared, LANES), jnp.float32)
        return carry

    lax.fori_loop(0, tiles, across, 0)
    lines = []
    for scale in range(SCALES):
        high, low = halves(blurred[scale].reshape(planes * height, depth))
        line = jnp.dot(jnp.concatenate([high, low], 1), y_ref[scale], preferred_element_type=jnp.float32)
        lines.append(line[:, :depth] + line[:, depth:])
    for scale in range(SCALES):
        high, low = halves(lines[scale])
        high, low = high.reshape(planes, height, depth), low.reshape(planes, height, depth)
        stacked = jnp.concatenate([high, low, high], 1)
        side_by_side = jnp.concatenate([stacked[q] for q in range(planes)], 1)
        result = jnp.dot(z_ref[scale], side_by_side, preferred_element_type=jnp.float32)
        put(fields, scale, lambda q: result[:, q * depth : (q + 1) * depth], planes, height // 2)


def blur_kernel(before_ref, own_ref, after_ref, y_ref, z_ref, zero_ref, one_ref, blurred):
    for channel, fields in enumerate((zero_ref, one_ref)):
        refs = [ref.at[channel] for ref in (before_ref, own_ref, after_ref)]
        blur(*refs, y_ref, z_ref, fields, blurred, [])


def main_kernel(
    copies, quarter, before_ref, own_ref, after_ref, y_ref, z_ref, zero_ref, one_ref, raw_ref, slots_ref, target_ref,
    keep_ref, send_ref, *scratch
):
    blurred, two_ref, pending, entries = scratch[:4]
    tables = scratch[4:]
    planes, height, depth = own_ref.shape[1:]
    half = height // 2
    blur(before_ref.at[0], own_ref.at[0], after_ref.at[0], y_ref, z_ref, two_ref, blurred, tables)

    sub = lax.broadcasted_iota(jnp.int32, (SLOTS, LANES), 0)
    group = LANES // (2 * SLOTS)
    owner_row = lax.broadcasted_iota(jnp.int32, (2 * FEAT, LANES), 0) % 8 // 4
    owner_lane = lax.broadcasted_iota(jnp.int32, (2 * FEAT, LANES), 1) // SLOTS
    owner = owner_lane - owner_row
    steps = planes * half // group

    def scatter(step):
        for number in range(LANES):
            table = tables[number % copies]
            target = pl.ds(target_ref[step, number], 1)
            table[target, :] = table[target, :] + entries[number : number + 1, :]

    def turn():
        sums = pending[...]
        entries[...] = jnp.concatenate([sums, sums], 0).T

    def block_sums(step):
        scatter(step)
        turn()
        plane = step // (half // group)
        base = step % (half // group) * group
        parts, hots = [], []
        for g in range(group):
            zz = base + g
            rows = pl.ds(pl.multiple_of((plane * half + zz) * 8, 8), 8)
            resp = [ref[rows, :] for ref in (zero_ref, one_ref, two_ref)]
            square = [r * r for r in resp]
            cube = [s * r for s, r in zip(square, resp)]
            fourth = [s * s for s in square]
            pairs = [resp[a] * resp[b] for a, b in ((0, 1), (0, 2), (1, 2))]
            high, low = halves(jnp.concatenate([*resp, *square, *cube, *fourth, *pairs, raw_ref[rows, :]], 0))
            parts.append(jnp.concatenate([high, low], 1))
            hots.append((slots_ref[plane, pl.ds(zz, 1), :] == sub).astype(jnp.float32))
            hots.append((slots_ref[plane, pl.ds(zz + half, 1), :] == sub).astype(jnp.float32))
        hot = jnp.concatenate(hots, 0).astype(jnp.bfloat16)
        dims = (((1,), (1,)), ((), ()))
        products = lax.dot_general(
            jnp.concatenate(parts, 0), jnp.concatenate([hot, hot], 1), dims, preferred_element_type=jnp.float32
        )
        sums = jnp.zeros((2 * FEAT, LANES), jnp.float32)
        for g in range(group):
            sums = jnp.where(owner == 2 * g, products[2 * g * FEAT : (2 * g + 2) * FEAT], sums)
        folded = []
        for number in range(2 * FEAT // 8):
            piece = sums[8 * number : 8 * number + 8]
            folded.append(piece + pltpu.roll(piece, 4, 0))
        pending[...] = jnp.concatenate(
            [jnp.where(sub < 4, folded[k], folded[k + 1]) for k in range(0, len(folded), 2)], 0
        )

    unroll = 2 if steps % 2 == 0 else 1

    def several(step, carry):
        for number in range(unroll):
            block_sums(step * unroll + number)
        return carry

    lax.fori_loop(0, steps // unroll, several, 0)
    scatter(steps)
    turn()
    scatter(steps + 1)

    kept = keep_ref.shape[0]
    places = kept // (2 * quarter)
    left = lax.broadcasted_iota(jnp.int32, (quarter, LANES), 1) < FEAT

    def combine(step, carry):
        for part in range(2):
            for out, first in ((keep_ref, 0), (send_ref, places)):
                row = pl.multiple_of((part * 2 * places + first + step) * 2 * quarter, 2 * quarter)
                total = tables[0][pl.ds(row, 2 * quarter), :]
                for table in tables[1:]:
                    total = total + table[pl.ds(row, 2 * quarter), :]
                place = pl.multiple_of((part * places + step) * quarter, quarter)
                out[pl.ds(place, quarter), :] = jnp.where(left, total[:quarter], total[quarter:])
        return carry

    lax.fori_loop(0, places, combine, 0)


def add_kernel(layers, *refs):
    ins, outs = refs[:-2], refs[-2:]
    count = len(ins) // 2
    for number, out in enumerate(outs):
        total = None
        for ref, start in zip(ins[number * count : (number + 1) * count], layers[number]):
            piece = ref[start : start + out.shape[0], :]
            total = piece if total is None else total + piece
        out[...] = total


def final_kernel(layers, *refs):
    ins, out_ref, ordered = refs[:-2], refs[-2], refs[-1]
    count = len(ins) // 2
    quarter = ins[count - 1].shape[0]
    for number in range(2):
        table = None
        for ref, start in zip(ins[number * count : (number + 1) * count], layers[number]):
            piece = ref[start : start + quarter, :]
            table = piece if table is None else table + piece
        table = table.T
        for side in range(2):
            rows = table[side * FEAT : (side + 1) * FEAT]
            count_row = rows[FEAT - 1 :]
            lane = lax.broadcasted_iota(jnp.int32, rows.shape, 0)
            result = jnp.where(lane == FEAT - 1, jnp.log(1.0 + rows), rows / jnp.maximum(count_row, 1.0))
            columns = pl.ds((2 * number + side) * quarter, quarter)
            first_row = (2 * number + side) * FEAT
            for kind in range(15):
                ordered[pl.ds(first_row + kind // 3 * RESP + kind % 3, SCALES, stride=3), :] = result[4 * kind : 4 * kind + 4]
            ordered[first_row + FEAT - 4 : first_row + FEAT, :] = result[FEAT - 4 :]
            out_ref[:, columns] = ordered[first_row : first_row + FEAT, :]


def on_chip(value):
    return pltpu.with_memory_space_constraint(value, pltpu.VMEM)


def shards(affinity, block_scale, slot_map, edge_list, valid_count, edge_home):
    planes, height, depth = affinity.shape[1:]
    owners = lax.axis_size("xy")
    rows_owned = edge_home.shape[0] // owners
    quarter = rows_owned // 4
    vmem = pl.BlockSpec(memory_space=pltpu.VMEM)
    smem = pl.BlockSpec(memory_space=pltpu.SMEM)

    small = owners * rows_owned <= 8192

    def room(mib):
        return pltpu.CompilerParams(vmem_limit_bytes=mib << 20) if small else None

    up = [(i, i + 1) for i in range(owners - 1)]
    down = [(j, i) for i, j in up]
    scaled, before, after = [], [], []
    for part in (slice(0, 2), slice(2, 3)):
        value = affinity[part].astype(jnp.float32) * block_scale[part, :, :, None]
        scaled.append(on_chip(value))
        before.append(on_chip(lax.ppermute(value[:, planes - HALO :], "xy", up)))
        after.append(on_chip(lax.ppermute(value[:, :HALO], "xy", down)))

    me = lax.axis_index("xy").astype(jnp.int32).reshape(1)
    lists = edge_list.transpose(0, 2, 1).reshape(planes * SLOTS, height)
    counts = jnp.broadcast_to(valid_count[:, None, :], (planes, SLOTS, height)).reshape(planes * SLOTS, height)
    index_shape = jax.ShapeDtypeStruct((planes * SLOTS, height), jnp.int32)
    field_shape = jax.ShapeDtypeStruct((planes * height * 4, LANES), jnp.float32)
    target, raw = pl.pallas_call(
        functools.partial(prepare_kernel, owners, rows_owned, height),
        out_shape=(jax.ShapeDtypeStruct((planes * SLOTS, height), jnp.int32), field_shape),
        in_specs=[smem] + [vmem] * 5,
        out_specs=(vmem, vmem),
        compiler_params=room(6),
        name="prepare",
    )(me, lists, counts, edge_home.reshape(-1, LANES), *scaled)
    target = target.reshape(planes, SLOTS, 2, height // 2).transpose(0, 3, 2, 1).reshape(-1, LANES)
    target = jnp.pad(target, ((2, 0), (0, 0)), constant_values=owners * rows_owned)

    along_y, along_z = filter_constants(height, depth)
    table_rows = owners * rows_owned
    copies = 4 if table_rows <= 8192 else 1
    clear_steps = height // 8
    cleared = -(-(table_rows + 8) // (8 * clear_steps)) * 8
    blurred = pltpu.VMEM((SCALES, planes, height, depth), jnp.float32)
    filters = (on_chip(jnp.asarray(along_y)), on_chip(jnp.asarray(along_z)))
    fields = pl.pallas_call(
        blur_kernel,
        out_shape=(field_shape, field_shape),
        in_specs=[vmem] * 5,
        out_specs=(vmem, vmem),
        scratch_shapes=[blurred],
        compiler_params=room(12),
        name="blur",
    )(before[0], scaled[0], after[0], *filters)
    table_shape = jax.ShapeDtypeStruct((owners * quarter, LANES), jnp.float32)
    keep, send = pl.pallas_call(
        functools.partial(main_kernel, copies, quarter),
        out_shape=(table_shape, table_shape),
        in_specs=[vmem] * 9 + [smem],
        out_specs=(vmem, vmem),
        scratch_shapes=[
            blurred,
            pltpu.VMEM(field_shape.shape, jnp.float32),
            pltpu.VMEM((FEAT, LANES), jnp.float32),
            pltpu.VMEM((LANES, LANES), jnp.float32),
        ]
        + [pltpu.VMEM((clear_steps * cleared, LANES), jnp.float32)] * copies,
        compiler_params=pltpu.CompilerParams(vmem_limit_bytes=44 << 20),
        name="features",
    )(before[1], scaled[1], after[1], *filters, *map(on_chip, fields), on_chip(raw), on_chip(slot_map), target)

    near = on_chip if small else lambda value: value

    def swap(value, bit):
        return near(lax.ppermute(value, "xy", [(i, i ^ (1 << bit)) for i in range(owners)]))

    order_first, order_second = order_bits(owners)
    whole = owners // 2 * quarter
    got = swap(send, 0)
    keep = near(keep)
    first, second = [keep, got], [keep, got]
    starts = ([0, 0], [whole, whole])
    middle = whole
    for bit_first, bit_second in zip(order_first[1:], order_second[1:]):
        middle //= 2
        layers = tuple(tuple(start + middle for start in part) for part in starts)
        shape = jax.ShapeDtypeStruct((middle, LANES), jnp.float32)
        send_first, send_second = pl.pallas_call(
            functools.partial(add_kernel, layers),
            out_shape=(shape, shape),
            in_specs=[vmem] * (2 * len(first)),
            out_specs=(vmem, vmem),
            compiler_params=room(10),
            name="add",
        )(*first, *second)
        first, second = first + [swap(send_first, bit_first)], second + [swap(send_second, bit_second)]
        starts = (starts[0] + [0], starts[1] + [0])
    out = pl.pallas_call(
        functools.partial(final_kernel, starts),
        out_shape=jax.ShapeDtypeStruct((FEAT, rows_owned), jnp.float32),
        in_specs=[vmem] * (2 * len(first)),
        out_specs=vmem,
        scratch_shapes=[pltpu.VMEM((4 * FEAT, LANES), jnp.float32)],
        compiler_params=room(10),
        name="final",
    )(*first, *second)
    return out.T


def solution(mesh):
    in_specs = (
        P(None, ("parts", "xy"), None, None),
        P(None, ("parts", "xy"), None),
        P(("parts", "xy"), None, None),
        P(("parts", "xy"), None, None),
        P(("parts", "xy"), None),
        P("parts"),
    )
    out_specs = P(("parts", "xy"), None)
    return jax.shard_map(shards, mesh=mesh, in_specs=in_specs, out_specs=out_specs, check_vma=False)
```

```python
import functools

import jax
import jax.numpy as jnp
import numpy as np
from jax import lax
from jax.experimental import pallas as pl
from jax.experimental.pallas import tpu as pltpu
from jax.sharding import PartitionSpec as P


SLOTS = 8
HALO = 8
FEAT = 64
LANES = 128

sigma_list = (0.8, 1.3, 2.0, 3.0)
SCALES = len(sigma_list)
RESP = 3 * SCALES


def taps(sigma):
    offsets = np.arange(-HALO, HALO + 1).astype(np.float32)
    weights = np.exp(-offsets * offsets / np.float32(2.0 * sigma * sigma)).astype(np.float32)
    return (weights / weights.sum(dtype=np.float32)).astype(np.float32)


def band(weights, length):
    rows = np.arange(length)[:, None]
    cols = np.arange(length)[None, :]
    offset = cols - rows + HALO
    inside = (offset >= 0) & (offset <= 2 * HALO)
    return np.where(inside, weights[np.clip(offset, 0, 2 * HALO)], 0.0).astype(np.float32)


def halves(value):
    high = value.astype(jnp.bfloat16)
    low = (value - high.astype(jnp.float32)).astype(jnp.bfloat16)
    return high, low


def constant_halves(value):
    high = value.astype(jnp.bfloat16)
    low = (value - high.astype(np.float32)).astype(jnp.bfloat16)
    return high, low


def filter_constants(height, depth):
    along_y, along_z = [], []
    for sigma in sigma_list:
        high, low = constant_halves(band(taps(sigma), depth).T)
        along_y.append(np.concatenate([np.concatenate([high, low], 1), np.concatenate([high, np.zeros_like(low)], 1)], 0))
        high, low = constant_halves(band(taps(sigma), height))
        along_z.append(np.concatenate([high, high, low], 1))
    return np.stack(along_y), np.stack(along_z)


def order_bits(owners):
    bits = owners.bit_length() - 1
    first = list(range(bits))
    return first, [0] + first[2:] + first[1:2]


def put(fields, row, value, planes, half):
    for q in range(planes):
        for b in range(2):
            fields[pl.ds(q * half * 8 + b * 4 + row, half, stride=8), :] = value(q)[b * half : (b + 1) * half]


def prepare_kernel(owners, rows_owned, height, me_ref, edge_ref, count_ref, home_ref, pair_ref, last_ref, target_ref, raw_ref):
    planes = last_ref.shape[1]
    for channel in range(3):
        own_ref = pair_ref.at[channel] if channel < 2 else last_ref.at[0]
        put(raw_ref, channel, lambda q: own_ref[q], planes, height // 2)
    put(raw_ref, 3, lambda q: jnp.ones((height, LANES), jnp.float32), planes, height // 2)
    entry_rows = edge_ref.shape[0] // 2
    both = jnp.concatenate([edge_ref[:entry_rows, :], edge_ref[entry_rows:, :]], 1)
    high = both // LANES
    low = both % LANES

    def pick(step, found):
        start = pl.multiple_of(step * 8, 8)
        lines = home_ref[pl.ds(start, 8), :]
        for number in range(8):
            line = jnp.broadcast_to(lines[number : number + 1], both.shape)
            found = jnp.where(high == start + number, jnp.take_along_axis(line, low, axis=1), found)
        return found

    found = lax.fori_loop(0, home_ref.shape[0] // 8, pick, jnp.zeros(both.shape, jnp.int32))
    home = jnp.concatenate([found[:, :height], found[:, height:]], 0)
    entry = lax.broadcasted_iota(jnp.int32, home.shape, 0)
    slot = entry % SLOTS
    owner = (home // rows_owned) ^ me_ref[0]
    within = home % rows_owned
    quarter = rows_owned // 4
    part = within // (2 * quarter)
    first, second = order_bits(owners)
    bits = len(first)
    place_first = jnp.zeros_like(owner)
    place_second = jnp.zeros_like(owner)
    for position in range(bits):
        place_first += ((owner >> first[position]) & 1) << (bits - 1 - position)
        place_second += ((owner >> second[position]) & 1) << (bits - 1 - position)
    place = jnp.where(part == 0, place_first, owners + place_second)
    row = place * (2 * quarter) + within % (2 * quarter)
    valid = slot < count_ref[...]
    target_ref[:, :height] = jnp.where(valid, row, owners * rows_owned)


def blur(before_ref, own_ref, after_ref, y_ref, z_ref, fields, blurred, tables):
    planes, height, depth = own_ref.shape
    weights = [[float(w) for w in taps(sigma)] for sigma in sigma_list]
    tiles = height // 8
    cleared = tables[0].shape[0] // tiles if tables else 0

    def across(step, carry):
        rows = pl.ds(pl.multiple_of(step * 8, 8), 8)
        values = [before_ref[planes - HALO + p, rows, :] for p in range(HALO)]
        values += [own_ref[p, rows, :] for p in range(planes)]
        values += [after_ref[p, rows, :] for p in range(HALO)]
        for q in range(planes):
            center = q + HALO
            sums = [values[center]] + [values[center - t] + values[center + t] for t in range(1, HALO + 1)]
            for scale in range(SCALES):
                total = sums[0] * weights[scale][HALO]
                for t in range(1, HALO + 1):
                    total = total + sums[t] * weights[scale][HALO + t]
                blurred[scale, q, rows, :] = total
        for table in tables:
            table[pl.ds(pl.multiple_of(step * cleared, 8), cleared), :] = jnp.zeros((cleared, LANES), jnp.float32)
        return carry

    lax.fori_loop(0, tiles, across, 0)
    lines = []
    for scale in range(SCALES):
        high, low = halves(blurred[scale].reshape(planes * height, depth))
        line = jnp.dot(jnp.concatenate([high, low], 1), y_ref[scale], preferred_element_type=jnp.float32)
        lines.append(line[:, :depth] + line[:, depth:])
    for scale in range(SCALES):
        high, low = halves(lines[scale])
        high, low = high.reshape(planes, height, depth), low.reshape(planes, height, depth)
        stacked = jnp.concatenate([high, low, high], 1)
        side_by_side = jnp.concatenate([stacked[q] for q in range(planes)], 1)
        result = jnp.dot(z_ref[scale], side_by_side, preferred_element_type=jnp.float32)
        put(fields, scale, lambda q: result[:, q * depth : (q + 1) * depth], planes, height // 2)


def blur_kernel(before_ref, own_ref, after_ref, y_ref, z_ref, zero_ref, one_ref, blurred):
    for channel, fields in enumerate((zero_ref, one_ref)):
        refs = [ref.at[channel] for ref in (before_ref, own_ref, after_ref)]
        blur(*refs, y_ref, z_ref, fields, blurred, [])


def main_kernel(
    copies, quarter, before_ref, own_ref, after_ref, y_ref, z_ref, zero_ref, one_ref, raw_ref, slots_ref, target_ref,
    keep_ref, send_ref, *scratch
):
    blurred, two_ref, pending, entries = scratch[:4]
    tables = scratch[4:]
    planes, height, depth = own_ref.shape[1:]
    half = height // 2
    blur(before_ref.at[0], own_ref.at[0], after_ref.at[0], y_ref, z_ref, two_ref, blurred, tables)

    sub = lax.broadcasted_iota(jnp.int32, (SLOTS, LANES), 0)
    group = LANES // (2 * SLOTS)
    owner_row = lax.broadcasted_iota(jnp.int32, (2 * FEAT, LANES), 0) % 8 // 4
    owner_lane = lax.broadcasted_iota(jnp.int32, (2 * FEAT, LANES), 1) // SLOTS
    owner = owner_lane - owner_row
    steps = planes * half // group

    def scatter(step):
        plane = step // (half // group)
        base = plane * (SLOTS * LANES) + step % (half // group) * group
        for number in range(LANES):
            pair, block, slot = number // (2 * SLOTS), number // SLOTS % 2, number % SLOTS
            table = tables[number % copies]
            target = pl.ds(target_ref[base + (slot * LANES + block * half + pair)], 1)
            table[target, :] = table[target, :] + entries[number : number + 1, :]

    def turn():
        sums = pending[...]
        entries[...] = jnp.concatenate([sums, sums], 0).T

    pending[...] = jnp.zeros_like(pending)
    entries[...] = jnp.zeros_like(entries)

    def block_sums(step):
        scatter(jnp.maximum(step - 2, 0))
        turn()
        plane = step // (half // group)
        base = step % (half // group) * group
        parts, hots = [], []
        for g in range(group):
            zz = base + g
            rows = pl.ds(pl.multiple_of((plane * half + zz) * 8, 8), 8)
            resp = [ref[rows, :] for ref in (zero_ref, one_ref, two_ref)]
            square = [r * r for r in resp]
            cube = [s * r for s, r in zip(square, resp)]
            fourth = [s * s for s in square]
            pairs = [resp[a] * resp[b] for a, b in ((0, 1), (0, 2), (1, 2))]
            high, low = halves(jnp.concatenate([*resp, *square, *cube, *fourth, *pairs, raw_ref[rows, :]], 0))
            parts.append(jnp.concatenate([high, low], 1))
            hots.append((slots_ref[plane, pl.ds(zz, 1), :] == sub).astype(jnp.float32))
            hots.append((slots_ref[plane, pl.ds(zz + half, 1), :] == sub).astype(jnp.float32))
        hot = jnp.concatenate(hots, 0).astype(jnp.bfloat16)
        dims = (((1,), (1,)), ((), ()))
        products = lax.dot_general(
            jnp.concatenate(parts, 0), jnp.concatenate([hot, hot], 1), dims, preferred_element_type=jnp.float32
        )
        sums = jnp.zeros((2 * FEAT, LANES), jnp.float32)
        for g in range(group):
            sums = jnp.where(owner == 2 * g, products[2 * g * FEAT : (2 * g + 2) * FEAT], sums)
        folded = []
        for number in range(2 * FEAT // 8):
            piece = sums[8 * number : 8 * number + 8]
            folded.append(piece + pltpu.roll(piece, 4, 0))
        pending[...] = jnp.concatenate(
            [jnp.where(sub < 4, folded[k], folded[k + 1]) for k in range(0, len(folded), 2)], 0
        )

    unroll = 2 if steps % 2 == 0 else 1

    def several(step, carry):
        for number in range(unroll):
            block_sums(step * unroll + number)
        return carry

    lax.fori_loop(0, steps // unroll, several, 0)
    scatter(steps - 2)
    turn()
    scatter(steps - 1)

    kept = keep_ref.shape[0]
    places = kept // (2 * quarter)
    left = lax.broadcasted_iota(jnp.int32, (quarter, LANES), 1) < FEAT

    def combine(step, carry):
        for part in range(2):
            for out, first in ((keep_ref, 0), (send_ref, places)):
                row = pl.multiple_of((part * 2 * places + first + step) * 2 * quarter, 2 * quarter)
                total = tables[0][pl.ds(row, 2 * quarter), :]
                for table in tables[1:]:
                    total = total + table[pl.ds(row, 2 * quarter), :]
                place = pl.multiple_of((part * places + step) * quarter, quarter)
                out[pl.ds(place, quarter), :] = jnp.where(left, total[:quarter], total[quarter:])
        return carry

    lax.fori_loop(0, places, combine, 0)


def add_kernel(layers, *refs):
    ins, outs = refs[:-2], refs[-2:]
    count = len(ins) // 2
    for number, out in enumerate(outs):
        total = None
        for ref, start in zip(ins[number * count : (number + 1) * count], layers[number]):
            piece = ref[start : start + out.shape[0], :]
            total = piece if total is None else total + piece
        out[...] = total


def final_kernel(layers, *refs):
    ins, out_ref, ordered = refs[:-2], refs[-2], refs[-1]
    count = len(ins) // 2
    quarter = ins[count - 1].shape[0]
    for number in range(2):
        table = None
        for ref, start in zip(ins[number * count : (number + 1) * count], layers[number]):
            piece = ref[start : start + quarter, :]
            table = piece if table is None else table + piece
        table = table.T
        for side in range(2):
            rows = table[side * FEAT : (side + 1) * FEAT]
            count_row = rows[FEAT - 1 :]
            lane = lax.broadcasted_iota(jnp.int32, rows.shape, 0)
            result = jnp.where(lane == FEAT - 1, jnp.log(1.0 + rows), rows / jnp.maximum(count_row, 1.0))
            columns = pl.ds((2 * number + side) * quarter, quarter)
            first_row = (2 * number + side) * FEAT
            for kind in range(15):
                ordered[pl.ds(first_row + kind // 3 * RESP + kind % 3, SCALES, stride=3), :] = result[4 * kind : 4 * kind + 4]
            ordered[first_row + FEAT - 4 : first_row + FEAT, :] = result[FEAT - 4 :]
            out_ref[:, columns] = ordered[first_row : first_row + FEAT, :]


def on_chip(value):
    return pltpu.with_memory_space_constraint(value, pltpu.VMEM)


def shards(affinity, block_scale, slot_map, edge_list, valid_count, edge_home):
    planes, height, depth = affinity.shape[1:]
    owners = lax.axis_size("xy")
    rows_owned = edge_home.shape[0] // owners
    quarter = rows_owned // 4
    vmem = pl.BlockSpec(memory_space=pltpu.VMEM)
    smem = pl.BlockSpec(memory_space=pltpu.SMEM)

    small = owners * rows_owned <= 8192

    def room(mib):
        return pltpu.CompilerParams(vmem_limit_bytes=mib << 20) if small else None

    up = [(i, i + 1) for i in range(owners - 1)]
    down = [(j, i) for i, j in up]
    scaled, before, after = [], [], []
    dequant = affinity.astype(jnp.float32) * block_scale[..., None]
    for part in (slice(0, 2), slice(2, 3)):
        value = dequant[part]
        scaled.append(on_chip(value))
        before.append(on_chip(lax.ppermute(value[:, planes - HALO :], "xy", up)))
        after.append(on_chip(lax.ppermute(value[:, :HALO], "xy", down)))

    me = lax.axis_index("xy").astype(jnp.int32).reshape(1)
    lists = edge_list.transpose(0, 2, 1).reshape(planes * SLOTS, height)
    counts = jnp.broadcast_to(valid_count[:, None, :], (planes, SLOTS, height)).reshape(planes * SLOTS, height)
    index_shape = jax.ShapeDtypeStruct((planes * SLOTS, height), jnp.int32)
    field_shape = jax.ShapeDtypeStruct((planes * height * 4, LANES), jnp.float32)
    target, raw = pl.pallas_call(
        functools.partial(prepare_kernel, owners, rows_owned, height),
        out_shape=(jax.ShapeDtypeStruct((planes * SLOTS, LANES), jnp.int32), field_shape),
        in_specs=[smem] + [vmem] * 5,
        out_specs=(vmem, vmem),
        compiler_params=room(6),
        name="prepare",
    )(me, lists, counts, edge_home.reshape(-1, LANES), *scaled)
    along_y, along_z = filter_constants(height, depth)
    table_rows = owners * rows_owned
    copies = 4 if table_rows <= 8192 else 1
    clear_steps = height // 8
    cleared = -(-(table_rows + 8) // (8 * clear_steps)) * 8
    blurred = pltpu.VMEM((SCALES, planes, height, depth), jnp.float32)
    filters = (on_chip(jnp.asarray(along_y)), on_chip(jnp.asarray(along_z)))
    fields = pl.pallas_call(
        blur_kernel,
        out_shape=(field_shape, field_shape),
        in_specs=[vmem] * 5,
        out_specs=(vmem, vmem),
        scratch_shapes=[blurred],
        compiler_params=room(12),
        name="blur",
    )(before[0], scaled[0], after[0], *filters)
    table_shape = jax.ShapeDtypeStruct((owners * quarter, LANES), jnp.float32)
    keep, send = pl.pallas_call(
        functools.partial(main_kernel, copies, quarter),
        out_shape=(table_shape, table_shape),
        in_specs=[vmem] * 9 + [smem],
        out_specs=(vmem, vmem),
        scratch_shapes=[
            blurred,
            pltpu.VMEM(field_shape.shape, jnp.float32),
            pltpu.VMEM((FEAT, LANES), jnp.float32),
            pltpu.VMEM((LANES, LANES), jnp.float32),
        ]
        + [pltpu.VMEM((clear_steps * cleared, LANES), jnp.float32)] * copies,
        compiler_params=pltpu.CompilerParams(vmem_limit_bytes=44 << 20),
        name="features",
    )(before[1], scaled[1], after[1], *filters, *map(on_chip, fields), on_chip(raw), on_chip(slot_map), target.reshape(-1))

    near = on_chip if small else lambda value: value

    def swap(value, bit):
        return near(lax.ppermute(value, "xy", [(i, i ^ (1 << bit)) for i in range(owners)]))

    order_first, order_second = order_bits(owners)
    whole = owners // 2 * quarter
    got = swap(send, 0)
    keep = near(keep)
    first, second = [keep, got], [keep, got]
    starts = ([0, 0], [whole, whole])
    middle = whole
    for bit_first, bit_second in zip(order_first[1:], order_second[1:]):
        middle //= 2
        layers = tuple(tuple(start + middle for start in part) for part in starts)
        shape = jax.ShapeDtypeStruct((middle, LANES), jnp.float32)
        send_first, send_second = pl.pallas_call(
            functools.partial(add_kernel, layers),
            out_shape=(shape, shape),
            in_specs=[vmem] * (2 * len(first)),
            out_specs=(vmem, vmem),
            compiler_params=room(10),
            name="add",
        )(*first, *second)
        first, second = first + [swap(send_first, bit_first)], second + [swap(send_second, bit_second)]
        starts = (starts[0] + [0], starts[1] + [0])
    out = pl.pallas_call(
        functools.partial(final_kernel, starts),
        out_shape=jax.ShapeDtypeStruct((FEAT, rows_owned), jnp.float32),
        in_specs=[vmem] * (2 * len(first)),
        out_specs=vmem,
        scratch_shapes=[pltpu.VMEM((4 * FEAT, LANES), jnp.float32)],
        compiler_params=room(10),
        name="final",
    )(*first, *second)
    return out.T


def solution(mesh):
    in_specs = (
        P(None, ("parts", "xy"), None, None),
        P(None, ("parts", "xy"), None),
        P(("parts", "xy"), None, None),
        P(("parts", "xy"), None, None),
        P(("parts", "xy"), None),
        P("parts"),
    )
    out_specs = P(("parts", "xy"), None)
    return jax.shard_map(shards, mesh=mesh, in_specs=in_specs, out_specs=out_specs, check_vma=False)
```

```python
import functools

import jax
import jax.numpy as jnp
import numpy as np
from jax import lax
from jax.experimental import pallas as pl
from jax.experimental.pallas import tpu as pltpu
from jax.sharding import PartitionSpec as P


SLOTS = 8
HALO = 8
FEAT = 64
LANES = 128

sigma_list = (0.8, 1.3, 2.0, 3.0)
SCALES = len(sigma_list)
RESP = 3 * SCALES


def taps(sigma):
    offsets = np.arange(-HALO, HALO + 1).astype(np.float32)
    weights = np.exp(-offsets * offsets / np.float32(2.0 * sigma * sigma)).astype(np.float32)
    return (weights / weights.sum(dtype=np.float32)).astype(np.float32)


def band(weights, length):
    rows = np.arange(length)[:, None]
    cols = np.arange(length)[None, :]
    offset = cols - rows + HALO
    inside = (offset >= 0) & (offset <= 2 * HALO)
    return np.where(inside, weights[np.clip(offset, 0, 2 * HALO)], 0.0).astype(np.float32)


def halves(value):
    high = value.astype(jnp.bfloat16)
    low = (value - high.astype(jnp.float32)).astype(jnp.bfloat16)
    return high, low


def constant_halves(value):
    high = value.astype(jnp.bfloat16)
    low = (value - high.astype(np.float32)).astype(jnp.bfloat16)
    return high, low


def filter_constants(height, depth):
    along_y, along_z = [], []
    for sigma in sigma_list:
        high, low = constant_halves(band(taps(sigma), depth).T)
        along_y.append(np.concatenate([np.concatenate([high, low], 1), np.concatenate([high, np.zeros_like(low)], 1)], 0))
        high, low = constant_halves(band(taps(sigma), height))
        along_z.append(np.concatenate([high, high, low], 1))
    return np.stack(along_y), np.stack(along_z)


def order_bits(owners):
    bits = owners.bit_length() - 1
    first = list(range(bits))
    return first, [0] + first[2:] + first[1:2]


def put(fields, row, value, planes, half):
    for q in range(planes):
        for b in range(2):
            fields[pl.ds(q * half * 8 + b * 4 + row, half, stride=8), :] = value(q)[b * half : (b + 1) * half]


def clear(tables):
    for table in tables:

        def some(step, carry, table=table):
            table[pl.ds(pl.multiple_of(step * 256, 256), 256), :] = jnp.zeros((256, LANES), jnp.float32)
            return carry

        lax.fori_loop(0, table.shape[0] // 256, some, 0)


def prepare_kernel(owners, rows_owned, height, me_ref, edge_ref, count_ref, home_ref, pair_ref, last_ref, target_ref, raw_ref, *tables):
    planes = last_ref.shape[1]
    clear(tables)
    for channel in range(3):
        own_ref = pair_ref.at[channel] if channel < 2 else last_ref.at[0]
        put(raw_ref, channel, lambda q: own_ref[q], planes, height // 2)
    put(raw_ref, 3, lambda q: jnp.ones((height, LANES), jnp.float32), planes, height // 2)
    entry_rows = edge_ref.shape[0] // 2
    both = jnp.concatenate([edge_ref[:entry_rows, :], edge_ref[entry_rows:, :]], 1)
    high = both // LANES
    low = both % LANES

    def pick(step, found):
        start = pl.multiple_of(step * 8, 8)
        lines = home_ref[pl.ds(start, 8), :]
        for number in range(8):
            line = jnp.broadcast_to(lines[number : number + 1], both.shape)
            found = jnp.where(high == start + number, jnp.take_along_axis(line, low, axis=1), found)
        return found

    found = lax.fori_loop(0, home_ref.shape[0] // 8, pick, jnp.zeros(both.shape, jnp.int32))
    home = jnp.concatenate([found[:, :height], found[:, height:]], 0)
    entry = lax.broadcasted_iota(jnp.int32, home.shape, 0)
    slot = entry % SLOTS
    owner = (home // rows_owned) ^ me_ref[0]
    within = home % rows_owned
    quarter = rows_owned // 4
    part = within // (2 * quarter)
    first, second = order_bits(owners)
    bits = len(first)
    place_first = jnp.zeros_like(owner)
    place_second = jnp.zeros_like(owner)
    for position in range(bits):
        place_first += ((owner >> first[position]) & 1) << (bits - 1 - position)
        place_second += ((owner >> second[position]) & 1) << (bits - 1 - position)
    place = jnp.where(part == 0, place_first, owners + place_second)
    row = place * (2 * quarter) + within % (2 * quarter)
    valid = slot < count_ref[...]
    target_ref[:, :height] = jnp.where(valid, row, owners * rows_owned)


def blur(before_ref, own_ref, after_ref, y_ref, z_ref, fields, blurred):
    planes, height, depth = own_ref.shape
    weights = [[float(w) for w in taps(sigma)] for sigma in sigma_list]
    tiles = height // 8

    def across(step, carry):
        rows = pl.ds(pl.multiple_of(step * 8, 8), 8)
        values = [before_ref[planes - HALO + p, rows, :] for p in range(HALO)]
        values += [own_ref[p, rows, :] for p in range(planes)]
        values += [after_ref[p, rows, :] for p in range(HALO)]
        for q in range(planes):
            center = q + HALO
            sums = [values[center]] + [values[center - t] + values[center + t] for t in range(1, HALO + 1)]
            for scale in range(SCALES):
                total = sums[0] * weights[scale][HALO]
                for t in range(1, HALO + 1):
                    total = total + sums[t] * weights[scale][HALO + t]
                blurred[scale, q, rows, :] = total
        return carry

    lax.fori_loop(0, tiles, across, 0)
    lines = []
    for scale in range(SCALES):
        high, low = halves(blurred[scale].reshape(planes * height, depth))
        line = jnp.dot(jnp.concatenate([high, low], 1), y_ref[scale], preferred_element_type=jnp.float32)
        lines.append(line[:, :depth] + line[:, depth:])
    for scale in range(SCALES):
        high, low = halves(lines[scale])
        high, low = high.reshape(planes, height, depth), low.reshape(planes, height, depth)
        stacked = jnp.concatenate([high, low, high], 1)
        side_by_side = jnp.concatenate([stacked[q] for q in range(planes)], 1)
        result = jnp.dot(z_ref[scale], side_by_side, preferred_element_type=jnp.float32)
        put(fields, scale, lambda q: result[:, q * depth : (q + 1) * depth], planes, height // 2)


def blur_kernel(before_ref, own_ref, after_ref, y_ref, z_ref, zero_ref, one_ref, blurred):
    for channel, fields in enumerate((zero_ref, one_ref)):
        refs = [ref.at[channel] for ref in (before_ref, own_ref, after_ref)]
        blur(*refs, y_ref, z_ref, fields, blurred)


def main_kernel(
    given, quarter, before_ref, own_ref, after_ref, y_ref, z_ref, zero_ref, one_ref, raw_ref, slots_ref, target_ref, *refs
):
    keep_ref, send_ref, *tables = refs[given : 2 * given + 2]
    blurred, two_ref, pending, entries, *own_tables = refs[2 * given + 2 :]
    clear(own_tables)
    tables += own_tables
    copies = len(tables)
    planes, height, depth = own_ref.shape[1:]
    half = height // 2
    blur(before_ref.at[0], own_ref.at[0], after_ref.at[0], y_ref, z_ref, two_ref, blurred)

    sub = lax.broadcasted_iota(jnp.int32, (SLOTS, LANES), 0)
    group = LANES // (2 * SLOTS)
    owner_row = lax.broadcasted_iota(jnp.int32, (2 * FEAT, LANES), 0) % 8 // 4
    owner_lane = lax.broadcasted_iota(jnp.int32, (2 * FEAT, LANES), 1) // SLOTS
    owner = owner_lane - owner_row
    steps = planes * half // group

    def scatter(step):
        plane = step // (half // group)
        base = plane * (SLOTS * LANES) + step % (half // group) * group
        for number in range(LANES):
            pair, block, slot = number // (2 * SLOTS), number // SLOTS % 2, number % SLOTS
            table = tables[number % copies]
            target = pl.ds(target_ref[base + (slot * LANES + block * half + pair)], 1)
            table[target, :] = table[target, :] + entries[number : number + 1, :]

    def turn():
        sums = pending[...]
        entries[...] = jnp.concatenate([sums, sums], 0).T

    pending[...] = jnp.zeros_like(pending)
    entries[...] = jnp.zeros_like(entries)

    def block_sums(step):
        scatter(jnp.maximum(step - 2, 0))
        turn()
        plane = step // (half // group)
        base = step % (half // group) * group
        parts, hots = [], []
        for g in range(group):
            zz = base + g
            rows = pl.ds(pl.multiple_of((plane * half + zz) * 8, 8), 8)
            resp = [ref[rows, :] for ref in (zero_ref, one_ref, two_ref)]
            square = [r * r for r in resp]
            cube = [s * r for s, r in zip(square, resp)]
            fourth = [s * s for s in square]
            pairs = [resp[a] * resp[b] for a, b in ((0, 1), (0, 2), (1, 2))]
            high, low = halves(jnp.concatenate([*resp, *square, *cube, *fourth, *pairs, raw_ref[rows, :]], 0))
            parts.append(jnp.concatenate([high, low], 1))
            hots.append((slots_ref[plane, pl.ds(zz, 1), :] == sub).astype(jnp.float32))
            hots.append((slots_ref[plane, pl.ds(zz + half, 1), :] == sub).astype(jnp.float32))
        hot = jnp.concatenate(hots, 0).astype(jnp.bfloat16)
        dims = (((1,), (1,)), ((), ()))
        products = lax.dot_general(
            jnp.concatenate(parts, 0), jnp.concatenate([hot, hot], 1), dims, preferred_element_type=jnp.float32
        )
        sums = jnp.zeros((2 * FEAT, LANES), jnp.float32)
        for g in range(group):
            sums = jnp.where(owner == 2 * g, products[2 * g * FEAT : (2 * g + 2) * FEAT], sums)
        folded = []
        for number in range(2 * FEAT // 8):
            piece = sums[8 * number : 8 * number + 8]
            folded.append(piece + pltpu.roll(piece, 4, 0))
        pending[...] = jnp.concatenate(
            [jnp.where(sub < 4, folded[k], folded[k + 1]) for k in range(0, len(folded), 2)], 0
        )

    unroll = 8 if steps % 8 == 0 else 1

    def several(step, carry):
        for number in range(unroll):
            block_sums(step * unroll + number)
        return carry

    lax.fori_loop(0, steps // unroll, several, 0)
    scatter(steps - 2)
    turn()
    scatter(steps - 1)

    kept = keep_ref.shape[0]
    places = kept // (2 * quarter)
    left = lax.broadcasted_iota(jnp.int32, (quarter, LANES), 1) < FEAT

    def combine(step, carry):
        for part in range(2):
            for out, first in ((keep_ref, 0), (send_ref, places)):
                row = pl.multiple_of((part * 2 * places + first + step) * 2 * quarter, 2 * quarter)
                total = tables[0][pl.ds(row, 2 * quarter), :]
                for table in tables[1:]:
                    total = total + table[pl.ds(row, 2 * quarter), :]
                place = pl.multiple_of((part * places + step) * quarter, quarter)
                out[pl.ds(place, quarter), :] = jnp.where(left, total[:quarter], total[quarter:])
        return carry

    lax.fori_loop(0, places, combine, 0)


def add_kernel(layers, *refs):
    ins, outs = refs[:-2], refs[-2:]
    count = len(ins) // 2
    for number, out in enumerate(outs):
        total = None
        for ref, start in zip(ins[number * count : (number + 1) * count], layers[number]):
            piece = ref[start : start + out.shape[0], :]
            total = piece if total is None else total + piece
        out[...] = total


def final_kernel(layers, *refs):
    ins, out_ref, ordered = refs[:-2], refs[-2], refs[-1]
    count = len(ins) // 2
    quarter = ins[count - 1].shape[0]
    for number in range(2):
        table = None
        for ref, start in zip(ins[number * count : (number + 1) * count], layers[number]):
            piece = ref[start : start + quarter, :]
            table = piece if table is None else table + piece
        table = table.T
        for side in range(2):
            rows = table[side * FEAT : (side + 1) * FEAT]
            count_row = rows[FEAT - 1 :]
            lane = lax.broadcasted_iota(jnp.int32, rows.shape, 0)
            result = jnp.where(lane == FEAT - 1, jnp.log(1.0 + rows), rows / jnp.maximum(count_row, 1.0))
            columns = pl.ds((2 * number + side) * quarter, quarter)
            first_row = (2 * number + side) * FEAT
            for kind in range(15):
                ordered[pl.ds(first_row + kind // 3 * RESP + kind % 3, SCALES, stride=3), :] = result[4 * kind : 4 * kind + 4]
            ordered[first_row + FEAT - 4 : first_row + FEAT, :] = result[FEAT - 4 :]
            out_ref[:, columns] = ordered[first_row : first_row + FEAT, :]


def on_chip(value):
    return pltpu.with_memory_space_constraint(value, pltpu.VMEM)


def shards(affinity, block_scale, slot_map, edge_list, valid_count, edge_home):
    planes, height, depth = affinity.shape[1:]
    owners = lax.axis_size("xy")
    rows_owned = edge_home.shape[0] // owners
    quarter = rows_owned // 4
    vmem = pl.BlockSpec(memory_space=pltpu.VMEM)
    smem = pl.BlockSpec(memory_space=pltpu.SMEM)

    small = owners * rows_owned <= 8192

    near = on_chip if small else lambda value: value

    def room(mib):
        return pltpu.CompilerParams(vmem_limit_bytes=mib << 20) if small else None

    up = [(i, i + 1) for i in range(owners - 1)]
    down = [(j, i) for i, j in up]
    scaled, before, after = [], [], []
    dequant = affinity.astype(jnp.float32) * block_scale[..., None]

    def send_halo(value):
        scaled.append(on_chip(value))
        before.append(on_chip(lax.ppermute(value[:, planes - HALO :], "xy", up)))
        after.append(on_chip(lax.ppermute(value[:, :HALO], "xy", down)))

    send_halo(dequant[:2])
    send_halo(dequant[2:])

    me = lax.axis_index("xy").astype(jnp.int32).reshape(1)
    lists = edge_list.transpose(0, 2, 1).reshape(planes * SLOTS, height)
    counts = jnp.broadcast_to(valid_count[:, None, :], (planes, SLOTS, height)).reshape(planes * SLOTS, height)
    index_shape = jax.ShapeDtypeStruct((planes * SLOTS, height), jnp.int32)
    field_shape = jax.ShapeDtypeStruct((planes * height * 4, LANES), jnp.float32)
    table_rows = owners * rows_owned
    given = 4 if small else 0
    padded = jax.ShapeDtypeStruct((-(-(table_rows + 8) // 256) * 256, LANES), jnp.float32)
    target, raw, *tables = pl.pallas_call(
        functools.partial(prepare_kernel, owners, rows_owned, height),
        out_shape=(jax.ShapeDtypeStruct((planes * SLOTS, LANES), jnp.int32), field_shape) + (padded,) * given,
        in_specs=[smem] + [vmem] * 5,
        out_specs=(vmem, vmem) + (vmem,) * given,
        compiler_params=room(6),
        name="prepare",
    )(me, lists, counts, edge_home.reshape(-1, LANES), dequant[:2], dequant[2:])

    along_y, along_z = filter_constants(height, depth)
    blurred = pltpu.VMEM((SCALES, planes, height, depth), jnp.float32)
    filters = (on_chip(jnp.asarray(along_y)), on_chip(jnp.asarray(along_z)))
    fields = pl.pallas_call(
        blur_kernel,
        out_shape=(field_shape, field_shape),
        in_specs=[vmem] * 5,
        out_specs=(vmem, vmem),
        scratch_shapes=[blurred],
        compiler_params=room(12),
        name="blur",
    )(before[0], scaled[0], after[0], *filters)
    table_shape = jax.ShapeDtypeStruct((owners * quarter, LANES), jnp.float32)
    keep, send, *_ = pl.pallas_call(
        functools.partial(main_kernel, given, quarter),
        out_shape=(table_shape, table_shape) + (padded,) * given,
        in_specs=[vmem] * 9 + [smem] + [vmem] * given,
        out_specs=(vmem, vmem) + (vmem,) * given,
        input_output_aliases={10 + number: 2 + number for number in range(given)},
        scratch_shapes=[
            blurred,
            pltpu.VMEM(field_shape.shape, jnp.float32),
            pltpu.VMEM((FEAT, LANES), jnp.float32),
            pltpu.VMEM((LANES, LANES), jnp.float32),
        ]
        + [pltpu.VMEM(padded.shape, jnp.float32)] * (0 if small else 1),
        compiler_params=pltpu.CompilerParams(vmem_limit_bytes=(24 if small else 44) << 20),
        name="features",
    )(before[1], scaled[1], after[1], *filters, *map(on_chip, fields), on_chip(raw), on_chip(slot_map), target.reshape(-1), *map(on_chip, tables))

    def swap(value, bit):
        return near(lax.ppermute(value, "xy", [(i, i ^ (1 << bit)) for i in range(owners)]))

    order_first, order_second = order_bits(owners)
    whole = owners // 2 * quarter
    got = swap(send, 0)
    keep = near(keep)
    first, second = [keep, got], [keep, got]
    starts = ([0, 0], [whole, whole])
    middle = whole
    for bit_first, bit_second in zip(order_first[1:], order_second[1:]):
        middle //= 2
        layers = tuple(tuple(start + middle for start in part) for part in starts)
        shape = jax.ShapeDtypeStruct((middle, LANES), jnp.float32)
        send_first, send_second = pl.pallas_call(
            functools.partial(add_kernel, layers),
            out_shape=(shape, shape),
            in_specs=[vmem] * (2 * len(first)),
            out_specs=(vmem, vmem),
            compiler_params=room(10),
            name="add",
        )(*first, *second)
        first, second = first + [swap(send_first, bit_first)], second + [swap(send_second, bit_second)]
        starts = (starts[0] + [0], starts[1] + [0])
    out = pl.pallas_call(
        functools.partial(final_kernel, starts),
        out_shape=jax.ShapeDtypeStruct((FEAT, rows_owned), jnp.float32),
        in_specs=[vmem] * (2 * len(first)),
        out_specs=vmem,
        scratch_shapes=[pltpu.VMEM((4 * FEAT, LANES), jnp.float32)],
        compiler_params=room(10),
        name="final",
    )(*first, *second)
    return out.T


def solution(mesh):
    in_specs = (
        P(None, ("parts", "xy"), None, None),
        P(None, ("parts", "xy"), None),
        P(("parts", "xy"), None, None),
        P(("parts", "xy"), None, None),
        P(("parts", "xy"), None),
        P("parts"),
    )
    out_specs = P(("parts", "xy"), None)
    return jax.shard_map(shards, mesh=mesh, in_specs=in_specs, out_specs=out_specs, check_vma=False)
```

```python
import functools

import jax
import jax.numpy as jnp
import numpy as np
from jax import lax
from jax.experimental import pallas as pl
from jax.experimental.pallas import tpu as pltpu
from jax.sharding import PartitionSpec as P


SLOTS = 8
HALO = 8
FEAT = 64
LANES = 128

sigma_list = (0.8, 1.3, 2.0, 3.0)
SCALES = len(sigma_list)
RESP = 3 * SCALES


def taps(sigma):
    offsets = np.arange(-HALO, HALO + 1).astype(np.float32)
    weights = np.exp(-offsets * offsets / np.float32(2.0 * sigma * sigma)).astype(np.float32)
    return (weights / weights.sum(dtype=np.float32)).astype(np.float32)


def band(weights, length):
    rows = np.arange(length)[:, None]
    cols = np.arange(length)[None, :]
    offset = cols - rows + HALO
    inside = (offset >= 0) & (offset <= 2 * HALO)
    return np.where(inside, weights[np.clip(offset, 0, 2 * HALO)], 0.0).astype(np.float32)


def halves(value):
    high = value.astype(jnp.bfloat16)
    low = (value - high.astype(jnp.float32)).astype(jnp.bfloat16)
    return high, low


def constant_halves(value):
    high = value.astype(jnp.bfloat16)
    low = (value - high.astype(np.float32)).astype(jnp.bfloat16)
    return high, low


def filter_constants(height, depth):
    along_y, along_z = [], []
    for sigma in sigma_list:
        high, low = constant_halves(band(taps(sigma), depth).T)
        along_y.append(np.concatenate([np.concatenate([high, low], 1), np.concatenate([high, np.zeros_like(low)], 1)], 0))
        high, low = constant_halves(band(taps(sigma), height))
        along_z.append(np.concatenate([high, high, low], 1))
    return np.stack(along_y), np.stack(along_z)


def order_bits(owners):
    bits = owners.bit_length() - 1
    first = list(range(bits))
    return first, [0] + first[2:] + first[1:2]


def put(fields, row, value, planes, half):
    for q in range(planes):
        for b in range(2):
            fields[pl.ds(q * half * 8 + b * 4 + row, half, stride=8), :] = value(q)[b * half : (b + 1) * half]


def clear(tables):
    for table in tables:

        def some(step, carry, table=table):
            table[pl.ds(pl.multiple_of(step * 256, 256), 256), :] = jnp.zeros((256, LANES), jnp.float32)
            return carry

        lax.fori_loop(0, table.shape[0] // 256, some, 0)


def prepare_kernel(
    owners, rows_owned, height, me_ref, edge_ref, count_ref, home_ref, pair_ref, last_ref,
    y_ref, z_ref, target_ref, raw_ref, y_out, z_out, *tables,
):
    y_out[...] = y_ref[...]
    z_out[...] = z_ref[...]
    planes = last_ref.shape[1]
    clear(tables)
    for channel in range(3):
        own_ref = pair_ref.at[channel] if channel < 2 else last_ref.at[0]
        put(raw_ref, channel, lambda q: own_ref[q], planes, height // 2)
    put(raw_ref, 3, lambda q: jnp.ones((height, LANES), jnp.float32), planes, height // 2)
    entry_rows = edge_ref.shape[0] // 2
    both = jnp.concatenate([edge_ref[:entry_rows, :], edge_ref[entry_rows:, :]], 1)
    high = both // LANES
    low = both % LANES

    def pick(step, found):
        start = pl.multiple_of(step * 8, 8)
        lines = home_ref[pl.ds(start, 8), :]
        for number in range(8):
            line = jnp.broadcast_to(lines[number : number + 1], both.shape)
            found = jnp.where(high == start + number, jnp.take_along_axis(line, low, axis=1), found)
        return found

    found = lax.fori_loop(0, home_ref.shape[0] // 8, pick, jnp.zeros(both.shape, jnp.int32))
    home = jnp.concatenate([found[:, :height], found[:, height:]], 0)
    entry = lax.broadcasted_iota(jnp.int32, home.shape, 0)
    slot = entry % SLOTS
    owner = (home // rows_owned) ^ me_ref[0]
    within = home % rows_owned
    quarter = rows_owned // 4
    part = within // (2 * quarter)
    first, second = order_bits(owners)
    bits = len(first)
    place_first = jnp.zeros_like(owner)
    place_second = jnp.zeros_like(owner)
    for position in range(bits):
        place_first += ((owner >> first[position]) & 1) << (bits - 1 - position)
        place_second += ((owner >> second[position]) & 1) << (bits - 1 - position)
    place = jnp.where(part == 0, place_first, owners + place_second)
    row = place * (2 * quarter) + within % (2 * quarter)
    valid = slot < count_ref[...]
    target_ref[:, :height] = jnp.where(valid, row, owners * rows_owned)


def blur(before_ref, own_ref, after_ref, y_ref, z_ref, fields, blurred):
    planes, height, depth = own_ref.shape
    weights = [[float(w) for w in taps(sigma)] for sigma in sigma_list]
    tiles = height // 8

    def across(step, carry):
        rows = pl.ds(pl.multiple_of(step * 8, 8), 8)
        values = [before_ref[planes - HALO + p, rows, :] for p in range(HALO)]
        values += [own_ref[p, rows, :] for p in range(planes)]
        values += [after_ref[p, rows, :] for p in range(HALO)]
        for q in range(planes):
            center = q + HALO
            sums = [values[center]] + [values[center - t] + values[center + t] for t in range(1, HALO + 1)]
            for scale in range(SCALES):
                total = sums[0] * weights[scale][HALO]
                for t in range(1, HALO + 1):
                    total = total + sums[t] * weights[scale][HALO + t]
                blurred[scale, q, rows, :] = total
        return carry

    lax.fori_loop(0, tiles, across, 0)
    lines = []
    for scale in range(SCALES):
        high, low = halves(blurred[scale].reshape(planes * height, depth))
        line = jnp.dot(jnp.concatenate([high, low], 1), y_ref[scale], preferred_element_type=jnp.float32)
        lines.append(line[:, :depth] + line[:, depth:])
    for scale in range(SCALES):
        high, low = halves(lines[scale])
        high, low = high.reshape(planes, height, depth), low.reshape(planes, height, depth)
        stacked = jnp.concatenate([high, low, high], 1)
        side_by_side = jnp.concatenate([stacked[q] for q in range(planes)], 1)
        result = jnp.dot(z_ref[scale], side_by_side, preferred_element_type=jnp.float32)
        put(fields, scale, lambda q: result[:, q * depth : (q + 1) * depth], planes, height // 2)


def blur_kernel(before_ref, own_ref, after_ref, y_ref, z_ref, zero_ref, one_ref, blurred):
    for channel, fields in enumerate((zero_ref, one_ref)):
        refs = [ref.at[channel] for ref in (before_ref, own_ref, after_ref)]
        blur(*refs, y_ref, z_ref, fields, blurred)


def main_kernel(
    given, quarter, before_ref, own_ref, after_ref, y_ref, z_ref, zero_ref, one_ref, raw_ref, slots_ref, target_ref, *refs
):
    keep_ref, send_ref, *tables = refs[given : 2 * given + 2]
    blurred, two_ref, pending, entries, *own_tables = refs[2 * given + 2 :]
    clear(own_tables)
    tables += own_tables
    copies = len(tables)
    planes, height, depth = own_ref.shape[1:]
    half = height // 2
    blur(before_ref.at[0], own_ref.at[0], after_ref.at[0], y_ref, z_ref, two_ref, blurred)

    sub = lax.broadcasted_iota(jnp.int32, (SLOTS, LANES), 0)
    group = LANES // (2 * SLOTS)
    owner_row = lax.broadcasted_iota(jnp.int32, (2 * FEAT, LANES), 0) % 8 // 4
    owner_lane = lax.broadcasted_iota(jnp.int32, (2 * FEAT, LANES), 1) // SLOTS
    owner = owner_lane - owner_row
    steps = planes * half // group

    def scatter(step):
        plane = step // (half // group)
        base = plane * (SLOTS * LANES) + step % (half // group) * group
        for number in range(LANES):
            pair, block, slot = number // (2 * SLOTS), number // SLOTS % 2, number % SLOTS
            table = tables[number % copies]
            target = pl.ds(target_ref[base + (slot * LANES + block * half + pair)], 1)
            table[target, :] = table[target, :] + entries[number : number + 1, :]

    def turn():
        sums = pending[...]
        entries[...] = jnp.concatenate([sums, sums], 0).T

    pending[...] = jnp.zeros_like(pending)
    entries[...] = jnp.zeros_like(entries)

    def block_sums(step):
        scatter(jnp.maximum(step - 2, 0))
        turn()
        plane = step // (half // group)
        base = step % (half // group) * group
        parts, hots = [], []
        for g in range(group):
            zz = base + g
            rows = pl.ds(pl.multiple_of((plane * half + zz) * 8, 8), 8)
            resp = [ref[rows, :] for ref in (zero_ref, one_ref, two_ref)]
            square = [r * r for r in resp]
            cube = [s * r for s, r in zip(square, resp)]
            fourth = [s * s for s in square]
            pairs = [resp[a] * resp[b] for a, b in ((0, 1), (0, 2), (1, 2))]
            high, low = halves(jnp.concatenate([*resp, *square, *cube, *fourth, *pairs, raw_ref[rows, :]], 0))
            parts.append(jnp.concatenate([high, low], 1))
            hots.append((slots_ref[plane, pl.ds(zz, 1), :] == sub).astype(jnp.float32))
            hots.append((slots_ref[plane, pl.ds(zz + half, 1), :] == sub).astype(jnp.float32))
        hot = jnp.concatenate(hots, 0).astype(jnp.bfloat16)
        dims = (((1,), (1,)), ((), ()))
        products = lax.dot_general(
            jnp.concatenate(parts, 0), jnp.concatenate([hot, hot], 1), dims, preferred_element_type=jnp.float32
        )
        sums = jnp.zeros((2 * FEAT, LANES), jnp.float32)
        for g in range(group):
            sums = jnp.where(owner == 2 * g, products[2 * g * FEAT : (2 * g + 2) * FEAT], sums)
        folded = []
        for number in range(2 * FEAT // 8):
            piece = sums[8 * number : 8 * number + 8]
            folded.append(piece + pltpu.roll(piece, 4, 0))
        pending[...] = jnp.concatenate(
            [jnp.where(sub < 4, folded[k], folded[k + 1]) for k in range(0, len(folded), 2)], 0
        )

    unroll = 8 if steps % 8 == 0 else 1

    def several(step, carry):
        for number in range(unroll):
            block_sums(step * unroll + number)
        return carry

    lax.fori_loop(0, steps // unroll, several, 0)
    scatter(steps - 2)
    turn()
    scatter(steps - 1)

    kept = keep_ref.shape[0]
    places = kept // (2 * quarter)
    left = lax.broadcasted_iota(jnp.int32, (quarter, LANES), 1) < FEAT

    def combine(step, carry):
        for part in range(2):
            for out, first in ((keep_ref, 0), (send_ref, places)):
                row = pl.multiple_of((part * 2 * places + first + step) * 2 * quarter, 2 * quarter)
                total = tables[0][pl.ds(row, 2 * quarter), :]
                for table in tables[1:]:
                    total = total + table[pl.ds(row, 2 * quarter), :]
                place = pl.multiple_of((part * places + step) * quarter, quarter)
                out[pl.ds(place, quarter), :] = jnp.where(left, total[:quarter], total[quarter:])
        return carry

    lax.fori_loop(0, places, combine, 0)


def add_kernel(layers, *refs):
    ins, outs = refs[:-2], refs[-2:]
    count = len(ins) // 2
    for number, out in enumerate(outs):
        total = None
        for ref, start in zip(ins[number * count : (number + 1) * count], layers[number]):
            piece = ref[start : start + out.shape[0], :]
            total = piece if total is None else total + piece
        out[...] = total


def final_kernel(layers, *refs):
    ins, out_ref, ordered = refs[:-2], refs[-2], refs[-1]
    count = len(ins) // 2
    quarter = ins[count - 1].shape[0]
    for number in range(2):
        table = None
        for ref, start in zip(ins[number * count : (number + 1) * count], layers[number]):
            piece = ref[start : start + quarter, :]
            table = piece if table is None else table + piece
        table = table.T
        for side in range(2):
            rows = table[side * FEAT : (side + 1) * FEAT]
            count_row = rows[FEAT - 1 :]
            lane = lax.broadcasted_iota(jnp.int32, rows.shape, 0)
            result = jnp.where(lane == FEAT - 1, jnp.log(1.0 + rows), rows / jnp.maximum(count_row, 1.0))
            columns = pl.ds((2 * number + side) * quarter, quarter)
            first_row = (2 * number + side) * FEAT
            for kind in range(15):
                ordered[pl.ds(first_row + kind // 3 * RESP + kind % 3, SCALES, stride=3), :] = result[4 * kind : 4 * kind + 4]
            ordered[first_row + FEAT - 4 : first_row + FEAT, :] = result[FEAT - 4 :]
            out_ref[:, columns] = ordered[first_row : first_row + FEAT, :]


def on_chip(value):
    return pltpu.with_memory_space_constraint(value, pltpu.VMEM)


def shards(affinity, block_scale, slot_map, edge_list, valid_count, edge_home):
    planes, height, depth = affinity.shape[1:]
    owners = lax.axis_size("xy")
    rows_owned = edge_home.shape[0] // owners
    quarter = rows_owned // 4
    vmem = pl.BlockSpec(memory_space=pltpu.VMEM)
    smem = pl.BlockSpec(memory_space=pltpu.SMEM)

    small = owners * rows_owned <= 8192

    near = on_chip if small else lambda value: value

    def room(mib):
        return pltpu.CompilerParams(vmem_limit_bytes=mib << 20) if small else None

    up = [(i, i + 1) for i in range(owners - 1)]
    down = [(j, i) for i, j in up]
    scaled, before, after = [], [], []
    dequant = affinity.astype(jnp.float32) * block_scale[..., None]

    def send_halo(value):
        scaled.append(on_chip(value))
        before.append(on_chip(lax.ppermute(value[:, planes - HALO :], "xy", up)))
        after.append(on_chip(lax.ppermute(value[:, :HALO], "xy", down)))

    send_halo(dequant[:2])
    send_halo(dequant[2:])

    me = lax.axis_index("xy").astype(jnp.int32).reshape(1)
    lists = edge_list.transpose(0, 2, 1).reshape(planes * SLOTS, height)
    counts = jnp.broadcast_to(valid_count[:, None, :], (planes, SLOTS, height)).reshape(planes * SLOTS, height)
    index_shape = jax.ShapeDtypeStruct((planes * SLOTS, height), jnp.int32)
    field_shape = jax.ShapeDtypeStruct((planes * height * 4, LANES), jnp.float32)
    table_rows = owners * rows_owned
    given = 4 if small else 0
    padded = jax.ShapeDtypeStruct((-(-(table_rows + 8) // 256) * 256, LANES), jnp.float32)
    constants = [jnp.asarray(value) for value in filter_constants(height, depth)]
    target, raw, filter_y, filter_z, *tables = pl.pallas_call(
        functools.partial(prepare_kernel, owners, rows_owned, height),
        out_shape=(jax.ShapeDtypeStruct((planes * SLOTS, LANES), jnp.int32), field_shape)
        + tuple(jax.ShapeDtypeStruct(value.shape, value.dtype) for value in constants)
        + (padded,) * given,
        in_specs=[smem] + [vmem] * 7,
        out_specs=(vmem,) * (4 + given),
        compiler_params=room(6),
        name="prepare",
    )(me, lists, counts, edge_home.reshape(-1, LANES), dequant[:2], dequant[2:], *constants)

    blurred = pltpu.VMEM((SCALES, planes, height, depth), jnp.float32)
    filters = (on_chip(filter_y), on_chip(filter_z))
    fields = pl.pallas_call(
        blur_kernel,
        out_shape=(field_shape, field_shape),
        in_specs=[vmem] * 5,
        out_specs=(vmem, vmem),
        scratch_shapes=[blurred],
        compiler_params=room(12),
        name="blur",
    )(before[0], scaled[0], after[0], *filters)
    table_shape = jax.ShapeDtypeStruct((owners * quarter, LANES), jnp.float32)
    keep, send, *_ = pl.pallas_call(
        functools.partial(main_kernel, given, quarter),
        out_shape=(table_shape, table_shape) + (padded,) * given,
        in_specs=[vmem] * 9 + [smem] + [vmem] * given,
        out_specs=(vmem, vmem) + (vmem,) * given,
        input_output_aliases={10 + number: 2 + number for number in range(given)},
        scratch_shapes=[
            blurred,
            pltpu.VMEM(field_shape.shape, jnp.float32),
            pltpu.VMEM((FEAT, LANES), jnp.float32),
            pltpu.VMEM((LANES, LANES), jnp.float32),
        ]
        + [pltpu.VMEM(padded.shape, jnp.float32)] * (0 if small else 1),
        compiler_params=pltpu.CompilerParams(vmem_limit_bytes=(24 if small else 44) << 20),
        name="features",
    )(before[1], scaled[1], after[1], *filters, *map(on_chip, fields), on_chip(raw), on_chip(slot_map), target.reshape(-1), *map(on_chip, tables))

    def swap(value, bit):
        return near(lax.ppermute(value, "xy", [(i, i ^ (1 << bit)) for i in range(owners)]))

    order_first, order_second = order_bits(owners)
    whole = owners // 2 * quarter
    got = swap(send, 0)
    keep = near(keep)
    first, second = [keep, got], [keep, got]
    starts = ([0, 0], [whole, whole])
    middle = whole
    for bit_first, bit_second in zip(order_first[1:], order_second[1:]):
        middle //= 2
        layers = tuple(tuple(start + middle for start in part) for part in starts)
        shape = jax.ShapeDtypeStruct((middle, LANES), jnp.float32)
        send_first, send_second = pl.pallas_call(
            functools.partial(add_kernel, layers),
            out_shape=(shape, shape),
            in_specs=[vmem] * (2 * len(first)),
            out_specs=(vmem, vmem),
            compiler_params=room(10),
            name="add",
        )(*first, *second)
        first, second = first + [swap(send_first, bit_first)], second + [swap(send_second, bit_second)]
        starts = (starts[0] + [0], starts[1] + [0])
    out = pl.pallas_call(
        functools.partial(final_kernel, starts),
        out_shape=jax.ShapeDtypeStruct((FEAT, rows_owned), jnp.float32),
        in_specs=[vmem] * (2 * len(first)),
        out_specs=vmem,
        scratch_shapes=[pltpu.VMEM((4 * FEAT, LANES), jnp.float32)],
        compiler_params=room(10),
        name="final",
    )(*first, *second)
    return out.T


def solution(mesh):
    in_specs = (
        P(None, ("parts", "xy"), None, None),
        P(None, ("parts", "xy"), None),
        P(("parts", "xy"), None, None),
        P(("parts", "xy"), None, None),
        P(("parts", "xy"), None),
        P("parts"),
    )
    out_specs = P(("parts", "xy"), None)
    return jax.shard_map(shards, mesh=mesh, in_specs=in_specs, out_specs=out_specs, check_vma=False)
```

```python
import functools

import jax
import jax.numpy as jnp
import numpy as np
from jax import lax
from jax.experimental import pallas as pl
from jax.experimental.pallas import tpu as pltpu
from jax.sharding import PartitionSpec as P


SLOTS = 8
HALO = 8
FEAT = 64
LANES = 128

sigma_list = (0.8, 1.3, 2.0, 3.0)
SCALES = len(sigma_list)
RESP = 3 * SCALES


def taps(sigma):
    offsets = np.arange(-HALO, HALO + 1).astype(np.float32)
    weights = np.exp(-offsets * offsets / np.float32(2.0 * sigma * sigma)).astype(np.float32)
    return (weights / weights.sum(dtype=np.float32)).astype(np.float32)


def band(weights, length):
    rows = np.arange(length)[:, None]
    cols = np.arange(length)[None, :]
    offset = cols - rows + HALO
    inside = (offset >= 0) & (offset <= 2 * HALO)
    return np.where(inside, weights[np.clip(offset, 0, 2 * HALO)], 0.0).astype(np.float32)


def halves(value):
    high = value.astype(jnp.bfloat16)
    low = (value - high.astype(jnp.float32)).astype(jnp.bfloat16)
    return high, low


def constant_halves(value):
    high = value.astype(jnp.bfloat16)
    low = (value - high.astype(np.float32)).astype(jnp.bfloat16)
    return high, low


def filter_constants(height, depth):
    along_y, along_z = [], []
    for sigma in sigma_list:
        high, low = constant_halves(band(taps(sigma), depth).T)
        along_y.append(np.concatenate([np.concatenate([high, low], 1), np.concatenate([high, np.zeros_like(low)], 1)], 0))
        high, low = constant_halves(band(taps(sigma), height))
        along_z.append(np.concatenate([high, high, low], 1))
    return np.stack(along_y), np.stack(along_z)


def order_bits(owners):
    bits = owners.bit_length() - 1
    first = list(range(bits))
    return first, [0] + first[2:3] + first[1:2] + first[3:]


def put(fields, row, value, planes, half):
    for q in range(planes):
        for b in range(2):
            fields[pl.ds(q * half * 8 + b * 4 + row, half, stride=8), :] = value(q)[b * half : (b + 1) * half]


def clear(tables):
    for table in tables:

        def some(step, carry, table=table):
            table[pl.ds(pl.multiple_of(step * 256, 256), 256), :] = jnp.zeros((256, LANES), jnp.float32)
            return carry

        lax.fori_loop(0, table.shape[0] // 256, some, 0)


def prepare_kernel(
    owners, rows_owned, height, me_ref, edge_ref, count_ref, home_ref, pair_ref, last_ref,
    y_ref, z_ref, target_ref, raw_ref, y_out, z_out, *tables,
):
    y_out[...] = y_ref[...]
    z_out[...] = z_ref[...]
    planes = last_ref.shape[1]
    clear(tables)
    for channel in range(3):
        own_ref = pair_ref.at[channel] if channel < 2 else last_ref.at[0]
        put(raw_ref, channel, lambda q: own_ref[q], planes, height // 2)
    put(raw_ref, 3, lambda q: jnp.ones((height, LANES), jnp.float32), planes, height // 2)
    entry_rows = edge_ref.shape[0] // 2
    both = jnp.concatenate([edge_ref[:entry_rows, :], edge_ref[entry_rows:, :]], 1)
    high = both // LANES
    low = both % LANES

    def pick(step, found):
        start = pl.multiple_of(step * 8, 8)
        lines = home_ref[pl.ds(start, 8), :]
        for number in range(8):
            line = jnp.broadcast_to(lines[number : number + 1], both.shape)
            found = jnp.where(high == start + number, jnp.take_along_axis(line, low, axis=1), found)
        return found

    found = lax.fori_loop(0, home_ref.shape[0] // 8, pick, jnp.zeros(both.shape, jnp.int32))
    home = jnp.concatenate([found[:, :height], found[:, height:]], 0)
    entry = lax.broadcasted_iota(jnp.int32, home.shape, 0)
    slot = entry % SLOTS
    owner = (home // rows_owned) ^ me_ref[0]
    within = home % rows_owned
    quarter = rows_owned // 4
    part = within // (2 * quarter)
    first, second = order_bits(owners)
    bits = len(first)
    place_first = jnp.zeros_like(owner)
    place_second = jnp.zeros_like(owner)
    for position in range(bits):
        place_first += ((owner >> first[position]) & 1) << (bits - 1 - position)
        place_second += ((owner >> second[position]) & 1) << (bits - 1 - position)
    place = jnp.where(part == 0, place_first, owners + place_second)
    row = place * (2 * quarter) + within % (2 * quarter)
    valid = slot < count_ref[...]
    target_ref[:, :height] = jnp.where(valid, row, owners * rows_owned)


def blur(before_ref, own_ref, after_ref, y_ref, z_ref, fields, blurred):
    planes, height, depth = own_ref.shape
    weights = [[float(w) for w in taps(sigma)] for sigma in sigma_list]
    tiles = height // 8

    def across(step, carry):
        rows = pl.ds(pl.multiple_of(step * 8, 8), 8)
        values = [before_ref[planes - HALO + p, rows, :] for p in range(HALO)]
        values += [own_ref[p, rows, :] for p in range(planes)]
        values += [after_ref[p, rows, :] for p in range(HALO)]
        for q in range(planes):
            center = q + HALO
            sums = [values[center]] + [values[center - t] + values[center + t] for t in range(1, HALO + 1)]
            for scale in range(SCALES):
                total = sums[0] * weights[scale][HALO]
                for t in range(1, HALO + 1):
                    total = total + sums[t] * weights[scale][HALO + t]
                blurred[scale, q, rows, :] = total
        return carry

    lax.fori_loop(0, tiles, across, 0)
    lines = []
    for scale in range(SCALES):
        high, low = halves(blurred[scale].reshape(planes * height, depth))
        line = jnp.dot(jnp.concatenate([high, low], 1), y_ref[scale], preferred_element_type=jnp.float32)
        lines.append(line[:, :depth] + line[:, depth:])
    for scale in range(SCALES):
        high, low = halves(lines[scale])
        high, low = high.reshape(planes, height, depth), low.reshape(planes, height, depth)
        stacked = jnp.concatenate([high, low, high], 1)
        side_by_side = jnp.concatenate([stacked[q] for q in range(planes)], 1)
        result = jnp.dot(z_ref[scale], side_by_side, preferred_element_type=jnp.float32)
        put(fields, scale, lambda q: result[:, q * depth : (q + 1) * depth], planes, height // 2)


def blur_kernel(before_ref, own_ref, after_ref, y_ref, z_ref, zero_ref, one_ref, blurred):
    for channel, fields in enumerate((zero_ref, one_ref)):
        refs = [ref.at[channel] for ref in (before_ref, own_ref, after_ref)]
        blur(*refs, y_ref, z_ref, fields, blurred)


def main_kernel(
    given, quarter, before_ref, own_ref, after_ref, y_ref, z_ref, zero_ref, one_ref, raw_ref, slots_ref, target_ref, *refs
):
    keep_ref, send_ref, *tables = refs[given : 2 * given + 2]
    blurred, two_ref, pending, entries, *own_tables = refs[2 * given + 2 :]
    clear(own_tables)
    tables += own_tables
    copies = len(tables)
    planes, height, depth = own_ref.shape[1:]
    half = height // 2
    blur(before_ref.at[0], own_ref.at[0], after_ref.at[0], y_ref, z_ref, two_ref, blurred)

    sub = lax.broadcasted_iota(jnp.int32, (SLOTS, LANES), 0)
    group = LANES // (2 * SLOTS)
    owner_row = lax.broadcasted_iota(jnp.int32, (2 * FEAT, LANES), 0) % 8 // 4
    owner_lane = lax.broadcasted_iota(jnp.int32, (2 * FEAT, LANES), 1) // SLOTS
    owner = owner_lane - owner_row
    steps = planes * half // group

    def scatter(step):
        plane = step // (half // group)
        base = plane * (SLOTS * LANES) + step % (half // group) * group
        for number in range(LANES):
            pair, block, slot = number // (2 * SLOTS), number // SLOTS % 2, number % SLOTS
            table = tables[number % copies]
            target = pl.ds(target_ref[base + (slot * LANES + block * half + pair)], 1)
            table[target, :] = table[target, :] + entries[number : number + 1, :]

    def turn():
        sums = pending[...]
        entries[...] = jnp.concatenate([sums, sums], 0).T

    pending[...] = jnp.zeros_like(pending)
    entries[...] = jnp.zeros_like(entries)

    def block_sums(step):
        scatter(jnp.maximum(step - 2, 0))
        turn()
        plane = step // (half // group)
        base = step % (half // group) * group
        parts, hots = [], []
        for g in range(group):
            zz = base + g
            rows = pl.ds(pl.multiple_of((plane * half + zz) * 8, 8), 8)
            resp = [ref[rows, :] for ref in (zero_ref, one_ref, two_ref)]
            square = [r * r for r in resp]
            cube = [s * r for s, r in zip(square, resp)]
            fourth = [s * s for s in square]
            pairs = [resp[a] * resp[b] for a, b in ((0, 1), (0, 2), (1, 2))]
            high, low = halves(jnp.concatenate([*resp, *square, *cube, *fourth, *pairs, raw_ref[rows, :]], 0))
            parts.append(jnp.concatenate([high, low], 1))
            hots.append((slots_ref[plane, pl.ds(zz, 1), :] == sub).astype(jnp.float32))
            hots.append((slots_ref[plane, pl.ds(zz + half, 1), :] == sub).astype(jnp.float32))
        hot = jnp.concatenate(hots, 0).astype(jnp.bfloat16)
        dims = (((1,), (1,)), ((), ()))
        products = lax.dot_general(
            jnp.concatenate(parts, 0), jnp.concatenate([hot, hot], 1), dims, preferred_element_type=jnp.float32
        )
        sums = jnp.zeros((2 * FEAT, LANES), jnp.float32)
        for g in range(group):
            sums = jnp.where(owner == 2 * g, products[2 * g * FEAT : (2 * g + 2) * FEAT], sums)
        folded = []
        for number in range(2 * FEAT // 8):
            piece = sums[8 * number : 8 * number + 8]
            folded.append(piece + pltpu.roll(piece, 4, 0))
        pending[...] = jnp.concatenate(
            [jnp.where(sub < 4, folded[k], folded[k + 1]) for k in range(0, len(folded), 2)], 0
        )

    unroll = 8 if steps % 8 == 0 else 1

    def several(step, carry):
        for number in range(unroll):
            block_sums(step * unroll + number)
        return carry

    lax.fori_loop(0, steps // unroll, several, 0)
    scatter(steps - 2)
    turn()
    scatter(steps - 1)

    kept = keep_ref.shape[0]
    places = kept // (2 * quarter)
    left = lax.broadcasted_iota(jnp.int32, (quarter, LANES), 1) < FEAT

    def combine(step, carry):
        for part in range(2):
            for out, first in ((keep_ref, 0), (send_ref, places)):
                row = pl.multiple_of((part * 2 * places + first + step) * 2 * quarter, 2 * quarter)
                total = tables[0][pl.ds(row, 2 * quarter), :]
                for table in tables[1:]:
                    total = total + table[pl.ds(row, 2 * quarter), :]
                place = pl.multiple_of((part * places + step) * quarter, quarter)
                out[pl.ds(place, quarter), :] = jnp.where(left, total[:quarter], total[quarter:])
        return carry

    lax.fori_loop(0, places, combine, 0)


def add_kernel(layers, *refs):
    ins, outs = refs[:-2], refs[-2:]
    count = len(ins) // 2
    for number, out in enumerate(outs):
        total = None
        for ref, start in zip(ins[number * count : (number + 1) * count], layers[number]):
            piece = ref[start : start + out.shape[0], :]
            total = piece if total is None else total + piece
        out[...] = total


def final_kernel(layers, *refs):
    ins, out_ref, ordered = refs[:-2], refs[-2], refs[-1]
    count = len(ins) // 2
    quarter = ins[count - 1].shape[0]
    for number in range(2):
        table = None
        for ref, start in zip(ins[number * count : (number + 1) * count], layers[number]):
            piece = ref[start : start + quarter, :]
            table = piece if table is None else table + piece
        table = table.T
        for side in range(2):
            rows = table[side * FEAT : (side + 1) * FEAT]
            count_row = rows[FEAT - 1 :]
            lane = lax.broadcasted_iota(jnp.int32, rows.shape, 0)
            result = jnp.where(lane == FEAT - 1, jnp.log(1.0 + rows), rows / jnp.maximum(count_row, 1.0))
            columns = pl.ds((2 * number + side) * quarter, quarter)
            first_row = (2 * number + side) * FEAT
            for kind in range(15):
                ordered[pl.ds(first_row + kind // 3 * RESP + kind % 3, SCALES, stride=3), :] = result[4 * kind : 4 * kind + 4]
            ordered[first_row + FEAT - 4 : first_row + FEAT, :] = result[FEAT - 4 :]
            out_ref[:, columns] = ordered[first_row : first_row + FEAT, :]


def on_chip(value):
    return pltpu.with_memory_space_constraint(value, pltpu.VMEM)


def shards(affinity, block_scale, slot_map, edge_list, valid_count, edge_home):
    planes, height, depth = affinity.shape[1:]
    owners = lax.axis_size("xy")
    rows_owned = edge_home.shape[0] // owners
    quarter = rows_owned // 4
    vmem = pl.BlockSpec(memory_space=pltpu.VMEM)
    smem = pl.BlockSpec(memory_space=pltpu.SMEM)

    small = owners * rows_owned <= 8192

    near = on_chip if small else lambda value: value

    def room(mib):
        return pltpu.CompilerParams(vmem_limit_bytes=mib << 20) if small else None

    up = [(i, i + 1) for i in range(owners - 1)]
    down = [(j, i) for i, j in up]
    scaled, before, after = [], [], []
    dequant = affinity.astype(jnp.float32) * block_scale[..., None]

    def send_halo(value):
        scaled.append(on_chip(value))
        before.append(on_chip(lax.ppermute(value[:, planes - HALO :], "xy", up)))
        after.append(on_chip(lax.ppermute(value[:, :HALO], "xy", down)))

    send_halo(dequant[:2])
    send_halo(dequant[2:])

    me = lax.axis_index("xy").astype(jnp.int32).reshape(1)
    lists = edge_list.transpose(0, 2, 1).reshape(planes * SLOTS, height)
    counts = jnp.broadcast_to(valid_count[:, None, :], (planes, SLOTS, height)).reshape(planes * SLOTS, height)
    index_shape = jax.ShapeDtypeStruct((planes * SLOTS, height), jnp.int32)
    field_shape = jax.ShapeDtypeStruct((planes * height * 4, LANES), jnp.float32)
    table_rows = owners * rows_owned
    given = 4 if small else 0
    padded = jax.ShapeDtypeStruct((-(-(table_rows + 8) // 256) * 256, LANES), jnp.float32)
    constants = [jnp.asarray(value) for value in filter_constants(height, depth)]
    target, raw, filter_y, filter_z, *tables = pl.pallas_call(
        functools.partial(prepare_kernel, owners, rows_owned, height),
        out_shape=(jax.ShapeDtypeStruct((planes * SLOTS, LANES), jnp.int32), field_shape)
        + tuple(jax.ShapeDtypeStruct(value.shape, value.dtype) for value in constants)
        + (padded,) * given,
        in_specs=[smem] + [vmem] * 7,
        out_specs=(vmem,) * (4 + given),
        compiler_params=room(6),
        name="prepare",
    )(me, lists, counts, edge_home.reshape(-1, LANES), dequant[:2], dequant[2:], *constants)

    blurred = pltpu.VMEM((SCALES, planes, height, depth), jnp.float32)
    filters = (on_chip(filter_y), on_chip(filter_z))
    fields = pl.pallas_call(
        blur_kernel,
        out_shape=(field_shape, field_shape),
        in_specs=[vmem] * 5,
        out_specs=(vmem, vmem),
        scratch_shapes=[blurred],
        compiler_params=room(12),
        name="blur",
    )(before[0], scaled[0], after[0], *filters)
    table_shape = jax.ShapeDtypeStruct((owners * quarter, LANES), jnp.float32)
    keep, send, *_ = pl.pallas_call(
        functools.partial(main_kernel, given, quarter),
        out_shape=(table_shape, table_shape) + (padded,) * given,
        in_specs=[vmem] * 9 + [smem] + [vmem] * given,
        out_specs=(vmem, vmem) + (vmem,) * given,
        input_output_aliases={10 + number: 2 + number for number in range(given)},
        scratch_shapes=[
            blurred,
            pltpu.VMEM(field_shape.shape, jnp.float32),
            pltpu.VMEM((FEAT, LANES), jnp.float32),
            pltpu.VMEM((LANES, LANES), jnp.float32),
        ]
        + [pltpu.VMEM(padded.shape, jnp.float32)] * (0 if small else 1),
        compiler_params=pltpu.CompilerParams(vmem_limit_bytes=(24 if small else 44) << 20),
        name="features",
    )(before[1], scaled[1], after[1], *filters, *map(on_chip, fields), on_chip(raw), on_chip(slot_map), target.reshape(-1), *map(on_chip, tables))

    def swap(value, bit):
        return near(lax.ppermute(value, "xy", [(i, i ^ (1 << bit)) for i in range(owners)]))

    order_first, order_second = order_bits(owners)
    whole = owners // 2 * quarter
    got = swap(send, 0)
    keep = near(keep)
    first, second = [keep, got], [keep, got]
    starts = ([0, 0], [whole, whole])
    middle = whole
    for bit_first, bit_second in zip(order_first[1:], order_second[1:]):
        middle //= 2
        layers = tuple(tuple(start + middle for start in part) for part in starts)
        shape = jax.ShapeDtypeStruct((middle, LANES), jnp.float32)
        send_first, send_second = pl.pallas_call(
            functools.partial(add_kernel, layers),
            out_shape=(shape, shape),
            in_specs=[vmem] * (2 * len(first)),
            out_specs=(vmem, vmem),
            compiler_params=room(10),
            name="add",
        )(*first, *second)
        first, second = first + [swap(send_first, bit_first)], second + [swap(send_second, bit_second)]
        starts = (starts[0] + [0], starts[1] + [0])
    out = pl.pallas_call(
        functools.partial(final_kernel, starts),
        out_shape=jax.ShapeDtypeStruct((FEAT, rows_owned), jnp.float32),
        in_specs=[vmem] * (2 * len(first)),
        out_specs=vmem,
        scratch_shapes=[pltpu.VMEM((4 * FEAT, LANES), jnp.float32)],
        compiler_params=room(10),
        name="final",
    )(*first, *second)
    return out.T


def solution(mesh):
    in_specs = (
        P(None, ("parts", "xy"), None, None),
        P(None, ("parts", "xy"), None),
        P(("parts", "xy"), None, None),
        P(("parts", "xy"), None, None),
        P(("parts", "xy"), None),
        P("parts"),
    )
    out_specs = P(("parts", "xy"), None)
    return jax.shard_map(shards, mesh=mesh, in_specs=in_specs, out_specs=out_specs, check_vma=False)
```

```python
import functools

import jax
import jax.numpy as jnp
import numpy as np
from jax import lax
from jax.experimental import pallas as pl
from jax.experimental.pallas import tpu as pltpu
from jax.sharding import PartitionSpec as P


SLOTS = 8
HALO = 8
FEAT = 64
LANES = 128

sigma_list = (0.8, 1.3, 2.0, 3.0)
SCALES = len(sigma_list)
RESP = 3 * SCALES


def taps(sigma):
    offsets = np.arange(-HALO, HALO + 1).astype(np.float32)
    weights = np.exp(-offsets * offsets / np.float32(2.0 * sigma * sigma)).astype(np.float32)
    return (weights / weights.sum(dtype=np.float32)).astype(np.float32)


def band(weights, length):
    rows = np.arange(length)[:, None]
    cols = np.arange(length)[None, :]
    offset = cols - rows + HALO
    inside = (offset >= 0) & (offset <= 2 * HALO)
    return np.where(inside, weights[np.clip(offset, 0, 2 * HALO)], 0.0).astype(np.float32)


def halves(value):
    high = value.astype(jnp.bfloat16)
    low = (value - high.astype(jnp.float32)).astype(jnp.bfloat16)
    return high, low


def constant_halves(value):
    high = value.astype(jnp.bfloat16)
    low = (value - high.astype(np.float32)).astype(jnp.bfloat16)
    return high, low


def filter_constants(height, depth):
    along_y, along_z = [], []
    for sigma in sigma_list:
        high, low = constant_halves(band(taps(sigma), depth).T)
        along_y.append(np.concatenate([np.concatenate([high, low], 1), np.concatenate([high, np.zeros_like(low)], 1)], 0))
        high, low = constant_halves(band(taps(sigma), height))
        along_z.append(np.concatenate([high, high, low], 1))
    return np.stack(along_y), np.stack(along_z)


def order_bits(owners):
    bits = owners.bit_length() - 1
    first = list(range(bits))
    return first, [0] + first[2:3] + first[1:2] + first[3:]


def put(fields, row, value, planes, half):
    for q in range(planes):
        for b in range(2):
            fields[pl.ds(q * half * 8 + b * 4 + row, half, stride=8), :] = value(q)[b * half : (b + 1) * half]


def clear(tables):
    for table in tables:

        def some(step, carry, table=table):
            table[pl.ds(pl.multiple_of(step * 256, 256), 256), :] = jnp.zeros((256, LANES), jnp.float32)
            return carry

        lax.fori_loop(0, table.shape[0] // 256, some, 0)


def prepare_kernel(
    owners, rows_owned, height, me_ref, edge_ref, count_ref, home_ref, pair_ref, last_ref,
    y_ref, z_ref, target_ref, raw_ref, y_out, z_out, *tables,
):
    y_out[...] = y_ref[...]
    z_out[...] = z_ref[...]
    planes = last_ref.shape[1]
    clear(tables)
    for channel in range(3):
        own_ref = pair_ref.at[channel] if channel < 2 else last_ref.at[0]
        put(raw_ref, channel, lambda q: own_ref[q], planes, height // 2)
    put(raw_ref, 3, lambda q: jnp.ones((height, LANES), jnp.float32), planes, height // 2)
    entry_rows = edge_ref.shape[0] // 2
    both = jnp.concatenate([edge_ref[:entry_rows, :], edge_ref[entry_rows:, :]], 1)
    high = both // LANES
    low = both % LANES

    def pick(step, found):
        start = pl.multiple_of(step * 8, 8)
        lines = home_ref[pl.ds(start, 8), :]
        for number in range(8):
            line = jnp.broadcast_to(lines[number : number + 1], both.shape)
            found = jnp.where(high == start + number, jnp.take_along_axis(line, low, axis=1), found)
        return found

    found = lax.fori_loop(0, home_ref.shape[0] // 8, pick, jnp.zeros(both.shape, jnp.int32))
    home = jnp.concatenate([found[:, :height], found[:, height:]], 0)
    entry = lax.broadcasted_iota(jnp.int32, home.shape, 0)
    slot = entry % SLOTS
    owner = (home // rows_owned) ^ me_ref[0]
    within = home % rows_owned
    quarter = rows_owned // 4
    part = within // (2 * quarter)
    first, second = order_bits(owners)
    bits = len(first)
    place_first = jnp.zeros_like(owner)
    place_second = jnp.zeros_like(owner)
    for position in range(bits):
        place_first += ((owner >> first[position]) & 1) << (bits - 1 - position)
        place_second += ((owner >> second[position]) & 1) << (bits - 1 - position)
    place = jnp.where(part == 0, place_first, owners + place_second)
    row = place * (2 * quarter) + within % (2 * quarter)
    valid = slot < count_ref[...]
    target_ref[:, :height] = jnp.where(valid, row, owners * rows_owned)


def blur(before_ref, own_ref, after_ref, y_ref, z_ref, fields, blurred):
    planes, height, depth = own_ref.shape
    weights = [[float(w) for w in taps(sigma)] for sigma in sigma_list]
    tiles = height // 8

    def across(step, carry):
        rows = pl.ds(pl.multiple_of(step * 8, 8), 8)
        values = [before_ref[planes - HALO + p, rows, :] for p in range(HALO)]
        values += [own_ref[p, rows, :] for p in range(planes)]
        values += [after_ref[p, rows, :] for p in range(HALO)]
        for q in range(planes):
            center = q + HALO
            sums = [values[center]] + [values[center - t] + values[center + t] for t in range(1, HALO + 1)]
            for scale in range(SCALES):
                total = sums[0] * weights[scale][HALO]
                for t in range(1, HALO + 1):
                    total = total + sums[t] * weights[scale][HALO + t]
                blurred[scale, q, rows, :] = total
        return carry

    lax.fori_loop(0, tiles, across, 0)
    lines = []
    for scale in range(SCALES):
        high, low = halves(blurred[scale].reshape(planes * height, depth))
        line = jnp.dot(jnp.concatenate([high, low], 1), y_ref[scale], preferred_element_type=jnp.float32)
        lines.append(line[:, :depth] + line[:, depth:])
    for scale in range(SCALES):
        high, low = halves(lines[scale])
        high, low = high.reshape(planes, height, depth), low.reshape(planes, height, depth)
        stacked = jnp.concatenate([high, low, high], 1)
        side_by_side = jnp.concatenate([stacked[q] for q in range(planes)], 1)
        result = jnp.dot(z_ref[scale], side_by_side, preferred_element_type=jnp.float32)
        put(fields, scale, lambda q: result[:, q * depth : (q + 1) * depth], planes, height // 2)


def blur_kernel(before_ref, own_ref, after_ref, y_ref, z_ref, zero_ref, one_ref, blurred):
    for channel, fields in enumerate((zero_ref, one_ref)):
        refs = [ref.at[channel] for ref in (before_ref, own_ref, after_ref)]
        blur(*refs, y_ref, z_ref, fields, blurred)


def main_kernel(
    given, quarter, before_ref, own_ref, after_ref, y_ref, z_ref, zero_ref, one_ref, raw_ref, slots_ref, target_ref, *refs
):
    outs = 2 * given + (1 if given else 2)
    send_ref, *rest = refs[given:outs]
    tables, keep_refs = (rest, []) if given else ([], rest)
    blurred, two_ref, pending, entries, *own_tables = refs[outs:]
    clear(own_tables)
    tables += own_tables
    copies = len(tables)
    planes, height, depth = own_ref.shape[1:]
    half = height // 2
    blur(before_ref.at[0], own_ref.at[0], after_ref.at[0], y_ref, z_ref, two_ref, blurred)

    sub = lax.broadcasted_iota(jnp.int32, (SLOTS, LANES), 0)
    group = LANES // (2 * SLOTS)
    owner_row = lax.broadcasted_iota(jnp.int32, (2 * FEAT, LANES), 0) % 8 // 4
    owner_lane = lax.broadcasted_iota(jnp.int32, (2 * FEAT, LANES), 1) // SLOTS
    owner = owner_lane - owner_row
    steps = planes * half // group

    def scatter(step):
        plane = step // (half // group)
        base = plane * (SLOTS * LANES) + step % (half // group) * group
        for number in range(LANES):
            pair, block, slot = number // (2 * SLOTS), number // SLOTS % 2, number % SLOTS
            table = tables[number % copies]
            target = pl.ds(target_ref[base + (slot * LANES + block * half + pair)], 1)
            table[target, :] = table[target, :] + entries[number : number + 1, :]

    def turn():
        sums = pending[...]
        entries[...] = jnp.concatenate([sums, sums], 0).T

    pending[...] = jnp.zeros_like(pending)
    entries[...] = jnp.zeros_like(entries)

    def block_sums(step):
        scatter(jnp.maximum(step - 2, 0))
        turn()
        plane = step // (half // group)
        base = step % (half // group) * group
        parts, hots = [], []
        for g in range(group):
            zz = base + g
            rows = pl.ds(pl.multiple_of((plane * half + zz) * 8, 8), 8)
            resp = [ref[rows, :] for ref in (zero_ref, one_ref, two_ref)]
            square = [r * r for r in resp]
            cube = [s * r for s, r in zip(square, resp)]
            fourth = [s * s for s in square]
            pairs = [resp[a] * resp[b] for a, b in ((0, 1), (0, 2), (1, 2))]
            high, low = halves(jnp.concatenate([*resp, *square, *cube, *fourth, *pairs, raw_ref[rows, :]], 0))
            parts.append(jnp.concatenate([high, low], 1))
            hots.append((slots_ref[plane, pl.ds(zz, 1), :] == sub).astype(jnp.float32))
            hots.append((slots_ref[plane, pl.ds(zz + half, 1), :] == sub).astype(jnp.float32))
        hot = jnp.concatenate(hots, 0).astype(jnp.bfloat16)
        dims = (((1,), (1,)), ((), ()))
        products = lax.dot_general(
            jnp.concatenate(parts, 0), jnp.concatenate([hot, hot], 1), dims, preferred_element_type=jnp.float32
        )
        sums = jnp.zeros((2 * FEAT, LANES), jnp.float32)
        for g in range(group):
            sums = jnp.where(owner == 2 * g, products[2 * g * FEAT : (2 * g + 2) * FEAT], sums)
        folded = []
        for number in range(2 * FEAT // 8):
            piece = sums[8 * number : 8 * number + 8]
            folded.append(piece + pltpu.roll(piece, 4, 0))
        pending[...] = jnp.concatenate(
            [jnp.where(sub < 4, folded[k], folded[k + 1]) for k in range(0, len(folded), 2)], 0
        )

    unroll = 16 if steps % 16 == 0 else 1

    def several(step, carry):
        for number in range(unroll):
            block_sums(step * unroll + number)
        return carry

    lax.fori_loop(0, steps // unroll, several, 0)
    scatter(steps - 2)
    turn()
    scatter(steps - 1)

    combine(quarter, tables, send_ref, True)
    for keep_ref in keep_refs:
        combine(quarter, tables, keep_ref, False)


def combine(quarter, tables, out, sent):
    places = out.shape[0] // (2 * quarter)
    left = lax.broadcasted_iota(jnp.int32, (quarter, LANES), 1) < FEAT

    def one(step, carry):
        for part in range(2):
            row = pl.multiple_of(((2 * part + sent) * places + step) * 2 * quarter, 2 * quarter)
            total = tables[0][pl.ds(row, 2 * quarter), :]
            for table in tables[1:]:
                total = total + table[pl.ds(row, 2 * quarter), :]
            place = pl.multiple_of((part * places + step) * quarter, quarter)
            out[pl.ds(place, quarter), :] = jnp.where(left, total[:quarter], total[quarter:])
        return carry

    lax.fori_loop(0, places, one, 0)


def keep_kernel(quarter, *refs):
    combine(quarter, refs[:-1], refs[-1], False)


def add_kernel(layers, *refs):
    ins, outs = refs[:-2], refs[-2:]
    count = len(ins) // 2
    for number, out in enumerate(outs):
        total = None
        for ref, start in zip(ins[number * count : (number + 1) * count], layers[number]):
            piece = ref[start : start + out.shape[0], :]
            total = piece if total is None else total + piece
        out[...] = total


def final_kernel(layers, *refs):
    ins, out_ref, ordered = refs[:-2], refs[-2], refs[-1]
    count = len(ins) // 2
    quarter = ins[count - 1].shape[0]
    for number in range(2):
        table = None
        for ref, start in zip(ins[number * count : (number + 1) * count], layers[number]):
            piece = ref[start : start + quarter, :]
            table = piece if table is None else table + piece
        table = table.T
        for side in range(2):
            rows = table[side * FEAT : (side + 1) * FEAT]
            count_row = rows[FEAT - 1 :]
            lane = lax.broadcasted_iota(jnp.int32, rows.shape, 0)
            result = jnp.where(lane == FEAT - 1, jnp.log(1.0 + rows), rows / jnp.maximum(count_row, 1.0))
            columns = pl.ds((2 * number + side) * quarter, quarter)
            first_row = (2 * number + side) * FEAT
            for kind in range(15):
                ordered[pl.ds(first_row + kind // 3 * RESP + kind % 3, SCALES, stride=3), :] = result[4 * kind : 4 * kind + 4]
            ordered[first_row + FEAT - 4 : first_row + FEAT, :] = result[FEAT - 4 :]
            out_ref[:, columns] = ordered[first_row : first_row + FEAT, :]


def on_chip(value):
    return pltpu.with_memory_space_constraint(value, pltpu.VMEM)


def shards(affinity, block_scale, slot_map, edge_list, valid_count, edge_home):
    planes, height, depth = affinity.shape[1:]
    owners = lax.axis_size("xy")
    rows_owned = edge_home.shape[0] // owners
    quarter = rows_owned // 4
    vmem = pl.BlockSpec(memory_space=pltpu.VMEM)
    smem = pl.BlockSpec(memory_space=pltpu.SMEM)

    small = owners * rows_owned <= 8192

    near = on_chip if small else lambda value: value

    def room(mib):
        return pltpu.CompilerParams(vmem_limit_bytes=mib << 20) if small else None

    up = [(i, i + 1) for i in range(owners - 1)]
    down = [(j, i) for i, j in up]
    scaled, before, after = [], [], []
    dequant = affinity.astype(jnp.float32) * block_scale[..., None]

    def send_halo(value):
        scaled.append(on_chip(value))
        before.append(on_chip(lax.ppermute(value[:, planes - HALO :], "xy", up)))
        after.append(on_chip(lax.ppermute(value[:, :HALO], "xy", down)))

    send_halo(dequant[:2])
    send_halo(dequant[2:])

    me = lax.axis_index("xy").astype(jnp.int32).reshape(1)
    lists = edge_list.transpose(0, 2, 1).reshape(planes * SLOTS, height)
    counts = jnp.broadcast_to(valid_count[:, None, :], (planes, SLOTS, height)).reshape(planes * SLOTS, height)
    index_shape = jax.ShapeDtypeStruct((planes * SLOTS, height), jnp.int32)
    field_shape = jax.ShapeDtypeStruct((planes * height * 4, LANES), jnp.float32)
    table_rows = owners * rows_owned
    given = 4 if small else 0
    padded = jax.ShapeDtypeStruct((-(-(table_rows + 8) // 256) * 256, LANES), jnp.float32)
    constants = [jnp.asarray(value) for value in filter_constants(height, depth)]
    target, raw, filter_y, filter_z, *tables = pl.pallas_call(
        functools.partial(prepare_kernel, owners, rows_owned, height),
        out_shape=(jax.ShapeDtypeStruct((planes * SLOTS, LANES), jnp.int32), field_shape)
        + tuple(jax.ShapeDtypeStruct(value.shape, value.dtype) for value in constants)
        + (padded,) * given,
        in_specs=[smem] + [vmem] * 7,
        out_specs=(vmem,) * (4 + given),
        compiler_params=room(6),
        name="prepare",
    )(me, lists, counts, edge_home.reshape(-1, LANES), dequant[:2], dequant[2:], *constants)

    blurred = pltpu.VMEM((SCALES, planes, height, depth), jnp.float32)
    filters = (on_chip(filter_y), on_chip(filter_z))
    fields = pl.pallas_call(
        blur_kernel,
        out_shape=(field_shape, field_shape),
        in_specs=[vmem] * 5,
        out_specs=(vmem, vmem),
        scratch_shapes=[blurred],
        compiler_params=room(12),
        name="blur",
    )(before[0], scaled[0], after[0], *filters)
    table_shape = jax.ShapeDtypeStruct((owners * quarter, LANES), jnp.float32)
    send, *rest = pl.pallas_call(
        functools.partial(main_kernel, given, quarter),
        out_shape=(table_shape,) + ((padded,) * given if small else (table_shape,)),
        in_specs=[vmem] * 9 + [smem] + [vmem] * given,
        out_specs=(vmem,) * (1 + (given if small else 1)),
        input_output_aliases={10 + number: 1 + number for number in range(given)},
        scratch_shapes=[
            blurred,
            pltpu.VMEM(field_shape.shape, jnp.float32),
            pltpu.VMEM((FEAT, LANES), jnp.float32),
            pltpu.VMEM((LANES, LANES), jnp.float32),
        ]
        + [pltpu.VMEM(padded.shape, jnp.float32)] * (0 if small else 1),
        compiler_params=pltpu.CompilerParams(vmem_limit_bytes=(24 if small else 44) << 20),
        name="features",
    )(before[1], scaled[1], after[1], *filters, *map(on_chip, fields), on_chip(raw), on_chip(slot_map), target.reshape(-1), *map(on_chip, tables))

    def swap(value, bit):
        return near(lax.ppermute(value, "xy", [(i, i ^ (1 << bit)) for i in range(owners)]))

    order_first, order_second = order_bits(owners)
    whole = owners // 2 * quarter
    got = swap(send, 0)
    if small:
        keep = pl.pallas_call(
            functools.partial(keep_kernel, quarter),
            out_shape=table_shape,
            in_specs=[vmem] * given,
            out_specs=vmem,
            compiler_params=room(4),
            name="keep",
        )(*map(on_chip, rest))
    else:
        keep = rest[0]
    keep = near(keep)
    first, second = [keep, got], [keep, got]
    starts = ([0, 0], [whole, whole])
    middle = whole
    for bit_first, bit_second in zip(order_first[1:], order_second[1:]):
        middle //= 2
        layers = tuple(tuple(start + middle for start in part) for part in starts)
        shape = jax.ShapeDtypeStruct((middle, LANES), jnp.float32)
        send_first, send_second = pl.pallas_call(
            functools.partial(add_kernel, layers),
            out_shape=(shape, shape),
            in_specs=[vmem] * (2 * len(first)),
            out_specs=(vmem, vmem),
            compiler_params=room(10),
            name="add",
        )(*first, *second)
        first, second = first + [swap(send_first, bit_first)], second + [swap(send_second, bit_second)]
        starts = (starts[0] + [0], starts[1] + [0])
    out = pl.pallas_call(
        functools.partial(final_kernel, starts),
        out_shape=jax.ShapeDtypeStruct((FEAT, rows_owned), jnp.float32),
        in_specs=[vmem] * (2 * len(first)),
        out_specs=vmem,
        scratch_shapes=[pltpu.VMEM((4 * FEAT, LANES), jnp.float32)],
        compiler_params=room(10),
        name="final",
    )(*first, *second)
    return out.T


def solution(mesh):
    in_specs = (
        P(None, ("parts", "xy"), None, None),
        P(None, ("parts", "xy"), None),
        P(("parts", "xy"), None, None),
        P(("parts", "xy"), None, None),
        P(("parts", "xy"), None),
        P("parts"),
    )
    out_specs = P(("parts", "xy"), None)
    return jax.shard_map(shards, mesh=mesh, in_specs=in_specs, out_specs=out_specs, check_vma=False)
```

```python
import functools

import jax
import jax.numpy as jnp
import numpy as np
from jax import lax
from jax.experimental import pallas as pl
from jax.experimental.pallas import tpu as pltpu
from jax.sharding import PartitionSpec as P


SLOTS = 8
HALO = 8
FEAT = 64
LANES = 128

sigma_list = (0.8, 1.3, 2.0, 3.0)
SCALES = len(sigma_list)
RESP = 3 * SCALES


def taps(sigma):
    offsets = np.arange(-HALO, HALO + 1).astype(np.float32)
    weights = np.exp(-offsets * offsets / np.float32(2.0 * sigma * sigma)).astype(np.float32)
    return (weights / weights.sum(dtype=np.float32)).astype(np.float32)


def band(weights, length):
    rows = np.arange(length)[:, None]
    cols = np.arange(length)[None, :]
    offset = cols - rows + HALO
    inside = (offset >= 0) & (offset <= 2 * HALO)
    return np.where(inside, weights[np.clip(offset, 0, 2 * HALO)], 0.0).astype(np.float32)


def halves(value):
    high = value.astype(jnp.bfloat16)
    low = (value - high.astype(jnp.float32)).astype(jnp.bfloat16)
    return high, low


def constant_halves(value):
    high = value.astype(jnp.bfloat16)
    low = (value - high.astype(np.float32)).astype(jnp.bfloat16)
    return high, low


def filter_constants(height, depth):
    along_y, along_z = [], []
    for sigma in sigma_list:
        high, low = constant_halves(band(taps(sigma), depth).T)
        along_y.append(np.concatenate([np.concatenate([high, low], 1), np.concatenate([high, np.zeros_like(low)], 1)], 0))
        high, low = constant_halves(band(taps(sigma), height))
        along_z.append(np.concatenate([high, high, low], 1))
    return np.stack(along_y), np.stack(along_z)


def order_bits(owners):
    bits = owners.bit_length() - 1
    first = list(range(bits))
    return first, [0] + first[2:3] + first[1:2] + first[3:]


def put(fields, row, value, planes, half):
    for q in range(planes):
        for b in range(2):
            fields[pl.ds(q * half * 8 + b * 4 + row, half, stride=8), :] = value(q)[b * half : (b + 1) * half]


def clear(tables):
    for table in tables:

        def some(step, carry, table=table):
            table[pl.ds(pl.multiple_of(step * 256, 256), 256), :] = jnp.zeros((256, LANES), jnp.float32)
            return carry

        lax.fori_loop(0, table.shape[0] // 256, some, 0)


def prepare_kernel(
    owners, rows_owned, height, me_ref, edge_ref, count_ref, home_ref, pair_ref, last_ref,
    y_ref, z_ref, target_ref, raw_ref, y_out, z_out, *tables,
):
    y_out[...] = y_ref[...]
    z_out[...] = z_ref[...]
    planes = last_ref.shape[1]
    clear(tables)
    for channel in range(3):
        own_ref = pair_ref.at[channel] if channel < 2 else last_ref.at[0]
        put(raw_ref, channel, lambda q: own_ref[q], planes, height // 2)
    put(raw_ref, 3, lambda q: jnp.ones((height, LANES), jnp.float32), planes, height // 2)
    entry_rows = edge_ref.shape[0] // 2
    both = jnp.concatenate([edge_ref[:entry_rows, :], edge_ref[entry_rows:, :]], 1)
    high = both // LANES
    low = both % LANES

    def pick(step, found):
        start = pl.multiple_of(step * 8, 8)
        lines = home_ref[pl.ds(start, 8), :]
        for number in range(8):
            line = jnp.broadcast_to(lines[number : number + 1], both.shape)
            found = jnp.where(high == start + number, jnp.take_along_axis(line, low, axis=1), found)
        return found

    found = lax.fori_loop(0, home_ref.shape[0] // 8, pick, jnp.zeros(both.shape, jnp.int32))
    home = jnp.concatenate([found[:, :height], found[:, height:]], 0)
    entry = lax.broadcasted_iota(jnp.int32, home.shape, 0)
    slot = entry % SLOTS
    owner = (home // rows_owned) ^ me_ref[0]
    within = home % rows_owned
    quarter = rows_owned // 4
    part = within // (2 * quarter)
    first, second = order_bits(owners)
    bits = len(first)
    place_first = jnp.zeros_like(owner)
    place_second = jnp.zeros_like(owner)
    for position in range(bits):
        place_first += ((owner >> first[position]) & 1) << (bits - 1 - position)
        place_second += ((owner >> second[position]) & 1) << (bits - 1 - position)
    place = jnp.where(part == 0, place_first, owners + place_second)
    row = place * (2 * quarter) + within % (2 * quarter)
    valid = slot < count_ref[...]
    target_ref[:, :height] = jnp.where(valid, row, owners * rows_owned)


def blur(before_ref, own_ref, after_ref, y_ref, z_ref, fields, blurred):
    planes, height, depth = own_ref.shape
    weights = [[float(w) for w in taps(sigma)] for sigma in sigma_list]
    tiles = height // 8

    def across(step, carry):
        rows = pl.ds(pl.multiple_of(step * 8, 8), 8)
        values = [before_ref[planes - HALO + p, rows, :] for p in range(HALO)]
        values += [own_ref[p, rows, :] for p in range(planes)]
        values += [after_ref[p, rows, :] for p in range(HALO)]
        for q in range(planes):
            center = q + HALO
            sums = [values[center]] + [values[center - t] + values[center + t] for t in range(1, HALO + 1)]
            for scale in range(SCALES):
                total = sums[0] * weights[scale][HALO]
                for t in range(1, HALO + 1):
                    total = total + sums[t] * weights[scale][HALO + t]
                blurred[scale, q, rows, :] = total
        return carry

    lax.fori_loop(0, tiles, across, 0)
    lines = []
    for scale in range(SCALES):
        high, low = halves(blurred[scale].reshape(planes * height, depth))
        line = jnp.dot(jnp.concatenate([high, low], 1), y_ref[scale], preferred_element_type=jnp.float32)
        lines.append(line[:, :depth] + line[:, depth:])
    for scale in range(SCALES):
        high, low = halves(lines[scale])
        high, low = high.reshape(planes, height, depth), low.reshape(planes, height, depth)
        stacked = jnp.concatenate([high, low, high], 1)
        side_by_side = jnp.concatenate([stacked[q] for q in range(planes)], 1)
        result = jnp.dot(z_ref[scale], side_by_side, preferred_element_type=jnp.float32)
        put(fields, scale, lambda q: result[:, q * depth : (q + 1) * depth], planes, height // 2)


def blur_kernel(before_ref, own_ref, after_ref, y_ref, z_ref, zero_ref, one_ref, blurred):
    for channel, fields in enumerate((zero_ref, one_ref)):
        refs = [ref.at[channel] for ref in (before_ref, own_ref, after_ref)]
        blur(*refs, y_ref, z_ref, fields, blurred)


def main_kernel(
    given, quarter, before_ref, own_ref, after_ref, y_ref, z_ref, zero_ref, one_ref, raw_ref, slots_ref, target_ref, *refs
):
    outs = 2 * given + (1 if given else 2)
    send_ref, *rest = refs[given:outs]
    tables, keep_refs = (rest, []) if given else ([], rest)
    blurred, two_ref, pending, entries, *own_tables = refs[outs:]
    clear(own_tables)
    tables += own_tables
    copies = len(tables)
    planes, height, depth = own_ref.shape[1:]
    half = height // 2
    blur(before_ref.at[0], own_ref.at[0], after_ref.at[0], y_ref, z_ref, two_ref, blurred)

    sub = lax.broadcasted_iota(jnp.int32, (SLOTS, LANES), 0)
    group = LANES // (2 * SLOTS)
    owner_row = lax.broadcasted_iota(jnp.int32, (8, LANES), 0) // 4
    owner_lane = lax.broadcasted_iota(jnp.int32, (8, LANES), 1) // SLOTS
    owner = owner_lane - owner_row
    steps = planes * half // group

    def scatter(step):
        plane = step // (half // group)
        base = plane * (SLOTS * LANES) + step % (half // group) * group
        for number in range(LANES):
            pair, block, slot = number // (2 * SLOTS), number // SLOTS % 2, number % SLOTS
            table = tables[number % copies]
            target = pl.ds(target_ref[base + (slot * LANES + block * half + pair)], 1)
            table[target, :] = table[target, :] + entries[number : number + 1, :]

    def turn():
        sums = pending[...]
        entries[...] = jnp.concatenate([sums, sums], 0).T

    pending[...] = jnp.zeros_like(pending)
    entries[...] = jnp.zeros_like(entries)

    def block_sums(step):
        scatter(jnp.maximum(step - 2, 0))
        turn()
        plane = step // (half // group)
        base = step % (half // group) * group
        parts, hots = [], []
        for g in range(group):
            zz = base + g
            rows = pl.ds(pl.multiple_of((plane * half + zz) * 8, 8), 8)
            resp = [ref[rows, :] for ref in (zero_ref, one_ref, two_ref)]
            square = [r * r for r in resp]
            cube = [s * r for s, r in zip(square, resp)]
            fourth = [s * s for s in square]
            pairs = [resp[a] * resp[b] for a, b in ((0, 1), (0, 2), (1, 2))]
            high, low = halves(jnp.concatenate([*resp, *square, *cube, *fourth, *pairs, raw_ref[rows, :]], 0))
            parts.append(jnp.concatenate([high, low], 1))
            hots.append((slots_ref[plane, pl.ds(zz, 1), :] == sub).astype(jnp.float32))
            hots.append((slots_ref[plane, pl.ds(zz + half, 1), :] == sub).astype(jnp.float32))
        hot = jnp.concatenate(hots, 0).astype(jnp.bfloat16)
        dims = (((1,), (1,)), ((), ()))
        products = lax.dot_general(
            jnp.concatenate(parts, 0), jnp.concatenate([hot, hot], 1), dims, preferred_element_type=jnp.float32
        )
        folded = []
        for row in range(0, 2 * FEAT, 8):
            piece = jnp.zeros((8, LANES), jnp.float32)
            for g in range(group):
                start = 2 * g * FEAT + row
                piece = jnp.where(owner == 2 * g, products[start : start + 8], piece)
            folded.append(piece + pltpu.roll(piece, 4, 0))
        pending[...] = jnp.concatenate(
            [jnp.where(sub < 4, folded[k], folded[k + 1]) for k in range(0, len(folded), 2)], 0
        )

    unroll = 16 if steps % 16 == 0 else 1

    def several(step, carry):
        for number in range(unroll):
            block_sums(step * unroll + number)
        return carry

    lax.fori_loop(0, steps // unroll, several, 0)
    scatter(steps - 2)
    turn()
    scatter(steps - 1)

    combine(quarter, tables, send_ref, True)
    for keep_ref in keep_refs:
        combine(quarter, tables, keep_ref, False)


def combine(quarter, tables, out, sent):
    places = out.shape[0] // (2 * quarter)
    left = lax.broadcasted_iota(jnp.int32, (quarter, LANES), 1) < FEAT

    def one(step, carry):
        for part in range(2):
            row = pl.multiple_of(((2 * part + sent) * places + step) * 2 * quarter, 2 * quarter)
            total = tables[0][pl.ds(row, 2 * quarter), :]
            for table in tables[1:]:
                total = total + table[pl.ds(row, 2 * quarter), :]
            place = pl.multiple_of((part * places + step) * quarter, quarter)
            out[pl.ds(place, quarter), :] = jnp.where(left, total[:quarter], total[quarter:])
        return carry

    lax.fori_loop(0, places, one, 0)


def keep_kernel(quarter, *refs):
    combine(quarter, refs[:-1], refs[-1], False)


def add_kernel(layers, *refs):
    ins, outs = refs[:-2], refs[-2:]
    count = len(ins) // 2
    for number, out in enumerate(outs):
        total = None
        for ref, start in zip(ins[number * count : (number + 1) * count], layers[number]):
            piece = ref[start : start + out.shape[0], :]
            total = piece if total is None else total + piece
        out[...] = total


def final_kernel(layers, *refs):
    ins, out_ref, ordered = refs[:-2], refs[-2], refs[-1]
    count = len(ins) // 2
    quarter = ins[count - 1].shape[0]
    for number in range(2):
        table = None
        for ref, start in zip(ins[number * count : (number + 1) * count], layers[number]):
            piece = ref[start : start + quarter, :]
            table = piece if table is None else table + piece
        table = table.T
        for side in range(2):
            rows = table[side * FEAT : (side + 1) * FEAT]
            count_row = rows[FEAT - 1 :]
            lane = lax.broadcasted_iota(jnp.int32, rows.shape, 0)
            result = jnp.where(lane == FEAT - 1, jnp.log(1.0 + rows), rows / jnp.maximum(count_row, 1.0))
            columns = pl.ds((2 * number + side) * quarter, quarter)
            first_row = (2 * number + side) * FEAT
            for kind in range(15):
                ordered[pl.ds(first_row + kind // 3 * RESP + kind % 3, SCALES, stride=3), :] = result[4 * kind : 4 * kind + 4]
            ordered[first_row + FEAT - 4 : first_row + FEAT, :] = result[FEAT - 4 :]
            out_ref[:, columns] = ordered[first_row : first_row + FEAT, :]


def on_chip(value):
    return pltpu.with_memory_space_constraint(value, pltpu.VMEM)


def shards(affinity, block_scale, slot_map, edge_list, valid_count, edge_home):
    planes, height, depth = affinity.shape[1:]
    owners = lax.axis_size("xy")
    rows_owned = edge_home.shape[0] // owners
    quarter = rows_owned // 4
    vmem = pl.BlockSpec(memory_space=pltpu.VMEM)
    smem = pl.BlockSpec(memory_space=pltpu.SMEM)

    small = owners * rows_owned <= 8192

    near = on_chip if small else lambda value: value

    def room(mib):
        return pltpu.CompilerParams(vmem_limit_bytes=mib << 20) if small else None

    up = [(i, i + 1) for i in range(owners - 1)]
    down = [(j, i) for i, j in up]
    scaled, before, after = [], [], []
    dequant = affinity.astype(jnp.float32) * block_scale[..., None]

    def send_halo(value):
        scaled.append(on_chip(value))
        before.append(on_chip(lax.ppermute(value[:, planes - HALO :], "xy", up)))
        after.append(on_chip(lax.ppermute(value[:, :HALO], "xy", down)))

    send_halo(dequant[:2])
    send_halo(dequant[2:])

    me = lax.axis_index("xy").astype(jnp.int32).reshape(1)
    lists = edge_list.transpose(0, 2, 1).reshape(planes * SLOTS, height)
    counts = jnp.broadcast_to(valid_count[:, None, :], (planes, SLOTS, height)).reshape(planes * SLOTS, height)
    index_shape = jax.ShapeDtypeStruct((planes * SLOTS, height), jnp.int32)
    field_shape = jax.ShapeDtypeStruct((planes * height * 4, LANES), jnp.float32)
    table_rows = owners * rows_owned
    given = 4 if small else 0
    padded = jax.ShapeDtypeStruct((-(-(table_rows + 8) // 256) * 256, LANES), jnp.float32)
    constants = [jnp.asarray(value) for value in filter_constants(height, depth)]
    target, raw, filter_y, filter_z, *tables = pl.pallas_call(
        functools.partial(prepare_kernel, owners, rows_owned, height),
        out_shape=(jax.ShapeDtypeStruct((planes * SLOTS, LANES), jnp.int32), field_shape)
        + tuple(jax.ShapeDtypeStruct(value.shape, value.dtype) for value in constants)
        + (padded,) * given,
        in_specs=[smem] + [vmem] * 7,
        out_specs=(vmem,) * (4 + given),
        compiler_params=room(6),
        name="prepare",
    )(me, lists, counts, edge_home.reshape(-1, LANES), dequant[:2], dequant[2:], *constants)

    blurred = pltpu.VMEM((SCALES, planes, height, depth), jnp.float32)
    filters = (on_chip(filter_y), on_chip(filter_z))
    fields = pl.pallas_call(
        blur_kernel,
        out_shape=(field_shape, field_shape),
        in_specs=[vmem] * 5,
        out_specs=(vmem, vmem),
        scratch_shapes=[blurred],
        compiler_params=room(12),
        name="blur",
    )(before[0], scaled[0], after[0], *filters)
    table_shape = jax.ShapeDtypeStruct((owners * quarter, LANES), jnp.float32)
    send, *rest = pl.pallas_call(
        functools.partial(main_kernel, given, quarter),
        out_shape=(table_shape,) + ((padded,) * given if small else (table_shape,)),
        in_specs=[vmem] * 9 + [smem] + [vmem] * given,
        out_specs=(vmem,) * (1 + (given if small else 1)),
        input_output_aliases={10 + number: 1 + number for number in range(given)},
        scratch_shapes=[
            blurred,
            pltpu.VMEM(field_shape.shape, jnp.float32),
            pltpu.VMEM((FEAT, LANES), jnp.float32),
            pltpu.VMEM((LANES, LANES), jnp.float32),
        ]
        + [pltpu.VMEM(padded.shape, jnp.float32)] * (0 if small else 1),
        compiler_params=pltpu.CompilerParams(vmem_limit_bytes=(24 if small else 44) << 20),
        name="features",
    )(before[1], scaled[1], after[1], *filters, *map(on_chip, fields), on_chip(raw), on_chip(slot_map), target.reshape(-1), *map(on_chip, tables))

    def swap(value, bit):
        return near(lax.ppermute(value, "xy", [(i, i ^ (1 << bit)) for i in range(owners)]))

    order_first, order_second = order_bits(owners)
    whole = owners // 2 * quarter
    got = swap(send, 0)
    if small:
        keep = pl.pallas_call(
            functools.partial(keep_kernel, quarter),
            out_shape=table_shape,
            in_specs=[vmem] * given,
            out_specs=vmem,
            compiler_params=room(4),
            name="keep",
        )(*map(on_chip, rest))
    else:
        keep = rest[0]
    keep = near(keep)
    first, second = [keep, got], [keep, got]
    starts = ([0, 0], [whole, whole])
    middle = whole
    for bit_first, bit_second in zip(order_first[1:], order_second[1:]):
        middle //= 2
        layers = tuple(tuple(start + middle for start in part) for part in starts)
        shape = jax.ShapeDtypeStruct((middle, LANES), jnp.float32)
        send_first, send_second = pl.pallas_call(
            functools.partial(add_kernel, layers),
            out_shape=(shape, shape),
            in_specs=[vmem] * (2 * len(first)),
            out_specs=(vmem, vmem),
            compiler_params=room(10),
            name="add",
        )(*first, *second)
        first, second = first + [swap(send_first, bit_first)], second + [swap(send_second, bit_second)]
        starts = (starts[0] + [0], starts[1] + [0])
    out = pl.pallas_call(
        functools.partial(final_kernel, starts),
        out_shape=jax.ShapeDtypeStruct((FEAT, rows_owned), jnp.float32),
        in_specs=[vmem] * (2 * len(first)),
        out_specs=vmem,
        scratch_shapes=[pltpu.VMEM((4 * FEAT, LANES), jnp.float32)],
        compiler_params=room(10),
        name="final",
    )(*first, *second)
    return out.T


def solution(mesh):
    in_specs = (
        P(None, ("parts", "xy"), None, None),
        P(None, ("parts", "xy"), None),
        P(("parts", "xy"), None, None),
        P(("parts", "xy"), None, None),
        P(("parts", "xy"), None),
        P("parts"),
    )
    out_specs = P(("parts", "xy"), None)
    return jax.shard_map(shards, mesh=mesh, in_specs=in_specs, out_specs=out_specs, check_vma=False)
```

```python
import functools

import jax
import jax.numpy as jnp
import numpy as np
from jax import lax
from jax.experimental import pallas as pl
from jax.experimental.pallas import tpu as pltpu
from jax.sharding import PartitionSpec as P


SLOTS = 8
HALO = 8
FEAT = 64
LANES = 128

sigma_list = (0.8, 1.3, 2.0, 3.0)
SCALES = len(sigma_list)
RESP = 3 * SCALES


def taps(sigma):
    offsets = np.arange(-HALO, HALO + 1).astype(np.float32)
    weights = np.exp(-offsets * offsets / np.float32(2.0 * sigma * sigma)).astype(np.float32)
    return (weights / weights.sum(dtype=np.float32)).astype(np.float32)


def band(weights, length):
    rows = np.arange(length)[:, None]
    cols = np.arange(length)[None, :]
    offset = cols - rows + HALO
    inside = (offset >= 0) & (offset <= 2 * HALO)
    return np.where(inside, weights[np.clip(offset, 0, 2 * HALO)], 0.0).astype(np.float32)


def halves(value):
    high = value.astype(jnp.bfloat16)
    low = (value - high.astype(jnp.float32)).astype(jnp.bfloat16)
    return high, low


def constant_halves(value):
    high = value.astype(jnp.bfloat16)
    low = (value - high.astype(np.float32)).astype(jnp.bfloat16)
    return high, low


def filter_constants(height, depth):
    along_y, along_z = [], []
    for sigma in sigma_list:
        high, low = constant_halves(band(taps(sigma), depth).T)
        along_y.append(np.concatenate([np.concatenate([high, low], 1), np.concatenate([high, np.zeros_like(low)], 1)], 0))
        high, low = constant_halves(band(taps(sigma), height))
        along_z.append(np.concatenate([high, high, low], 1))
    return np.stack(along_y), np.stack(along_z)


def order_bits(owners):
    bits = owners.bit_length() - 1
    first = list(range(bits))
    return [0] + first[2:3] + first[1:2] + first[3:], first


def put(fields, row, value, planes, half):
    for q in range(planes):
        for b in range(2):
            fields[pl.ds(q * half * 8 + b * 4 + row, half, stride=8), :] = value(q)[b * half : (b + 1) * half]


def clear(tables):
    for table in tables:

        def some(step, carry, table=table):
            table[pl.ds(pl.multiple_of(step * 256, 256), 256), :] = jnp.zeros((256, LANES), jnp.float32)
            return carry

        lax.fori_loop(0, table.shape[0] // 256, some, 0)


def prepare_kernel(
    owners, rows_owned, height, me_ref, edge_ref, count_ref, home_ref, pair_ref, last_ref,
    y_ref, z_ref, target_ref, raw_ref, y_out, z_out, *tables,
):
    y_out[...] = y_ref[...]
    z_out[...] = z_ref[...]
    planes = last_ref.shape[1]
    clear(tables)
    for channel in range(3):
        own_ref = pair_ref.at[channel] if channel < 2 else last_ref.at[0]
        put(raw_ref, channel, lambda q: own_ref[q], planes, height // 2)
    put(raw_ref, 3, lambda q: jnp.ones((height, LANES), jnp.float32), planes, height // 2)
    entry_rows = edge_ref.shape[0] // 2
    both = jnp.concatenate([edge_ref[:entry_rows, :], edge_ref[entry_rows:, :]], 1)
    high = both // LANES
    low = both % LANES

    def pick(step, found):
        start = pl.multiple_of(step * 8, 8)
        lines = home_ref[pl.ds(start, 8), :]
        for number in range(8):
            line = jnp.broadcast_to(lines[number : number + 1], both.shape)
            found = jnp.where(high == start + number, jnp.take_along_axis(line, low, axis=1), found)
        return found

    found = lax.fori_loop(0, home_ref.shape[0] // 8, pick, jnp.zeros(both.shape, jnp.int32))
    home = jnp.concatenate([found[:, :height], found[:, height:]], 0)
    entry = lax.broadcasted_iota(jnp.int32, home.shape, 0)
    slot = entry % SLOTS
    owner = (home // rows_owned) ^ me_ref[0]
    within = home % rows_owned
    quarter = rows_owned // 4
    part = within // (2 * quarter)
    first, second = order_bits(owners)
    bits = len(first)
    place_first = jnp.zeros_like(owner)
    place_second = jnp.zeros_like(owner)
    for position in range(bits):
        place_first += ((owner >> first[position]) & 1) << (bits - 1 - position)
        place_second += ((owner >> second[position]) & 1) << (bits - 1 - position)
    place = jnp.where(part == 0, place_first, owners + place_second)
    row = place * (2 * quarter) + within % (2 * quarter)
    valid = slot < count_ref[...]
    target_ref[:, :height] = jnp.where(valid, row, owners * rows_owned)


def blur(before_ref, own_ref, after_ref, y_ref, z_ref, fields, blurred):
    channels, planes, height, depth = own_ref.shape
    weights = [[float(w) for w in taps(sigma)] for sigma in sigma_list]
    tiles = height // 8

    def across(step, carry):
        channel = step // tiles
        rows = pl.ds(pl.multiple_of(step % tiles * 8, 8), 8)
        values = [before_ref[channel, planes - HALO + p, rows, :] for p in range(HALO)]
        values += [own_ref[channel, p, rows, :] for p in range(planes)]
        values += [after_ref[channel, p, rows, :] for p in range(HALO)]
        for q in range(planes):
            center = q + HALO
            sums = [values[center]] + [values[center - t] + values[center + t] for t in range(1, HALO + 1)]
            for scale in range(SCALES):
                total = sums[0] * weights[scale][HALO]
                for t in range(1, HALO + 1):
                    total = total + sums[t] * weights[scale][HALO + t]
                blurred[scale, channel * planes + q, rows, :] = total
        return carry

    lax.fori_loop(0, channels * tiles, across, 0)
    count = channels * planes
    lines = []
    for scale in range(SCALES):
        high, low = halves(blurred[scale].reshape(count * height, depth))
        line = jnp.dot(jnp.concatenate([high, low], 1), y_ref[scale], preferred_element_type=jnp.float32)
        lines.append(line[:, :depth] + line[:, depth:])
    for scale in range(SCALES):
        high, low = halves(lines[scale])
        high, low = high.reshape(count, height, depth), low.reshape(count, height, depth)
        stacked = jnp.concatenate([high, low, high], 1)
        side_by_side = jnp.concatenate([stacked[p] for p in range(count)], 1)
        result = jnp.dot(z_ref[scale], side_by_side, preferred_element_type=jnp.float32)
        for channel in range(channels):
            part = result[:, channel * planes * depth : (channel + 1) * planes * depth]
            put(fields[channel], scale, lambda q: part[:, q * depth : (q + 1) * depth], planes, height // 2)


def blur_kernel(before_ref, own_ref, after_ref, y_ref, z_ref, zero_ref, one_ref, blurred):
    blur(before_ref, own_ref, after_ref, y_ref, z_ref, (zero_ref, one_ref), blurred)


def main_kernel(
    given, quarter, before_ref, own_ref, after_ref, y_ref, z_ref, zero_ref, one_ref, raw_ref, slots_ref, target_ref, *refs
):
    outs = 2 * given + (1 if given else 2)
    send_ref, *rest = refs[given:outs]
    tables, keep_refs = (rest, []) if given else ([], rest)
    blurred, two_ref, pending, entries, *own_tables = refs[outs:]
    clear(own_tables)
    tables += own_tables
    copies = len(tables)
    planes, height, depth = own_ref.shape[1:]
    half = height // 2
    blur(before_ref, own_ref, after_ref, y_ref, z_ref, (two_ref,), blurred)

    sub = lax.broadcasted_iota(jnp.int32, (SLOTS, LANES), 0)
    group = LANES // (2 * SLOTS)
    owner_row = lax.broadcasted_iota(jnp.int32, (8, LANES), 0) // 4
    owner_lane = lax.broadcasted_iota(jnp.int32, (8, LANES), 1) // SLOTS
    owner = owner_lane - owner_row
    steps = planes * half // group

    def scatter(step):
        plane = step // (half // group)
        base = plane * (SLOTS * LANES) + step % (half // group) * group
        for number in range(LANES):
            pair, block, slot = number // (2 * SLOTS), number // SLOTS % 2, number % SLOTS
            table = tables[number % copies]
            target = pl.ds(target_ref[base + (slot * LANES + block * half + pair)], 1)
            table[target, :] = table[target, :] + entries[number : number + 1, :]

    def turn():
        sums = pending[...]
        entries[...] = jnp.concatenate([sums, sums], 0).T

    pending[...] = jnp.zeros_like(pending)
    entries[...] = jnp.zeros_like(entries)

    def block_sums(step):
        scatter(jnp.maximum(step - 2, 0))
        turn()
        plane = step // (half // group)
        base = step % (half // group) * group
        parts, hots = [], []
        for g in range(group):
            zz = base + g
            rows = pl.ds(pl.multiple_of((plane * half + zz) * 8, 8), 8)
            resp = [ref[rows, :] for ref in (zero_ref, one_ref, two_ref)]
            square = [r * r for r in resp]
            cube = [s * r for s, r in zip(square, resp)]
            fourth = [s * s for s in square]
            pairs = [resp[a] * resp[b] for a, b in ((0, 1), (0, 2), (1, 2))]
            high, low = halves(jnp.concatenate([*resp, *square, *cube, *fourth, *pairs, raw_ref[rows, :]], 0))
            parts.append(jnp.concatenate([high, low], 1))
            hots.append((slots_ref[plane, pl.ds(zz, 1), :] == sub).astype(jnp.float32))
            hots.append((slots_ref[plane, pl.ds(zz + half, 1), :] == sub).astype(jnp.float32))
        hot = jnp.concatenate(hots, 0).astype(jnp.bfloat16)
        dims = (((1,), (1,)), ((), ()))
        products = lax.dot_general(
            jnp.concatenate(parts, 0), jnp.concatenate([hot, hot], 1), dims, preferred_element_type=jnp.float32
        )
        folded = []
        for row in range(0, 2 * FEAT, 8):
            piece = jnp.zeros((8, LANES), jnp.float32)
            for g in range(group):
                start = 2 * g * FEAT + row
                piece = jnp.where(owner == 2 * g, products[start : start + 8], piece)
            folded.append(piece + pltpu.roll(piece, 4, 0))
        pending[...] = jnp.concatenate(
            [jnp.where(sub < 4, folded[k], folded[k + 1]) for k in range(0, len(folded), 2)], 0
        )

    unroll = 16 if steps % 16 == 0 else 1

    def several(step, carry):
        for number in range(unroll):
            block_sums(step * unroll + number)
        return carry

    lax.fori_loop(0, steps // unroll, several, 0)
    scatter(steps - 2)
    turn()
    scatter(steps - 1)

    combine(quarter, tables, send_ref, True)
    for keep_ref in keep_refs:
        combine(quarter, tables, keep_ref, False)


def combine(quarter, tables, out, sent):
    places = out.shape[0] // (2 * quarter)
    left = lax.broadcasted_iota(jnp.int32, (quarter, LANES), 1) < FEAT

    def one(step, carry):
        for part in range(2):
            row = pl.multiple_of(((2 * part + sent) * places + step) * 2 * quarter, 2 * quarter)
            total = tables[0][pl.ds(row, 2 * quarter), :]
            for table in tables[1:]:
                total = total + table[pl.ds(row, 2 * quarter), :]
            place = pl.multiple_of((part * places + step) * quarter, quarter)
            out[pl.ds(place, quarter), :] = jnp.where(left, total[:quarter], total[quarter:])
        return carry

    lax.fori_loop(0, places, one, 0)


def keep_kernel(quarter, *refs):
    combine(quarter, refs[:-1], refs[-1], False)


def add_kernel(layers, *refs):
    ins, outs = refs[:-2], refs[-2:]
    count = len(ins) // 2
    for number, out in enumerate(outs):
        total = None
        for ref, start in zip(ins[number * count : (number + 1) * count], layers[number]):
            piece = ref[start : start + out.shape[0], :]
            total = piece if total is None else total + piece
        out[...] = total


def final_kernel(layers, *refs):
    ins, out_ref, ordered = refs[:-2], refs[-2], refs[-1]
    count = len(ins) // 2
    quarter = ins[count - 1].shape[0]
    for number in range(2):
        table = None
        for ref, start in zip(ins[number * count : (number + 1) * count], layers[number]):
            piece = ref[start : start + quarter, :]
            table = piece if table is None else table + piece
        table = table.T
        for side in range(2):
            rows = table[side * FEAT : (side + 1) * FEAT]
            count_row = rows[FEAT - 1 :]
            lane = lax.broadcasted_iota(jnp.int32, rows.shape, 0)
            result = jnp.where(lane == FEAT - 1, jnp.log(1.0 + rows), rows / jnp.maximum(count_row, 1.0))
            columns = pl.ds((2 * number + side) * quarter, quarter)
            first_row = (2 * number + side) * FEAT
            for kind in range(15):
                ordered[pl.ds(first_row + kind // 3 * RESP + kind % 3, SCALES, stride=3), :] = result[4 * kind : 4 * kind + 4]
            ordered[first_row + FEAT - 4 : first_row + FEAT, :] = result[FEAT - 4 :]
            out_ref[:, columns] = ordered[first_row : first_row + FEAT, :]


def on_chip(value):
    return pltpu.with_memory_space_constraint(value, pltpu.VMEM)


def shards(affinity, block_scale, slot_map, edge_list, valid_count, edge_home):
    planes, height, depth = affinity.shape[1:]
    owners = lax.axis_size("xy")
    rows_owned = edge_home.shape[0] // owners
    quarter = rows_owned // 4
    vmem = pl.BlockSpec(memory_space=pltpu.VMEM)
    smem = pl.BlockSpec(memory_space=pltpu.SMEM)

    small = owners * rows_owned <= 8192

    near = on_chip if small else lambda value: value

    def room(mib):
        return pltpu.CompilerParams(vmem_limit_bytes=mib << 20) if small else None

    up = [(i, i + 1) for i in range(owners - 1)]
    down = [(j, i) for i, j in up]
    scaled, before, after = [], [], []
    dequant = affinity.astype(jnp.float32) * block_scale[..., None]

    def send_halo(value):
        scaled.append(on_chip(value))
        before.append(on_chip(lax.ppermute(value[:, planes - HALO :], "xy", up)))
        after.append(on_chip(lax.ppermute(value[:, :HALO], "xy", down)))

    send_halo(dequant[:2])
    send_halo(dequant[2:])

    me = lax.axis_index("xy").astype(jnp.int32).reshape(1)
    lists = edge_list.transpose(0, 2, 1).reshape(planes * SLOTS, height)
    counts = jnp.broadcast_to(valid_count[:, None, :], (planes, SLOTS, height)).reshape(planes * SLOTS, height)
    index_shape = jax.ShapeDtypeStruct((planes * SLOTS, height), jnp.int32)
    field_shape = jax.ShapeDtypeStruct((planes * height * 4, LANES), jnp.float32)
    table_rows = owners * rows_owned
    given = 4 if small else 0
    padded = jax.ShapeDtypeStruct((-(-(table_rows + 8) // 256) * 256, LANES), jnp.float32)
    constants = [jnp.asarray(value) for value in filter_constants(height, depth)]
    target, raw, filter_y, filter_z, *tables = pl.pallas_call(
        functools.partial(prepare_kernel, owners, rows_owned, height),
        out_shape=(jax.ShapeDtypeStruct((planes * SLOTS, LANES), jnp.int32), field_shape)
        + tuple(jax.ShapeDtypeStruct(value.shape, value.dtype) for value in constants)
        + (padded,) * given,
        in_specs=[smem] + [vmem] * 7,
        out_specs=(vmem,) * (4 + given),
        compiler_params=room(6),
        name="prepare",
    )(me, lists, counts, edge_home.reshape(-1, LANES), dequant[:2], dequant[2:], *constants)

    blurred = pltpu.VMEM((SCALES, planes, height, depth), jnp.float32)
    filters = (on_chip(filter_y), on_chip(filter_z))
    fields = pl.pallas_call(
        blur_kernel,
        out_shape=(field_shape, field_shape),
        in_specs=[vmem] * 5,
        out_specs=(vmem, vmem),
        scratch_shapes=[pltpu.VMEM((SCALES, 2 * planes, height, depth), jnp.float32)],
        compiler_params=room(20),
        name="blur",
    )(before[0], scaled[0], after[0], *filters)
    table_shape = jax.ShapeDtypeStruct((owners * quarter, LANES), jnp.float32)
    send, *rest = pl.pallas_call(
        functools.partial(main_kernel, given, quarter),
        out_shape=(table_shape,) + ((padded,) * given if small else (table_shape,)),
        in_specs=[vmem] * 9 + [smem] + [vmem] * given,
        out_specs=(vmem,) * (1 + (given if small else 1)),
        input_output_aliases={10 + number: 1 + number for number in range(given)},
        scratch_shapes=[
            blurred,
            pltpu.VMEM(field_shape.shape, jnp.float32),
            pltpu.VMEM((FEAT, LANES), jnp.float32),
            pltpu.VMEM((LANES, LANES), jnp.float32),
        ]
        + [pltpu.VMEM(padded.shape, jnp.float32)] * (0 if small else 1),
        compiler_params=pltpu.CompilerParams(vmem_limit_bytes=(24 if small else 44) << 20),
        name="features",
    )(before[1], scaled[1], after[1], *filters, *map(on_chip, fields), on_chip(raw), on_chip(slot_map), target.reshape(-1), *map(on_chip, tables))

    def swap(value, bit):
        return near(lax.ppermute(value, "xy", [(i, i ^ (1 << bit)) for i in range(owners)]))

    order_first, order_second = order_bits(owners)
    whole = owners // 2 * quarter
    got = swap(send, 0)
    if small:
        keep = pl.pallas_call(
            functools.partial(keep_kernel, quarter),
            out_shape=table_shape,
            in_specs=[vmem] * given,
            out_specs=vmem,
            compiler_params=room(4),
            name="keep",
        )(*map(on_chip, rest))
    else:
        keep = rest[0]
    keep = near(keep)
    first, second = [keep, got], [keep, got]
    starts = ([0, 0], [whole, whole])
    middle = whole
    for bit_first, bit_second in zip(order_first[1:], order_second[1:]):
        middle //= 2
        layers = tuple(tuple(start + middle for start in part) for part in starts)
        shape = jax.ShapeDtypeStruct((middle, LANES), jnp.float32)
        send_first, send_second = pl.pallas_call(
            functools.partial(add_kernel, layers),
            out_shape=(shape, shape),
            in_specs=[vmem] * (2 * len(first)),
            out_specs=(vmem, vmem),
            compiler_params=room(10),
            name="add",
        )(*first, *second)
        first, second = first + [swap(send_first, bit_first)], second + [swap(send_second, bit_second)]
        starts = (starts[0] + [0], starts[1] + [0])
    out = pl.pallas_call(
        functools.partial(final_kernel, starts),
        out_shape=jax.ShapeDtypeStruct((FEAT, rows_owned), jnp.float32),
        in_specs=[vmem] * (2 * len(first)),
        out_specs=vmem,
        scratch_shapes=[pltpu.VMEM((4 * FEAT, LANES), jnp.float32)],
        compiler_params=room(10),
        name="final",
    )(*first, *second)
    return out.T


def solution(mesh):
    in_specs = (
        P(None, ("parts", "xy"), None, None),
        P(None, ("parts", "xy"), None),
        P(("parts", "xy"), None, None),
        P(("parts", "xy"), None, None),
        P(("parts", "xy"), None),
        P("parts"),
    )
    out_specs = P(("parts", "xy"), None)
    return jax.shard_map(shards, mesh=mesh, in_specs=in_specs, out_specs=out_specs, check_vma=False)
```
